32 devices in a mesh: wide: 8 (over z, y), narrow: 4 (over x, core).
Axes of the slice: x: 2, y: 2, z: 4, core: 2. Of those that a mesh axis runs over, the one named last changes fastest.
Arguments:
- inputs: bfloat16 [8192, 768], P(('wide', 'narrow')), may hold values from -6 to 6
- memory: bfloat16 [8192, 768], P(('wide', 'narrow')), may hold values from -6 to 6
- segment_ids: int32 [8, 1024], P('wide'), may hold values from 0 to 3, never falling along the last dimension, each value on 1 to 512 neighbouring positions
- memory_ids: int32 [8, 1024], P('wide'), may hold values from 0 to 3, never falling along the last dimension, each value on 1 to 512 neighbouring positions
- self_gain: float32 [768], replicated, may hold values from 0.25 to 1.75
- self_query: bfloat16 [768, 768], P('wide', 'narrow'), may hold values from -0.02734375 to 0.02734375
- self_key: bfloat16 [768, 768], P('wide', 'narrow'), may hold values from -0.21875 to 0.21875
- self_value: bfloat16 [768, 768], P('wide', 'narrow'), may hold values from -0.21875 to 0.21875
- self_out: bfloat16 [768, 768], P('narrow', 'wide'), may hold values from -1.75 to 1.75
- bias_table: float32 [32, 12], P(None, 'narrow'), may hold values from -4 to 4
- cross_gain: float32 [768], replicated, may hold values from 0.25 to 1.75
- cross_query: bfloat16 [768, 768], P('wide', 'narrow'), may hold values from -0.02734375 to 0.02734375
- cross_key: bfloat16 [768, 768], P('wide', 'narrow'), may hold values from -0.21875 to 0.21875
- cross_value: bfloat16 [768, 768], P('wide', 'narrow'), may hold values from -0.21875 to 0.21875
- cross_out: bfloat16 [768, 768], P('narrow', 'wide'), may hold values from -1.75 to 1.75
- ff_gain: float32 [768], replicated, may hold values from 0.25 to 1.75
- ff_gate: bfloat16 [768, 2048], P('wide', 'narrow'), may hold values from -0.21875 to 0.21875
- ff_up: bfloat16 [768, 2048], P('wide', 'narrow'), may hold values from -0.21875 to 0.21875
- ff_down: bfloat16 [2048, 768], P('narrow', 'wide'), may hold values from -0.1875 to 0.1875
- cotangent: bfloat16 [8192, 768], P(('wide', 'narrow')), may hold values from -6 to 6
Outputs:
- output: bfloat16 [8192, 768], P(('wide', 'narrow'))
- grad_inputs: bfloat16 [8192, 768], P(('wide', 'narrow'))
- grad_memory: bfloat16 [8192, 768], P(('wide', 'narrow'))
- grad_self_gain: float32 [768], replicated
- grad_self_query: float32 [768, 768], P('wide', 'narrow')
- grad_self_key: float32 [768, 768], P('wide', 'narrow')
- grad_self_value: float32 [768, 768], P('wide', 'narrow')
- grad_self_out: float32 [768, 768], P('narrow', 'wide')
- grad_bias_table: float32 [32, 12], replicated
- grad_cross_gain: float32 [768], replicated
- grad_cross_query: float32 [768, 768], P('wide', 'narrow')
- grad_cross_key: float32 [768, 768], P('wide', 'narrow')
- grad_cross_value: float32 [768, 768], P('wide', 'narrow')
- grad_cross_out: float32 [768, 768], P('narrow', 'wide')
- grad_ff_gain: float32 [768], replicated
- grad_ff_gate: float32 [768, 2048], P('wide', 'narrow')
- grad_ff_up: float32 [768, 2048], P('wide', 'narrow')
- grad_ff_down: float32 [2048, 768], P('narrow', 'wide')
The draws below stay inside these ranges and needn't reach their ends.
Inputs may be any that keep to these rules, and one draw needn't show every extreme that they name: `segment_ids`: along each row the ids never fall; every id of 0 to 3 holds 1 to 512 positions, one exactly 512. `memory_ids`: along each row the ids never fall; every id of 0 to 3 holds 1 to 512 positions, one exactly 512.
All inputs are finite; a program needn't handle non-finite values.
Results may differ from the reference program's by a relative error of at most 0.024.
Values may be sent and summed in bfloat16 or wider, within the bound.
A program may use at most 192 MiB of HBM per device.

```python
import math
import jax
import jax.numpy as jnp
import numpy as np
from jax import lax

D = 768
H = 12
DH = 64
FF = 2048
NB = 32
MAX_DIST = 128
SEQ = 1024
MEM = 1024
DOCS = 4
SEQUENCES = 8
TOKENS = 8192
MEM_TOKENS = 8192


def shard_levels(own_key, dims, split, low, top_value):
    gain = 1.0
    for dim, shards_of in split:
        heights = jax.random.uniform(jax.random.fold_in(jax.random.fold_in(own_key, 6), dim), (shards_of,), jnp.float32, low / len(split), top_value / len(split))
        gain = gain * jnp.repeat(jnp.exp(heights), dims[dim] // shards_of).reshape((-1,) + (1,) * (len(dims) - 1 - dim))
    return gain


def length_profile(count, total, most, lean):
    weights = [(1 << 20) // math.isqrt(standing ** lean) + 1 for standing in range(2, count + 1)]
    surplus, counts = total - most - (count - 1), [1] * (count - 1)
    while surplus > 0:
        candidates = [i for i in range(count - 1) if counts[i] < most]
        whole, remaining = sum([weights[i] for i in candidates]), surplus
        for i in candidates:
            addition = min(most - counts[i], max(1, remaining * weights[i] // whole), surplus)
            counts[i] = counts[i] + addition
            surplus = surplus - addition
    return np.array([most] + counts)


def uneven(key, count, total, most, slope):
    if count == 2:
        one = jax.random.randint(key, (), max(1, total - most), min(most, total - 1) + 1)
        return jnp.stack([one, total - one])
    lengths = jnp.asarray(length_profile(count, total, most, slope), jnp.int32)
    twos = (count - 1) // 2
    source_of, sink = lengths[1:1 + 2 * twos:2], lengths[2:2 + 2 * twos:2]
    slack = jnp.minimum(source_of - 1, most - sink)
    shifted = jax.random.randint(jax.random.fold_in(key, 1), (twos,), 0, 1 << 20) % (slack + 1)
    lengths = lengths.at[1:1 + 2 * twos:2].set(source_of - shifted).at[2:2 + 2 * twos:2].set(sink + shifted)
    return lengths[jax.random.permutation(jax.random.fold_in(key, 2), count)]


def centred(key, extent, scale, most, pieces=(), kind=jnp.bfloat16):
    factor_of = shard_levels(key, extent, pieces, -0.22, 0.18) if pieces else 1.0
    values = jax.random.normal(key, extent, jnp.float32) * scale * factor_of
    return jnp.minimum(jnp.maximum(values, -most), most).astype(kind)


def setup_inputs(seed: int = 0) -> dict:
    seeds = jax.random.split(jax.random.key(seed), 21)
    inputs = centred(seeds[0], (TOKENS, D), 1.0, 6.0, ((0, 32),))
    memory = centred(seeds[1], (MEM_TOKENS, D), 1.0, 6.0, ((0, 32),))
    segment_ids = jax.vmap(lambda own: jnp.searchsorted(jnp.cumsum(uneven(own, DOCS, SEQ, SEQ // 2, 0)), jnp.arange(SEQ), side="right"))(jax.random.split(seeds[2], SEQUENCES)).reshape((SEQUENCES, SEQ)).astype(jnp.int32)
    memory_ids = jax.vmap(lambda own: jnp.searchsorted(jnp.cumsum(uneven(own, DOCS, MEM, MEM // 2, 0)), jnp.arange(MEM), side="right"))(jax.random.split(seeds[3], SEQUENCES)).reshape((SEQUENCES, MEM)).astype(jnp.int32)
    self_gain = jnp.clip(1.0 + 0.15 * jax.random.normal(seeds[4], (D,), jnp.float32), 0.25, 1.75)
    self_query = centred(seeds[5], (D, H * DH), (D * DH) ** -0.5, 0.02734375, ((0, 8), (1, 4)))
    self_key = centred(seeds[6], (D, H * DH), D ** -0.5, 0.21875, ((0, 8), (1, 4)))
    self_value = centred(seeds[7], (D, H * DH), D ** -0.5, 0.21875, ((0, 8), (1, 4)))
    self_out = centred(seeds[8], (H * DH, D), (max(1, H * DH // 64)) ** -0.5, 1.75, ((0, 4), (1, 8)))
    bias_table = centred(seeds[9], (NB, H), 1.0, 4.0, ((1, 4),), jnp.float32)
    cross_gain = jnp.clip(1.0 + 0.15 * jax.random.normal(seeds[10], (D,), jnp.float32), 0.25, 1.75)
    cross_query = centred(seeds[11], (D, H * DH), (D * DH) ** -0.5, 0.02734375, ((0, 8), (1, 4)))
    cross_key = centred(seeds[12], (D, H * DH), D ** -0.5, 0.21875, ((0, 8), (1, 4)))
    cross_value = centred(seeds[13], (D, H * DH), D ** -0.5, 0.21875, ((0, 8), (1, 4)))
    cross_out = centred(seeds[14], (H * DH, D), (max(1, H * DH // 64)) ** -0.5, 1.75, ((0, 4), (1, 8)))
    ff_gain = jnp.clip(1.0 + 0.15 * jax.random.normal(seeds[15], (D,), jnp.float32), 0.25, 1.75)
    ff_gate = centred(seeds[16], (D, FF), D ** -0.5, 0.21875, ((0, 8), (1, 4)))
    ff_up = centred(seeds[17], (D, FF), D ** -0.5, 0.21875, ((0, 8), (1, 4)))
    ff_down = centred(seeds[18], (FF, D), (FF // 2) ** -0.5, 0.1875, ((0, 4), (1, 8)))
    cotangent = centred(seeds[19], (TOKENS, D), 1.0, 6.0, ((0, 32),))
    return dict(inputs=inputs, memory=memory, segment_ids=segment_ids, memory_ids=memory_ids, self_gain=self_gain, self_query=self_query, self_key=self_key, self_value=self_value, self_out=self_out, bias_table=bias_table, cross_gain=cross_gain, cross_query=cross_query, cross_key=cross_key, cross_value=cross_value, cross_out=cross_out, ff_gain=ff_gain, ff_gate=ff_gate, ff_up=ff_up, ff_down=ff_down, cotangent=cotangent)


@jax.custom_vjp
def low(v):
    return lax.optimization_barrier(v.astype(jnp.bfloat16)).astype(jnp.float32)

@jax.custom_vjp
def low_back(v):
    return v

def low_keep(v):
    return (low(v), None)

def low_pass(kept, grad):
    return (grad,)

def back_keep(v):
    return (v, None)

def back_low(kept, grad):
    return (low(grad),)
low.defvjp(low_keep, low_pass)
low_back.defvjp(back_keep, back_low)

def bucket_table(length, buckets, reach):
    exact_part = buckets // 2
    distance = np.arange(length)
    spread = np.log(np.maximum(distance, exact_part) / exact_part) / np.log(reach / exact_part) * (buckets - exact_part)
    far_bucket = np.minimum(exact_part + np.floor(spread).astype(np.int64), buckets - 1)
    return np.where(distance < exact_part, distance, far_bucket).astype(np.int32)

def rms_norm(values, norm_gain):
    factor = lax.rsqrt(lax.optimization_barrier(jnp.mean(values * values, axis=-1, keepdims=True)) + 1e-06)
    return values * factor * norm_gain

def gelu_tanh(values):
    return 0.5 * values * (1.0 + jnp.tanh(math.sqrt(2.0 / math.pi) * (values + 0.044715 * values * values * values)))

def project(left, right):
    return jnp.dot(left, right, precision=lax.Precision.HIGHEST)

def heads_product(queries, key_rows):
    q_heads = queries.reshape(queries.shape[0], H, DH)
    k_heads = key_rows.reshape(key_rows.shape[0], H, DH)
    return jnp.einsum('qhd,khd->hqk', q_heads, k_heads, precision=lax.Precision.HIGHEST)

def masked_softmax(scores, allowed):
    masked = jnp.where(allowed, scores, -1000000000.0)
    peak = lax.optimization_barrier(jnp.max(masked, axis=-1, keepdims=True))
    expons = jnp.exp(masked - peak)
    return expons / lax.optimization_barrier(jnp.sum(expons, axis=-1, keepdims=True))

def weighted(probs, value_rows):
    v_heads = value_rows.reshape(value_rows.shape[0], H, DH)
    context = jnp.einsum('hqk,khd->qhd', low(probs), v_heads, precision=lax.Precision.HIGHEST)
    return low(low_back(context.reshape(context.shape[0], H * DH)))

def by_rows(values, length):
    return values.reshape(SEQUENCES, length, values.shape[-1])

def layer(inputs, memory, self_gain, self_query, self_key, self_value, self_out, bias_table, cross_gain, cross_query, cross_key, cross_value, cross_out, ff_gain, ff_gate, ff_up, ff_down, segment_ids, memory_ids):
    normed = low(rms_norm(inputs, self_gain))
    queries = low(low_back(project(normed, self_query)))
    key_rows = low(low_back(project(normed, self_key)))
    value_rows = low(low_back(project(normed, self_value)))
    buckets = jnp.asarray(bucket_table(SEQ, NB, MAX_DIST))
    positions = jnp.arange(SEQ, dtype=jnp.int32)
    distance = positions[:, None] - positions[None, :]
    bias = jnp.transpose(bias_table[buckets[jnp.maximum(distance, 0)]], (2, 0, 1))
    causal = distance >= 0

    def self_one(item):
        q_seq, k_seq, v_seq, id_row = item
        scores = low_back(heads_product(q_seq, k_seq) + bias)
        allowed = (id_row[:, None] == id_row[None, :]) & causal
        return weighted(masked_softmax(scores, allowed[None]), v_seq)
    context = lax.map(jax.checkpoint(self_one), (by_rows(queries, SEQ), by_rows(key_rows, SEQ), by_rows(value_rows, SEQ), segment_ids))
    x_two = inputs + low_back(project(context.reshape(TOKENS, H * DH), self_out))
    normed_cross = low(rms_norm(x_two, cross_gain))
    cross_q = low(low_back(project(normed_cross, cross_query)))
    cross_k = low(low_back(project(memory, cross_key)))
    cross_v = low(low_back(project(memory, cross_value)))

    def cross_one(item):
        q_seq, k_seq, v_seq, id_row, memory_row = item
        scores = low_back(heads_product(q_seq, k_seq))
        allowed = id_row[:, None] == memory_row[None, :]
        return weighted(masked_softmax(scores, allowed[None]), v_seq)
    context_cross = lax.map(jax.checkpoint(cross_one), (by_rows(cross_q, SEQ), by_rows(cross_k, MEM), by_rows(cross_v, MEM), segment_ids, memory_ids))
    x_three = x_two + low_back(project(context_cross.reshape(TOKENS, H * DH), cross_out))
    normed_ff = low(rms_norm(x_three, ff_gain))
    gate_vals = low_back(project(normed_ff, ff_gate))
    up_vals = low_back(project(normed_ff, ff_up))
    hidden = low(gelu_tanh(gate_vals) * up_vals)
    return x_three + low_back(project(hidden, ff_down))

def reference(inputs, memory, segment_ids, memory_ids, self_gain, self_query, self_key, self_value, self_out, bias_table, cross_gain, cross_query, cross_key, cross_value, cross_out, ff_gain, ff_gate, ff_up, ff_down, cotangent):
    floats = tuple((arr.astype(jnp.float32) for arr in (inputs, memory, self_gain, self_query, self_key, self_value, self_out, bias_table, cross_gain, cross_query, cross_key, cross_value, cross_out, ff_gain, ff_gate, ff_up, ff_down)))

    def forward(*params):
        return layer(*params, segment_ids, memory_ids)
    result, pullback = jax.vjp(forward, *floats)
    grads = pullback(cotangent.astype(jnp.float32))
    return (result.astype(jnp.bfloat16), grads[0].astype(jnp.bfloat16), grads[1].astype(jnp.bfloat16), grads[2], grads[3], grads[4], grads[5], grads[6], grads[7], grads[8], grads[9], grads[10], grads[11], grads[12], grads[13], grads[14], grads[15], grads[16])
```

```python
import functools
import math

import jax
import jax.numpy as jnp
import numpy as np
from jax import lax
from jax.experimental import pallas as pl
from jax.experimental.pallas import tpu as pltpu
from jax.sharding import PartitionSpec as P

DH = 64
NB = 32
MAX_DIST = 128
EPS = 1e-06
NEG = -1e30
QB = 256
ROW_CHUNKS = 4
MESH = pl.DeviceIdType.MESH
F32 = jnp.float32
BF16 = jnp.bfloat16


def bucket_table(length, buckets, reach):
    exact_part = buckets // 2
    distance = np.arange(length)
    spread = (
        np.log(np.maximum(distance, exact_part) / exact_part)
        / np.log(reach / exact_part)
        * (buckets - exact_part)
    )
    far_bucket = np.minimum(exact_part + np.floor(spread).astype(np.int64), buckets - 1)
    return np.where(distance < exact_part, distance, far_bucket).astype(np.int32)


class Spot:
    def __init__(self, wide_split):
        n = lax.axis_index("narrow")
        self.n = n
        self.x = n // 2
        self.c = n % 2
        self.sib = self.x * 2 + (1 - self.c)
        self.xp = (1 - self.x) * 2 + self.c
        self.xsib = (1 - self.x) * 2 + (1 - self.c)
        self.wide_split = wide_split
        if wide_split:
            w = lax.axis_index("wide")
            self.w = w
            self.z = w // 2
            self.y = w % 2
            self.yp = self.z * 2 + (1 - self.y)

    def at_n(self, n):
        return {"narrow": n}

    def at_w(self, w):
        return {"wide": w}


def remote(src, dst, send, recv, dev):
    return pltpu.make_async_remote_copy(
        src_ref=src, dst_ref=dst, send_sem=send, recv_sem=recv, device_id=dev, device_id_type=MESH
    )


def greet(spot, use_zy, use_all_z=False):
    barrier = pltpu.get_barrier_semaphore()

    def hello(dev):
        pl.semaphore_signal(barrier, inc=1, device_id=dev, device_id_type=MESH)

    hello(spot.at_n(spot.sib))
    hello(spot.at_n(spot.xp))
    count = 2
    if use_zy:
        hello(spot.at_w(spot.yp))
        count = count + 1
        if use_all_z:
            for step in range(1, 4):
                hello(spot.at_w(((spot.z + step) % 4) * 2 + spot.y))
            count = count + 3
        else:

            @pl.when(spot.z > 0)
            def _():
                hello(spot.at_w(spot.w - 2))

            @pl.when(spot.z < 3)
            def _():
                hello(spot.at_w(spot.w + 2))

            inner = jnp.where(jnp.logical_and(spot.z > 0, spot.z < 3), 1, 0)
            count = count + 1 + inner
    pl.semaphore_wait(barrier, count)


class RowGather:
    def __init__(self, name, chunks=ROW_CHUNKS):
        self.name = name
        self.chunks = chunks

    def need(self, scratch):
        dma = pltpu.SemaphoreType.DMA((self.chunks,))
        for part in ("xs", "xr", "ss", "sr", "fs", "fr", "lo"):
            scratch[self.name + part] = dma

    def bind(self, env, spot, src, full):
        self.env, self.spot, self.src, self.full = env, spot, src, full
        self.size = src.shape[0] // self.chunks

    def sem(self, part, k):
        return self.env[self.name + part].at[k]

    def rows(self, k):
        return pl.ds(k * self.size, self.size)

    def to_x(self, k):
        s = self.spot
        return remote(
            self.src.at[self.rows(k)],
            self.full.at[s.n, self.rows(k)],
            self.sem("xs", k),
            self.sem("xr", k),
            s.at_n(s.xp),
        )

    def to_sib(self, k):
        s = self.spot
        return remote(
            self.src.at[self.rows(k)],
            self.full.at[s.n, self.rows(k)],
            self.sem("ss", k),
            self.sem("sr", k),
            s.at_n(s.sib),
        )

    def onward(self, k):
        s = self.spot
        here = self.full.at[s.xp, self.rows(k)]
        return remote(here, here, self.sem("fs", k), self.sem("fr", k), s.at_n(s.sib))

    def local(self, k):
        return pltpu.make_async_copy(
            self.src.at[self.rows(k)],
            self.full.at[self.spot.n, self.rows(k)],
            self.sem("lo", k),
        )

    def send(self, k):
        self.to_x(k).start()
        self.to_sib(k).start()
        self.local(k).start()

    def forward(self, k):
        self.to_x(k).wait_recv()
        self.onward(k).start()

    def finish(self):
        for k in range(self.chunks):
            self.to_sib(k).wait_recv()
            self.onward(k).wait_recv()
            self.to_x(k).wait_send()
            self.to_sib(k).wait_send()
            self.onward(k).wait_send()
            self.local(k).wait()


class RowReduce:
    def __init__(self, name, rows, cols, chunks=ROW_CHUNKS):
        self.name, self.nrows, self.ncols, self.chunks = name, rows, cols, chunks

    def need(self, scratch):
        dma = pltpu.SemaphoreType.DMA((self.chunks,))
        for part in ("as", "ar", "bs", "br", "xs", "xr"):
            scratch[self.name + part] = dma
        shape = (self.nrows, self.ncols)
        for part in ("fars", "owns", "out", "inn"):
            scratch[self.name + part] = pltpu.VMEM(shape, BF16)

    def bind(self, env, spot, part):
        self.env, self.spot, self.part = env, spot, part
        self.size = self.nrows // self.chunks

    def sem(self, part, k):
        return self.env[self.name + part].at[k]

    def rows(self, k):
        return pl.ds(k * self.size, self.size)

    def buf(self, part, k):
        return self.env[self.name + part].at[self.rows(k)]

    def far_sib(self, k):
        s = self.spot
        return remote(
            self.part.at[s.xsib, self.rows(k)],
            self.buf("fars", k),
            self.sem("as", k),
            self.sem("ar", k),
            s.at_n(s.sib),
        )

    def own_sib(self, k):
        s = self.spot
        return remote(
            self.part.at[s.sib, self.rows(k)],
            self.buf("owns", k),
            self.sem("bs", k),
            self.sem("br", k),
            s.at_n(s.sib),
        )

    def across(self, k):
        s = self.spot
        return remote(
            self.buf("out", k), self.buf("inn", k), self.sem("xs", k), self.sem("xr", k), s.at_n(s.xp)
        )

    def open(self):
        for k in range(self.chunks):
            self.far_sib(k).start()
        for k in range(self.chunks):
            self.own_sib(k).start()

    def cross(self, k):
        self.far_sib(k).wait_recv()
        mine = self.part[self.spot.xp, self.rows(k), :].astype(F32)
        self.buf("out", k)[...] = (mine + self.buf("fars", k)[...].astype(F32)).astype(BF16)
        self.across(k).start()

    def total(self, k):
        self.own_sib(k).wait_recv()
        self.across(k).wait_recv()
        mine = self.part[self.spot.n, self.rows(k), :].astype(F32)
        return (mine + self.buf("owns", k)[...].astype(F32)) + self.buf("inn", k)[...].astype(F32)

    def finish(self):
        for k in range(self.chunks):
            self.far_sib(k).wait_send()
            self.own_sib(k).wait_send()
            self.across(k).wait_send()


class WideGather:
    def __init__(self, name, halves=2):
        self.name, self.halves = name, halves

    def need(self, scratch):
        h = self.halves
        scratch[self.name + "rs"] = pltpu.SemaphoreType.DMA((4, h))
        scratch[self.name + "ls"] = pltpu.SemaphoreType.DMA((4, h))
        scratch[self.name + "ys"] = pltpu.SemaphoreType.DMA((7, h))
        scratch[self.name + "rv"] = pltpu.SemaphoreType.DMA((8, h))
        scratch[self.name + "lo"] = pltpu.SemaphoreType.DMA

    def bind(self, env, spot, src, full):
        self.env, self.spot, self.src, self.full = env, spot, src, full
        self.size = src.shape[0] // self.halves

    def hop(self, kind, k, slab, half, own):
        s = self.spot
        dev = {"rs": s.w + 2, "ls": s.w - 2, "ys": s.yp}[kind]
        rows = pl.ds(half * self.size, self.size)
        src = self.src.at[rows] if own else self.full.at[slab, rows]
        return remote(
            src,
            self.full.at[slab, rows],
            self.env[self.name + kind].at[k, half],
            self.env[self.name + "rv"].at[slab, half],
            s.at_w(dev),
        )

    def own_copy(self):
        return pltpu.make_async_copy(
            self.src, self.full.at[self.spot.w], self.env[self.name + "lo"]
        )

    def open(self):
        s = self.spot
        self.own_copy().start()

        @pl.when(s.z < 3)
        def _():
            for half in range(self.halves):
                self.hop("rs", 0, s.w, half, True).start()

        @pl.when(s.z > 0)
        def _():
            for half in range(self.halves):
                self.hop("ls", 0, s.w, half, True).start()

        for half in range(self.halves):
            self.hop("ys", 0, s.w, half, True).start()

    def step(self, k):
        s = self.spot

        @pl.when(s.z - k >= 0)
        def _():
            slab = s.w - 2 * k
            for half in range(self.halves):
                self.hop("rs", k, slab, half, False).wait_recv()

                @pl.when(s.z < 3)
                def _():
                    self.hop("rs", k, slab, half, False).start()

                self.hop("ys", k, slab, half, False).start()

        @pl.when(s.z + k <= 3)
        def _():
            slab = s.w + 2 * k
            for half in range(self.halves):
                self.hop("ls", k, slab, half, False).wait_recv()

                @pl.when(s.z > 0)
                def _():
                    self.hop("ls", k, slab, half, False).start()

                self.hop("ys", 3 + k, slab, half, False).start()

    def finish(self):
        s = self.spot
        self.own_copy().wait()
        for half in range(self.halves):
            for zo in range(4):
                self.hop("ys", 0, zo * 2 + (1 - s.y), half, False).wait_recv()
            self.hop("ys", 0, s.w, half, False).wait_send()

            @pl.when(s.z < 3)
            def _():
                self.hop("rs", 0, s.w, half, False).wait_send()

            @pl.when(s.z > 0)
            def _():
                self.hop("ls", 0, s.w, half, False).wait_send()

            for k in range(1, 4):

                @pl.when(s.z - k >= 0)
                def _():
                    @pl.when(s.z < 3)
                    def _():
                        self.hop("rs", k, s.w - 2 * k, half, False).wait_send()

                    self.hop("ys", k, s.w - 2 * k, half, False).wait_send()

                @pl.when(s.z + k <= 3)
                def _():
                    @pl.when(s.z > 0)
                    def _():
                        self.hop("ls", k, s.w + 2 * k, half, False).wait_send()

                    self.hop("ys", 3 + k, s.w + 2 * k, half, False).wait_send()


class WideReduce:
    def __init__(self, name, rows, cols):
        self.name, self.nrows, self.ncols = name, rows, cols

    def need(self, scratch):
        for part in ("ys", "yr", "rs", "rr", "ls", "lr"):
            scratch[self.name + part] = pltpu.SemaphoreType.DMA((4,))
        shape = (4, self.nrows, self.ncols)
        for part in ("yin", "acc", "rin", "rout", "lin", "lout"):
            scratch[self.name + part] = pltpu.VMEM(shape, BF16)

    def bind(self, env, spot, part):
        self.env, self.spot, self.part = env, spot, part

    def buf(self, part, d):
        return self.env[self.name + part].at[d]

    def sem(self, part, d):
        return self.env[self.name + part].at[d]

    def over_y(self, d):
        s = self.spot
        return remote(
            self.part.at[d * 2 + (1 - s.y)],
            self.buf("yin", d),
            self.sem("ys", d),
            self.sem("yr", d),
            s.at_w(s.yp),
        )

    def right(self, d, first):
        src = self.buf("acc" if first else "rout", d)
        return remote(
            src, self.buf("rin", d), self.sem("rs", d), self.sem("rr", d), self.spot.at_w(self.spot.w + 2)
        )

    def left(self, d, first):
        src = self.buf("acc" if first else "lout", d)
        return remote(
            src, self.buf("lin", d), self.sem("ls", d), self.sem("lr", d), self.spot.at_w(self.spot.w - 2)
        )

    def open(self):
        for d in (3, 0, 2, 1):
            self.over_y(d).start()

    def first(self, d):
        s = self.spot
        self.over_y(d).wait_recv()
        mine = self.part[d * 2 + s.y].astype(F32)
        self.buf("acc", d)[...] = (mine + self.buf("yin", d)[...].astype(F32)).astype(BF16)
        if d > 0:

            @pl.when(s.z == 0)
            def _():
                self.right(d, True).start()

        if d < 3:

            @pl.when(s.z == 3)
            def _():
                self.left(d, True).start()

    def chain_right(self, d):
        s = self.spot

        @pl.when(jnp.logical_and(s.z > 0, s.z < d))
        def _():
            self.right(d, False).wait_recv()
            self.buf("rout", d)[...] = (
                self.buf("rin", d)[...].astype(F32) + self.buf("acc", d)[...].astype(F32)
            ).astype(BF16)
            self.right(d, False).start()

    def chain_left(self, d):
        s = self.spot

        @pl.when(jnp.logical_and(s.z < 3, s.z > d))
        def _():
            self.left(d, False).wait_recv()
            self.buf("lout", d)[...] = (
                self.buf("lin", d)[...].astype(F32) + self.buf("acc", d)[...].astype(F32)
            ).astype(BF16)
            self.left(d, False).start()

    def total(self, out):
        s = self.spot
        for d in range(4):

            @pl.when(s.z == d)
            def _():
                value = self.buf("acc", d)[...].astype(F32)
                if d > 0:
                    self.right(d, False).wait_recv()
                    value = value + self.buf("rin", d)[...].astype(F32)
                if d < 3:
                    self.left(d, False).wait_recv()
                    value = value + self.buf("lin", d)[...].astype(F32)
                out[...] = value

    def finish(self):
        s = self.spot
        for d in range(4):
            self.over_y(d).wait_send()

            @pl.when(s.z < d)
            def _():
                self.right(d, False).wait_send()

            @pl.when(s.z > d)
            def _():
                self.left(d, False).wait_send()


class SmallSum:
    def __init__(self, name, rows, cols):
        self.name, self.shape = name, (rows, cols)

    def need(self, scratch):
        for part in ("s", "r"):
            scratch[self.name + part] = pltpu.SemaphoreType.DMA((3,))
        scratch[self.name + "zs"] = pltpu.SemaphoreType.DMA((4,))
        scratch[self.name + "zr"] = pltpu.SemaphoreType.DMA((4,))
        scratch[self.name + "v"] = pltpu.VMEM((4,) + self.shape, F32)
        scratch[self.name + "in"] = pltpu.VMEM((3,) + self.shape, F32)
        scratch[self.name + "z"] = pltpu.VMEM((4,) + self.shape, F32)

    def run(self, env, spot, value, out):
        held, inn, zin = env[self.name + "v"], env[self.name + "in"], env[self.name + "z"]
        held[0] = value
        devs = (spot.at_n(spot.sib), spot.at_n(spot.xp), spot.at_w(spot.yp))
        copies = []
        for i in range(3):
            copy = remote(
                held.at[i], inn.at[i], env[self.name + "s"].at[i], env[self.name + "r"].at[i], devs[i]
            )
            copy.start()
            copies.append(copy)
            copy.wait_recv()
            held[i + 1] = held[i] + inn[i]
        zin[spot.z] = held[3]

        def hop(step):
            other = (spot.z + step) % 4
            return remote(
                held.at[3],
                zin.at[spot.z],
                env[self.name + "zs"].at[step],
                env[self.name + "zr"].at[spot.z],
                spot.at_w(other * 2 + spot.y),
            )

        def came(step):
            other = (spot.z + step) % 4
            return remote(
                held.at[3],
                zin.at[other],
                env[self.name + "zs"].at[step],
                env[self.name + "zr"].at[other],
                spot.at_w(other * 2 + spot.y),
            )

        for step in range(1, 4):
            hop(step).start()
        for step in range(1, 4):
            came(step).wait_recv()
        out[...] = ((zin[0] + zin[1]) + zin[2]) + zin[3]
        for copy in copies:
            copy.wait_send()
        for step in range(1, 4):
            hop(step).wait_send()


VM = pltpu.VMEM
ANY = pl.ANY


def call(body, inputs, outputs, scratch, cid, name):
    in_names, out_names, scr_names = list(inputs), list(outputs), list(scratch)

    def kernel(*refs):
        body(dict(zip(in_names + out_names + scr_names, refs)))

    results = pl.pallas_call(
        kernel,
        out_shape=[jax.ShapeDtypeStruct(outputs[k][0], outputs[k][1]) for k in out_names],
        in_specs=[pl.BlockSpec(memory_space=inputs[k][1]) for k in in_names],
        out_specs=[pl.BlockSpec(memory_space=outputs[k][2]) for k in out_names],
        scratch_shapes=[scratch[k] for k in scr_names],
        compiler_params=pltpu.CompilerParams(
            collective_id=cid, has_side_effects=True, vmem_limit_bytes=60 * 1024 * 1024
        ),
        name=name,
    )(*[inputs[k][0] for k in in_names])
    return dict(zip(out_names, results))


def mean_square(values):
    return jnp.mean(values * values, axis=-1, keepdims=True)


def norm_rows(values, gain):
    return values * lax.rsqrt(mean_square(values) + EPS) * gain


def norm_back(values, gain, dn):
    r = lax.rsqrt(mean_square(values) + EPS)
    u = values * r
    dg = dn * gain
    rows = r * (dg - u * jnp.mean(dg * u, axis=-1, keepdims=True))
    return rows, jnp.sum(dn * u, axis=0, keepdims=True)


def first_gather(inputs, memory, gain, shard, zy):
    rows, cols = inputs.shape
    scratch = {"own": pltpu.VMEM((rows, cols), BF16)}
    ga, gm, wg = RowGather("ga"), RowGather("gm"), WideGather("wg")
    tasks = [ga, gm] + ([wg] if zy else [])
    for t in tasks:
        t.need(scratch)
    ins = {"x": (inputs, VM), "m": (memory, VM), "g": (gain, VM)}
    outs = {"full": ((4, rows, cols), BF16, ANY), "mem": ((4, rows, cols), BF16, ANY)}
    if zy:
        ins["w"] = (shard, VM)
        outs["wf"] = ((8,) + shard.shape, BF16, ANY)

    def body(env):
        spot = Spot(zy)
        greet(spot, zy)
        ga.bind(env, spot, env["own"], env["full"])
        gm.bind(env, spot, env["m"], env["mem"])
        if zy:
            wg.bind(env, spot, env["w"], env["wf"])
            wg.open()
        for k in range(ga.chunks):
            part = env["x"][ga.rows(k), :].astype(F32)
            env["own"][ga.rows(k), :] = norm_rows(part, env["g"][...]).astype(BF16)
            ga.send(k)
        for k in range(gm.chunks):
            gm.send(k)
        for k in range(ga.chunks):
            ga.forward(k)
            if zy and k in (1, 3):
                wg.step((k + 1) // 2)
        for k in range(gm.chunks):
            gm.forward(k)
            if zy and k == 0:
                wg.step(3)
        ga.finish()
        gm.finish()
        if zy:
            wg.finish()

    return call(body, ins, outs, scratch, 0, "gather_first")


def forward_phase(part, x_rows, gain, shard, zy, extra, cid, name):
    rows, cols = x_rows.shape
    scratch = {"own": pltpu.VMEM((rows, cols), BF16)}
    rr, ga, wg, ge = RowReduce("rr", rows, cols), RowGather("ga"), WideGather("wg"), RowGather("ge")
    tasks = [rr, ga] + ([wg] if zy else []) + ([ge] if extra is not None else [])
    for t in tasks:
        t.need(scratch)
    ins = {"p": (part, VM), "x": (x_rows, VM), "g": (gain, VM)}
    outs = {"sum": ((rows, cols), F32, VM), "full": ((4, rows, cols), BF16, ANY)}
    if zy:
        ins["w"] = (shard, VM)
        outs["wf"] = ((8,) + shard.shape, BF16, ANY)
    if extra is not None:
        ins["e"] = (extra, VM)
        outs["ef"] = ((4, rows, cols), BF16, ANY)

    def body(env):
        spot = Spot(zy)
        greet(spot, zy)
        rr.bind(env, spot, env["p"])
        ga.bind(env, spot, env["own"], env["full"])
        if zy:
            wg.bind(env, spot, env["w"], env["wf"])
            wg.open()
        rr.open()
        for k in range(rr.chunks):
            rr.cross(k)
        for k in range(rr.chunks):
            value = env["x"][rr.rows(k), :].astype(F32) + rr.total(k)
            env["sum"][rr.rows(k), :] = value
            env["own"][rr.rows(k), :] = norm_rows(value, env["g"][...]).astype(BF16)
            ga.send(k)
            if zy and k in (0, 2):
                wg.step(k // 2 + 1)
        if extra is not None:
            ge.bind(env, spot, env["e"], env["ef"])
            for k in range(ge.chunks):
                ge.send(k)
        for k in range(ga.chunks):
            ga.forward(k)
            if zy and k == 0:
                wg.step(3)
        if extra is not None:
            for k in range(ge.chunks):
                ge.forward(k)
            ge.finish()
        rr.finish()
        ga.finish()
        if zy:
            wg.finish()

    return call(body, ins, outs, scratch, cid, name)


def backward_phase(part, values, gain, res, grads, zy, extra, extra_base, last, small, cid, name):
    rows, cols = values.shape
    scratch = {}
    rr = RowReduce("rr", rows, cols)
    ga, re = RowGather("ga"), RowReduce("re", rows, cols)
    tasks = [rr]
    ins = {"p": (part, VM), "v": (values, VM), "g": (gain, VM), "res": (res, VM)}
    outs = {"gg": ((1, cols), F32, VM)}
    if last:
        outs["gx"] = ((rows, cols), BF16, VM)
    else:
        tasks.append(ga)
        scratch["own"] = pltpu.VMEM((rows, cols), BF16)
        outs["sum"] = ((rows, cols), F32, VM)
        outs["full"] = ((4, rows, cols), BF16, ANY)
    if zy:
        wr = WideReduce("wr", grads.shape[1], grads.shape[2])
        tasks.append(wr)
        ins["w"] = (grads, VM)
        outs["wg"] = (grads.shape[1:], F32, VM)
    if extra is not None:
        tasks.append(re)
        ins["e"] = (extra, VM)
        outs["eo"] = ((rows, cols), BF16, VM)
        if extra_base is not None:
            ins["eb"] = (extra_base, VM)
    if small is not None and zy:
        ss = SmallSum("ss", *small.shape)
        tasks.append(ss)
        ins["small"] = (small, VM)
        outs["tot"] = (small.shape, F32, VM)
    for t in tasks:
        t.need(scratch)

    def body(env):
        spot = Spot(zy)
        greet(spot, zy, small is not None)
        rr.bind(env, spot, env["p"])
        if zy:
            wr.bind(env, spot, env["w"])
            wr.open()
        rr.open()
        for k in range(rr.chunks):
            rr.cross(k)
        if not last:
            ga.bind(env, spot, env["own"], env["full"])
        if extra is not None:
            re.bind(env, spot, env["e"])
            re.open()
        order = (3, 0, 2, 1)
        gain_sum = jnp.zeros((1, cols), F32)
        for k in range(rr.chunks):
            dn = rr.total(k)
            add, gsum = norm_back(env["v"][rr.rows(k), :].astype(F32), env["g"][...], dn)
            gain_sum = gain_sum + gsum
            value = env["res"][rr.rows(k), :].astype(F32) + add
            if last:
                env["gx"][rr.rows(k), :] = value.astype(BF16)
            else:
                env["sum"][rr.rows(k), :] = value
                env["own"][rr.rows(k), :] = value.astype(BF16)
                ga.send(k)
            if zy:
                wr.first(order[k])
        env["gg"][...] = gain_sum
        if extra is not None:
            for k in range(re.chunks):
                re.cross(k)
        hops = [
            (wr.chain_right, 3),
            (wr.chain_left, 0),
            (wr.chain_right, 2),
            (wr.chain_left, 1),
        ] if zy else []
        if not last:
            for k in range(ga.chunks):
                ga.forward(k)
                if hops:
                    fn, d = hops.pop(0)
                    fn(d)
        for fn, d in hops:
            fn(d)
        if small is not None and zy:
            row = lax.broadcasted_iota(jnp.int32, small.shape, 0)
            value = jnp.where(row == 0, jnp.broadcast_to(gain_sum, small.shape), env["small"][...])
            ss.run(env, spot, value, env["tot"])
        if extra is not None:
            for k in range(re.chunks):
                value = re.total(k)
                if extra_base is not None:
                    value = env["eb"][re.rows(k), :] + value
                env["eo"][re.rows(k), :] = value.astype(BF16)
            re.finish()
        if zy:
            wr.total(env["wg"])
            wr.finish()
        rr.finish()
        if not last:
            ga.finish()

    return call(body, ins, outs, scratch, cid, name)


def nt(left, right):
    return lax.dot_general(left, right, (((1,), (1,)), ((), ())), preferred_element_type=F32)


def nn(left, right):
    return lax.dot_general(left, right, (((1,), (0,)), ((), ())), preferred_element_type=F32)


def tn(left, right):
    return lax.dot_general(left, right, (((0,), (0,)), ((), ())), preferred_element_type=F32)


def head_rows(values, h):
    lane = lax.broadcasted_iota(jnp.int32, values.shape, 1)
    return jnp.where(lane // DH == h, values, jnp.zeros_like(values))


def make_toeplitz(bias_ref, near_ref, heads):
    for h in range(heads):
        row = jnp.broadcast_to(bias_ref[h], (QB, 2 * QB))
        near_ref[h] = pltpu.roll(row, 0, 1, stride=1, stride_axis=0)


def diagonal_sums(tile):
    rows, width = tile.shape
    while rows > 1:
        rows = rows // 2
        tile = tile[:rows] + pltpu.roll(tile[rows:], width - rows, 1)
    return tile


def fill_mask(mask_ref, segk_ref, segq_ref, qb, nk, causal):
    sq = segq_ref[:, qb * QB : (qb + 1) * QB]
    for first in range(0, nk, QB):
        sk = segk_ref[first : first + QB, :]
        sk = jnp.concatenate([sk] * (QB // sk.shape[1]), axis=1)
        ok = sk == sq
        if causal and first == qb * QB:
            j = lax.broadcasted_iota(jnp.int32, (QB, QB), 0)
            i = lax.broadcasted_iota(jnp.int32, (QB, QB), 1)
            ok = jnp.logical_and(ok, j <= i)
        mask_ref[first : first + QB, :] = jnp.where(ok, 0.0, NEG)


def score_tiles(k_ref, qh, mask_ref, near_ref, far_ref, h, qb, nk, causal):
    tiles = []
    for first in range(0, nk, QB):
        s = nt(k_ref[first : first + QB, :], qh) + mask_ref[first : first + QB, :]
        if causal:
            back = qb - first // QB
            if back == 0:
                s = s + near_ref[h][:, 0:QB]
            elif back == 1:
                s = s + near_ref[h][:, QB : 2 * QB]
            else:
                s = s + far_ref[h]
        tiles.append(s)
    return tiles


def attend_fwd(q, k, vt, segq, segk, bias):
    length, columns = q.shape
    keys = k.shape[0]
    heads = columns // DH
    causal = bias is not None

    def kernel(*refs):
        if causal:
            q_ref, k_ref, vt_ref, sq_ref, sk_ref, b_ref, far_ref, ctx_ref, lse_ref, mask_ref, near_ref = refs
            make_toeplitz(b_ref, near_ref, heads)
        else:
            q_ref, k_ref, vt_ref, sq_ref, sk_ref, ctx_ref, lse_ref, mask_ref = refs
            near_ref = far_ref = None
        for qb in range(length // QB):
            nk = (qb + 1) * QB if causal else keys
            cols = slice(qb * QB, (qb + 1) * QB)
            fill_mask(mask_ref, sk_ref, sq_ref, qb, nk, causal)

            def one(h, carry):
                qh = head_rows(q_ref[cols, :], h)
                tiles = score_tiles(k_ref, qh, mask_ref, near_ref, far_ref, h, qb, nk, causal)
                peak = functools.reduce(
                    jnp.maximum, [jnp.max(t, axis=0, keepdims=True) for t in tiles]
                )
                total = jnp.zeros((1, QB), F32)
                acc = jnp.zeros((DH, QB), F32)
                hrows = pl.ds(pl.multiple_of(h * DH, DH), DH)
                for i, t in enumerate(tiles):
                    e = jnp.exp(t - peak)
                    total = total + jnp.sum(e, axis=0, keepdims=True)
                    acc = acc + nn(vt_ref[hrows, i * QB : (i + 1) * QB], e.astype(BF16))
                ctx_ref[hrows, cols] = (acc / total).astype(BF16)
                lse_ref[h, :, cols] = peak + jnp.log(total)
                return carry

            lax.fori_loop(0, heads, one, 0)

    args = [q, k, vt, segq, segk]
    specs = [pl.BlockSpec(memory_space=VM)] * 5
    scratch = [pltpu.VMEM((keys, QB), F32)]
    if causal:
        args += [bias[0], bias[1]]
        specs += [pl.BlockSpec(memory_space=VM), pl.BlockSpec(memory_space=pltpu.SMEM)]
        scratch.append(pltpu.VMEM((heads, QB, 2 * QB), F32))
    return pl.pallas_call(
        kernel,
        out_shape=[
            jax.ShapeDtypeStruct((columns, length), BF16),
            jax.ShapeDtypeStruct((heads, 1, length), F32),
        ],
        in_specs=specs,
        out_specs=[pl.BlockSpec(memory_space=VM)] * 2,
        scratch_shapes=scratch,
        name="self_fwd" if causal else "cross_fwd",
    )(*args)


def attend_bwd(q, k, kt, v, dctx, segq, segk, lse, bias):
    length, columns = q.shape
    keys = k.shape[0]
    heads = columns // DH
    causal = bias is not None

    def kernel(*refs):
        q_ref, k_ref, kt_ref, v_ref, d_ref, sq_ref, sk_ref, lse_ref = refs[:8]
        refs = refs[8:]
        if causal:
            b_ref, far_ref = refs[:2]
            refs = refs[2:]
            dq_ref, dk_ref, dv_ref, gn_ref, gf_ref = refs[:5]
            dka, dva, mask_ref, near_ref, gnear = refs[5:]
            make_toeplitz(b_ref, near_ref, heads)
            gnear[...] = jnp.zeros_like(gnear)
            gf_ref[...] = jnp.zeros_like(gf_ref)
        else:
            dq_ref, dk_ref, dv_ref, dka, dva, mask_ref = refs
            near_ref = far_ref = None
        dka[...] = jnp.zeros_like(dka)
        dva[...] = jnp.zeros_like(dva)
        for qb in range(length // QB):
            nk = (qb + 1) * QB if causal else keys
            cols = slice(qb * QB, (qb + 1) * QB)
            fill_mask(mask_ref, sk_ref, sq_ref, qb, nk, causal)

            def one(h, carry):
                qh = head_rows(q_ref[cols, :], h)
                dh = head_rows(d_ref[cols, :], h)
                lrow = lse_ref[h, :, cols]
                tiles = score_tiles(k_ref, qh, mask_ref, near_ref, far_ref, h, qb, nk, causal)
                probs, dps = [], []
                delta = jnp.zeros((1, QB), F32)
                for i, t in enumerate(tiles):
                    p = jnp.exp(t - lrow)
                    dp = nt(v_ref[i * QB : (i + 1) * QB, :], dh)
                    delta = delta + jnp.sum(p * dp, axis=0, keepdims=True)
                    dva[i * QB : (i + 1) * QB, :] += nn(p.astype(BF16), dh)
                    probs.append(p)
                    dps.append(dp)
                hrows = pl.ds(pl.multiple_of(h * DH, DH), DH)
                acc = jnp.zeros((DH, QB), F32)
                far_sum = jnp.zeros((1, QB), F32)
                for i, (p, dp) in enumerate(zip(probs, dps)):
                    ds = p * (dp - delta)
                    low = ds.astype(BF16)
                    if causal:
                        back = qb - i
                        if back == 0:
                            gnear[h, :, 0:QB] += ds
                        elif back == 1:
                            gnear[h, :, QB : 2 * QB] += ds
                        else:
                            far_sum = far_sum + jnp.sum(ds, axis=0, keepdims=True)
                    dka[i * QB : (i + 1) * QB, :] += nn(low, qh)
                    acc = acc + nn(kt_ref[hrows, i * QB : (i + 1) * QB], low)
                dq_ref[hrows, cols] = acc.astype(BF16)
                if causal:
                    gf_ref[h] += far_sum
                return carry

            lax.fori_loop(0, heads, one, 0)
        dk_ref[...] = dka[...].astype(BF16)
        dv_ref[...] = dva[...].astype(BF16)
        if causal:
            for h in range(heads):
                gn_ref[h] = diagonal_sums(gnear[h])

    args = [q, k, kt, v, dctx, segq, segk, lse]
    specs = [pl.BlockSpec(memory_space=VM)] * 8
    outs = [
        jax.ShapeDtypeStruct((columns, length), BF16),
        jax.ShapeDtypeStruct((keys, columns), BF16),
        jax.ShapeDtypeStruct((keys, columns), BF16),
    ]
    scratch = [
        pltpu.VMEM((keys, columns), F32),
        pltpu.VMEM((keys, columns), F32),
        pltpu.VMEM((keys, QB), F32),
    ]
    if causal:
        args += [bias[0], bias[1]]
        specs += [pl.BlockSpec(memory_space=VM), pl.BlockSpec(memory_space=pltpu.SMEM)]
        outs += [
            jax.ShapeDtypeStruct((heads, 1, 2 * QB), F32),
            jax.ShapeDtypeStruct((heads, 1, QB), F32),
        ]
        scratch += [pltpu.VMEM((heads, QB, 2 * QB), F32), pltpu.VMEM((heads, QB, 2 * QB), F32)]
    return pl.pallas_call(
        kernel,
        out_shape=outs,
        in_specs=specs,
        out_specs=[pl.BlockSpec(memory_space=VM)] * len(outs),
        scratch_shapes=scratch,
        name="self_bwd" if causal else "cross_bwd",
    )(*args)


def gelu_parts(v):
    c = math.sqrt(2.0 / math.pi)
    t = jnp.tanh(c * (v + 0.044715 * v * v * v))
    value = 0.5 * v * (1.0 + t)
    slope = 0.5 * (1.0 + t) + 0.5 * v * (1.0 - t * t) * c * (1.0 + 3.0 * 0.044715 * v * v)
    return value, slope


def shards(
    zy,
    inputs,
    memory,
    segment_ids,
    memory_ids,
    self_gain,
    self_query,
    self_key,
    self_value,
    self_out,
    bias_table,
    cross_gain,
    cross_query,
    cross_key,
    cross_value,
    cross_out,
    ff_gain,
    ff_gate,
    ff_up,
    ff_down,
    cotangent,
):
    model = inputs.shape[1]
    length = segment_ids.shape[1]
    cols = self_query.shape[1]
    hidden_cols = ff_gate.shape[1]
    heads = cols // DH

    sh_self = jnp.concatenate([self_query, self_key, self_value, self_out.T], axis=1)
    sh_cross = jnp.concatenate([cross_query, cross_key, cross_value, cross_out.T], axis=1)
    sh_ff = jnp.concatenate([ff_gate, ff_up, ff_down.T], axis=1)
    wrows = sh_self.shape[0]
    wide = model // wrows

    def whole(shard):
        return lax.all_gather(shard, "wide", axis=0, tiled=True)

    gain_s, gain_c, gain_f = (g.reshape(1, model) for g in (self_gain, cross_gain, ff_gain))
    segq = segment_ids.reshape(1, length)
    segk_self = jnp.broadcast_to(segment_ids.reshape(length, 1), (length, 128))
    segk_mem = jnp.broadcast_to(memory_ids.reshape(-1, 1), (memory_ids.shape[1], 128))

    buckets = bucket_table(2 * QB, NB, MAX_DIST)
    bias_row = jnp.zeros((heads, 2 * QB), F32)
    where = jnp.asarray(buckets)[None, :]
    for b in range(NB):
        bias_row = jnp.where(where == b, bias_table[b][:, None], bias_row)
    bias = (bias_row.reshape(heads, 1, 2 * QB), bias_table[NB - 1])

    got = first_gather(inputs, memory, gain_s, sh_self, zy)
    w_self = (got["wf"].reshape(model, -1) if zy else whole(sh_self))
    full_self = got["full"].reshape(length, model)
    full_mem = got["mem"].reshape(-1, model)
    wq, wk, wv, wo = (w_self[:, i * cols : (i + 1) * cols] for i in range(4))
    q1 = nn(full_self, wq).astype(BF16)
    k1 = nn(full_self, wk).astype(BF16)
    kt1 = lax.dot_general(wk, full_self, (((0,), (1,)), ((), ())), preferred_element_type=F32).astype(BF16)
    v1 = nn(full_self, wv).astype(BF16)
    vt1 = lax.dot_general(wv, full_self, (((0,), (1,)), ((), ())), preferred_element_type=F32).astype(BF16)
    ctx1, lse1 = attend_fwd(q1, k1, vt1, segq, segk_self, bias)
    part1 = lax.dot_general(ctx1, wo, (((0,), (1,)), ((), ())), preferred_element_type=F32).astype(BF16)

    got = forward_phase(
        part1.reshape(4, -1, model), inputs, gain_c, sh_cross, zy, None, 1, "phase_cross"
    )
    w_cross = (got["wf"].reshape(model, -1) if zy else whole(sh_cross))
    x_two = got["sum"]
    full_cross = got["full"].reshape(length, model)
    cq, ck, cv, co = (w_cross[:, i * cols : (i + 1) * cols] for i in range(4))
    q2 = nn(full_cross, cq).astype(BF16)
    k2 = nn(full_mem, ck).astype(BF16)
    kt2 = lax.dot_general(ck, full_mem, (((0,), (1,)), ((), ())), preferred_element_type=F32).astype(BF16)
    v2 = nn(full_mem, cv).astype(BF16)
    vt2 = lax.dot_general(cv, full_mem, (((0,), (1,)), ((), ())), preferred_element_type=F32).astype(BF16)
    ctx2, lse2 = attend_fwd(q2, k2, vt2, segq, segk_mem, None)
    part2 = lax.dot_general(ctx2, co, (((0,), (1,)), ((), ())), preferred_element_type=F32).astype(BF16)

    got = forward_phase(
        part2.reshape(4, -1, model), x_two, gain_f, sh_ff, zy, cotangent, 2, "phase_ff"
    )
    w_ff = (got["wf"].reshape(model, -1) if zy else whole(sh_ff))
    x_three = got["sum"]
    full_ff = got["full"].reshape(length, model)
    dy3 = got["ef"].reshape(length, model)
    w_gu, w_down_t = w_ff[:, : 2 * hidden_cols], w_ff[:, 2 * hidden_cols :]

    gate_up = nn(full_ff, w_gu)
    gate, up = gate_up[:, :hidden_cols], gate_up[:, hidden_cols:]
    value, slope = gelu_parts(gate)
    hidden = (value * up).astype(BF16)
    part3 = nt(hidden, w_down_t).astype(BF16)
    dhid = nn(dy3, w_down_t)
    dgu = jnp.concatenate([(dhid * up * slope).astype(BF16), (dhid * value).astype(BF16)], axis=1)
    g_ff = jnp.concatenate([tn(full_ff, dgu).astype(BF16), tn(dy3, hidden).astype(BF16)], axis=1)
    dn3 = nt(dgu, w_gu).astype(BF16)

    got = backward_phase(
        dn3.reshape(4, -1, model), x_three, gain_f, cotangent,
        g_ff.reshape(wide, wrows, -1), zy, part3.reshape(4, -1, model), x_three, False, None, 3, "phase_back_ff",
    )
    result = got["eo"]
    g2 = got["sum"]
    dy2 = got["full"].reshape(length, model)
    gg_ff = got["gg"]
    red_ff = got.get("wg")

    dctx2 = nn(dy2, co).astype(BF16)
    dqt2, dk2, dv2 = attend_bwd(q2, k2, kt2, v2, dctx2, segq, segk_mem, lse2, None)
    g_cross = jnp.concatenate(
        [
            lax.dot_general(full_cross, dqt2, (((0,), (1,)), ((), ())), preferred_element_type=F32).astype(BF16),
            tn(full_mem, dk2).astype(BF16),
            tn(full_mem, dv2).astype(BF16),
            lax.dot_general(dy2, ctx2, (((0,), (1,)), ((), ())), preferred_element_type=F32).astype(BF16),
        ],
        axis=1,
    )
    dn2 = lax.dot_general(dqt2, cq, (((0,), (1,)), ((), ())), preferred_element_type=F32).astype(BF16)
    dmem = (nt(dk2, ck) + nt(dv2, cv)).astype(BF16)
    got = backward_phase(
        dn2.reshape(4, -1, model), x_two, gain_c, g2,
        g_cross.reshape(wide, wrows, -1), zy, dmem.reshape(4, -1, model), None, False, None, 4, "phase_back_cross",
    )
    grad_memory = got["eo"]
    g1 = got["sum"]
    dy1 = got["full"].reshape(length, model)
    gg_cross = got["gg"]
    red_cross = got.get("wg")

    dctx1 = nn(dy1, wo).astype(BF16)
    dqt1, dk1, dv1, g_near, g_far = attend_bwd(q1, k1, kt1, v1, dctx1, segq, segk_self, lse1, bias)
    g_self = jnp.concatenate(
        [
            lax.dot_general(full_self, dqt1, (((0,), (1,)), ((), ())), preferred_element_type=F32).astype(BF16),
            tn(full_self, dk1).astype(BF16),
            tn(full_self, dv1).astype(BF16),
            lax.dot_general(dy1, ctx1, (((0,), (1,)), ((), ())), preferred_element_type=F32).astype(BF16),
        ],
        axis=1,
    )
    dn1 = (
        lax.dot_general(dqt1, wq, (((0,), (1,)), ((), ())), preferred_element_type=F32)
        + nt(dk1, wk)
        + nt(dv1, wv)
    ).astype(BF16)

    pick = jnp.asarray((buckets[:, None] == np.arange(NB)[None, :]).astype(np.float32))
    table = jnp.sum(pick[:, :, None] * g_near.reshape(heads, 2 * QB).T[:, None, :], axis=0)
    far = jnp.sum(g_far, axis=(1, 2))
    table = jnp.where(jnp.arange(NB)[:, None] == NB - 1, table + far[None, :], table)
    place = (jnp.arange(4, dtype=jnp.int32) == lax.axis_index("narrow")).astype(F32)
    table = (place[None, :, None] * table[:, None, :]).reshape(1, NB * 4 * heads)
    small = jnp.concatenate(
        [
            jnp.zeros((1, model), F32),
            gg_cross,
            gg_ff,
            jnp.pad(table, ((0, 0), (0, model - table.shape[1]))),
            jnp.zeros((4, model), F32),
        ],
        axis=0,
    )
    got = backward_phase(
        dn1.reshape(4, -1, model), inputs, gain_s, g1,
        g_self.reshape(wide, wrows, -1), zy, None, None, True, small, 5, "phase_back_self",
    )
    grad_inputs = got["gx"]
    if zy:
        total = got["tot"]
        red_self = got["wg"]
    else:
        total = lax.psum(small.at[0].set(got["gg"][0]), ("wide", "narrow"))

        def scatter(g):
            return lax.psum_scatter(g, "wide", scatter_dimension=0, tiled=True).astype(F32)

        red_self, red_cross, red_ff = scatter(g_self), scatter(g_cross), scatter(g_ff)

    def four(red):
        return [red[:, i * cols : (i + 1) * cols] for i in range(3)] + [red[:, 3 * cols :].T]

    s_self, s_cross = four(red_self), four(red_cross)
    return (
        result,
        grad_inputs,
        grad_memory,
        total[0],
        *s_self,
        total[3, : NB * 4 * heads].reshape(NB, 4 * heads),
        total[1],
        *s_cross,
        total[2],
        red_ff[:, :hidden_cols],
        red_ff[:, hidden_cols : 2 * hidden_cols],
        red_ff[:, 2 * hidden_cols :].T,
    )


def solution(mesh):
    zy = mesh.shape["wide"] == 8
    rows = P(("wide", "narrow"), None)
    w_in, w_out = P("wide", "narrow"), P("narrow", "wide")
    placed = (
        rows, rows, P("wide", None), P("wide", None), P(),
        w_in, w_in, w_in, w_out, P(None, "narrow"), P(),
        w_in, w_in, w_in, w_out, P(), w_in, w_in, w_out, rows,
    )
    outs = (
        rows, rows, rows, P(), w_in, w_in, w_in, w_out, P(), P(),
        w_in, w_in, w_in, w_out, P(), w_in, w_in, w_out,
    )
    return jax.shard_map(
        functools.partial(shards, zy), mesh=mesh, in_specs=placed, out_specs=outs, check_vma=False
    )
```

```python
import math
from types import SimpleNamespace

import jax
import jax.numpy as jnp
import numpy as np
from jax import lax
from jax.experimental import pallas as pl
from jax.experimental.pallas import tpu as pltpu
from jax.sharding import PartitionSpec as P

DH = 64
NB = 32
MAX_DIST = 128
EPS = 1e-06
NEG = -1e30
QB = 256
ROW_CHUNKS = 4
WIDE = "wide"
NARROW = "narrow"
MESH = pl.DeviceIdType.MESH
F32 = jnp.float32
BF16 = jnp.bfloat16
VM = pltpu.VMEM
DMA = pltpu.SemaphoreType.DMA


def bucket_table(length, buckets, reach):
    exact_part = buckets // 2
    distance = np.arange(length)
    spread = (
        np.log(np.maximum(distance, exact_part) / exact_part)
        / np.log(reach / exact_part)
        * (buckets - exact_part)
    )
    far_bucket = np.minimum(exact_part + np.floor(spread).astype(np.int64), buckets - 1)
    return np.where(distance < exact_part, distance, far_bucket).astype(np.int32)


def bucket_ranges(length):
    table = bucket_table(length, NB, MAX_DIST)
    found = []
    for which in range(NB):
        places = np.nonzero(table == which)[0]
        if len(places):
            found.append((which, int(places[0]), int(places[-1]) + 1))
    return found


class Slots:
    def __init__(self):
        self.items = []

    def add(self, holder, **specs):
        for name, spec in specs.items():
            self.items.append((holder, name, spec))

    def fill(self, refs):
        for (holder, name, _), ref in zip(self.items, refs):
            setattr(holder, name, ref)


def run_kernel(body, ins, outs, scratch, cid, name):
    counts = len(ins.items), len(outs.items)

    def kernel(*refs):
        ins.fill(refs[: counts[0]])
        outs.fill(refs[counts[0] : counts[0] + counts[1]])
        scratch.fill(refs[counts[0] + counts[1] :])
        body()

    params = {} if cid is None else dict(collective_id=cid, has_side_effects=True)
    return pl.pallas_call(
        kernel,
        out_shape=[jax.ShapeDtypeStruct(*spec) for _, _, spec in outs.items],
        in_specs=[pl.BlockSpec(memory_space=spec[1]) for _, _, spec in ins.items],
        out_specs=[pl.BlockSpec(memory_space=VM) for _ in outs.items],
        scratch_shapes=[spec for _, _, spec in scratch.items],
        compiler_params=pltpu.CompilerParams(vmem_limit_bytes=66_900_000, **params),
        name=name,
    )(*[spec[0] for _, _, spec in ins.items])


class Spot:
    def __init__(self, wide_split):
        n = lax.axis_index(NARROW)
        self.n = n
        self.x = n // 2
        self.c = n % 2
        self.sib = self.x * 2 + (1 - self.c)
        self.xp = (1 - self.x) * 2 + self.c
        self.xsib = (1 - self.x) * 2 + (1 - self.c)
        if wide_split:
            w = lax.axis_index(WIDE)
            self.w = w
            self.z = w // 2
            self.y = w % 2
            self.yp = self.z * 2 + (1 - self.y)

    def at_n(self, n):
        return {NARROW: n}

    def at_w(self, w):
        return {WIDE: w}

    def at_z(self, z):
        return {WIDE: z * 2 + self.y}


def remote(src, dst, send, recv, dev):
    return pltpu.make_async_remote_copy(
        src_ref=src, dst_ref=dst, send_sem=send, recv_sem=recv, device_id=dev, device_id_type=MESH
    )


def greet(spot, zy):
    barrier = pltpu.get_barrier_semaphore()

    def hello(dev):
        pl.semaphore_signal(barrier, inc=1, device_id=dev, device_id_type=MESH)

    hello(spot.at_n(spot.sib))
    hello(spot.at_n(spot.xp))
    if zy:
        hello(spot.at_w(spot.yp))
        for step in range(1, 4):
            hello(spot.at_z((spot.z + step) % 4))
    pl.semaphore_wait(barrier, 6 if zy else 2)


def aligned(start, size):
    return pl.ds(pl.multiple_of(start, 16), size)


class RowGather:
    def __init__(self, slots, rows, chunks=ROW_CHUNKS):
        self.nrows, self.chunks, self.size = rows, chunks, rows // chunks
        sems = DMA((chunks,))
        slots.add(self, xs=sems, xr=sems, ss=sems, sr=sems, fs=sems, fr=sems)

    def bind(self, spot, full):
        self.spot, self.full = spot, full

    def hop(self, k, block, dev, send, recv):
        rows = self.full.at[aligned(block * self.nrows + k * self.size, self.size)]
        return remote(rows, rows, send.at[k], recv.at[k], self.spot.at_n(dev))

    def to_x(self, k):
        return self.hop(k, self.spot.n, self.spot.xp, self.xs, self.xr)

    def from_x(self, k):
        return self.hop(k, self.spot.xp, self.spot.xp, self.xs, self.xr)

    def to_sib(self, k):
        return self.hop(k, self.spot.n, self.spot.sib, self.ss, self.sr)

    def from_sib(self, k):
        return self.hop(k, self.spot.sib, self.spot.sib, self.ss, self.sr)

    def onward(self, k):
        return self.hop(k, self.spot.xp, self.spot.sib, self.fs, self.fr)

    def from_onward(self, k):
        return self.hop(k, self.spot.xsib, self.spot.sib, self.fs, self.fr)

    def send(self, k):
        self.to_x(k).start()
        self.to_sib(k).start()

    def send_all(self):
        for k in range(self.chunks):
            self.send(k)

    def forward(self, first, after):
        for k in range(first, after):
            self.from_x(k).wait_recv()
            self.onward(k).start()

    def have_sib(self):
        for k in range(self.chunks):
            self.from_sib(k).wait_recv()

    def have_xsib(self):
        for k in range(self.chunks):
            self.from_onward(k).wait_recv()

    def finish(self):
        for k in range(self.chunks):
            self.to_x(k).wait_send()
            self.to_sib(k).wait_send()
            self.onward(k).wait_send()


class RowReduce:
    def __init__(self, slots, rows, cols, chunks=ROW_CHUNKS):
        self.nrows, self.chunks, self.size = rows, chunks, rows // chunks
        sems, buf = DMA((chunks,)), VM((rows, cols), BF16)
        slots.add(self, as_=sems, ar=sems, bs=sems, br=sems, xs=sems, xr=sems, far=buf, own=buf, inn=buf)

    def bind(self, spot, part):
        self.spot, self.part = spot, part

    def buf(self, ref, k):
        return ref.at[pl.ds(k * self.size, self.size)]

    def mine(self, block, k):
        return self.part.at[aligned(block * self.nrows + k * self.size, self.size)]

    def far_sib(self, k):
        s = self.spot
        return remote(self.mine(s.xsib, k), self.buf(self.far, k), self.as_.at[k], self.ar.at[k], s.at_n(s.sib))

    def own_sib(self, k):
        s = self.spot
        return remote(self.mine(s.sib, k), self.buf(self.own, k), self.bs.at[k], self.br.at[k], s.at_n(s.sib))

    def across(self, k):
        s = self.spot
        return remote(self.buf(self.far, k), self.buf(self.inn, k), self.xs.at[k], self.xr.at[k], s.at_n(s.xp))

    def send_far(self):
        for k in range(self.chunks):
            self.far_sib(k).start()

    def send_own(self):
        for k in range(self.chunks):
            self.own_sib(k).start()

    def cross(self):
        for k in range(self.chunks):
            self.far_sib(k).wait_recv()
            here = self.buf(self.far, k)
            here[...] = (self.mine(self.spot.xp, k)[...].astype(F32) + here[...].astype(F32)).astype(BF16)
            self.across(k).start()

    def total(self, k):
        self.own_sib(k).wait_recv()
        self.across(k).wait_recv()
        value = self.mine(self.spot.n, k)[...].astype(F32) + self.buf(self.own, k)[...].astype(F32)
        return value + self.buf(self.inn, k)[...].astype(F32)

    def finish(self):
        for k in range(self.chunks):
            self.far_sib(k).wait_send()
            self.own_sib(k).wait_send()
            self.across(k).wait_send()


class WideGather:
    steps = (1, -1, 2, -2, 3, -3)

    def __init__(self, slots, rows, halves=2):
        self.nrows, self.halves, self.size = rows, halves, rows // halves
        slots.add(self, zs=DMA((6, halves)), zr=DMA((4, halves)), ys=DMA((4, halves)), yr=DMA((4, halves)))

    def bind(self, spot, full):
        self.spot, self.full = spot, full

    def rows(self, z, y, half):
        return self.full.at[aligned((z * 2 + y) * self.nrows + half * self.size, self.size)]

    def along(self, i, half):
        s = self.spot
        rows = self.rows(s.z, s.y, half)
        return remote(rows, rows, self.zs.at[i, half], self.zr.at[s.z, half], s.at_z(s.z + self.steps[i]))

    def came(self, z, half):
        s = self.spot
        rows = self.rows(z, s.y, half)
        return remote(rows, rows, self.zs.at[0, half], self.zr.at[z, half], s.at_z(z))

    def over(self, z, half):
        s = self.spot
        rows = self.rows(z, s.y, half)
        return remote(rows, rows, self.ys.at[z, half], self.yr.at[z, half], s.at_w(s.yp))

    def crossed(self, z, half):
        s = self.spot
        rows = self.rows(z, 1 - s.y, half)
        return remote(rows, rows, self.ys.at[z, half], self.yr.at[z, half], s.at_w(s.yp))

    def when_inside(self, step, fn):
        there = self.spot.z + step

        @pl.when(there >= 0 if step < 0 else there <= 3)
        def _():
            fn(there)

    def open(self):
        for half in range(self.halves):
            self.over(self.spot.z, half).start()
        for i, step in enumerate(self.steps):
            for half in range(self.halves):
                self.when_inside(step, lambda there: self.along(i, half).start())

    def forward(self, distance):
        for half in range(self.halves):
            for step in (distance, -distance):

                def pass_on(there):
                    self.came(there, half).wait_recv()
                    self.over(there, half).start()

                self.when_inside(step, pass_on)

    def have(self):
        for half in range(self.halves):
            for z in range(4):
                self.crossed(z, half).wait_recv()

    def finish(self):
        for half in range(self.halves):
            for z in range(4):
                self.over(z, half).wait_send()
            for i, step in enumerate(self.steps):
                self.when_inside(step, lambda there: self.along(i, half).wait_send())


class WideReduce:
    steps = (2, 3, 1, 0)

    def __init__(self, slots, rows, cols, width):
        self.nrows, self.width, self.chunks = rows, width, cols // width
        sems, buf = DMA((self.chunks, 4)), VM((4, rows, cols), BF16)
        slots.add(self, ys=sems, yr=sems, zs=sems, zr=sems, acc=buf, inn=buf)

    def bind(self, spot, part, out, out_col):
        self.spot, self.part, self.out, self.out_col = spot, part, out, out_col

    def cols(self, c):
        return pl.ds(c * self.width, self.width)

    def slab(self, c, z, y):
        return self.part.at[aligned((z * 2 + y) * self.nrows, self.nrows), self.cols(c)]

    def over(self, c, z):
        s = self.spot
        return remote(
            self.slab(c, z, 1 - s.y), self.acc.at[z, :, self.cols(c)], self.ys.at[c, z], self.yr.at[c, z], s.at_w(s.yp)
        )

    def along(self, c, z):
        s = self.spot
        return remote(
            self.acc.at[z, :, self.cols(c)], self.inn.at[s.z, :, self.cols(c)],
            self.zs.at[c, z], self.zr.at[c, s.z], s.at_z(z),
        )

    def came(self, c, z):
        here = self.inn.at[z, :, self.cols(c)]
        return remote(here, here, self.zs.at[c, z], self.zr.at[c, z], self.spot.at_z(z))

    def targets(self):
        return [(self.spot.z + step) % 4 for step in self.steps]

    def open(self, c):
        for z in self.targets():
            self.over(c, z).start()

    def first(self, c):
        for step, z in zip(self.steps, self.targets()):
            self.over(c, z).wait_recv()
            here = self.acc.at[z, :, self.cols(c)]
            here[...] = (self.slab(c, z, self.spot.y)[...].astype(F32) + here[...].astype(F32)).astype(BF16)
            if step:
                self.along(c, z).start()

    def total(self, c):
        value = self.acc[self.spot.z, :, self.cols(c)].astype(F32)
        for z in self.targets()[:3]:
            self.came(c, z).wait_recv()
            value = value + self.inn[z, :, self.cols(c)].astype(F32)
        self.out[:, pl.ds(self.out_col + c * self.width, self.width)] = value

    def finish(self):
        for c in range(self.chunks):
            for step, z in zip(self.steps, self.targets()):
                self.over(c, z).wait_send()
                if step:
                    self.along(c, z).wait_send()


class SmallSum:
    def __init__(self, slots, rows, cols):
        four = VM((4, rows, cols), F32)
        slots.add(
            self, ps=DMA((3,)), pr=DMA((3,)), zs=DMA((4,)), zr=DMA((4,)), held=four, inn=VM((3, rows, cols), F32), zin=four
        )

    def run(self, spot, value, out):
        held, inn, zin = self.held, self.inn, self.zin
        held[0] = value
        devs = (spot.at_n(spot.sib), spot.at_n(spot.xp), spot.at_w(spot.yp))
        copies = []
        for i in range(3):
            copy = remote(held.at[i], inn.at[i], self.ps.at[i], self.pr.at[i], devs[i])
            copy.start()
            copies.append(copy)
            copy.wait_recv()
            held[i + 1] = held[i] + inn[i]
        zin[spot.z] = held[3]

        def hop(step, landed):
            other = (spot.z + step) % 4
            return remote(
                held.at[3], zin.at[landed], self.zs.at[step], self.zr.at[landed], spot.at_z(other)
            )

        for step in range(1, 4):
            hop(step, spot.z).start()
        for step in range(1, 4):
            hop(step, (spot.z + step) % 4).wait_recv()
        out[...] = ((zin[0] + zin[1]) + zin[2]) + zin[3]
        for copy in copies:
            copy.wait_send()
        for step in range(1, 4):
            hop(step, spot.z).wait_send()


class Idle:
    chunks = 0

    def bind(self, *args):
        pass

    open = forward = have = finish = first = total = bind


def nt(left, right):
    return lax.dot_general(left, right, (((1,), (1,)), ((), ())), preferred_element_type=F32)


def nn(left, right):
    return lax.dot_general(left, right, (((1,), (0,)), ((), ())), preferred_element_type=F32)


def tn(left, right):
    return lax.dot_general(left, right, (((0,), (0,)), ((), ())), preferred_element_type=F32)


def mean_square(values):
    return jnp.mean(values * values, axis=-1, keepdims=True)


def norm_rows(values, gain):
    return values * lax.rsqrt(mean_square(values) + EPS) * gain


def norm_back(values, gain, dn):
    r = lax.rsqrt(mean_square(values) + EPS)
    u = values * r
    dg = dn * gain
    rows = r * (dg - u * jnp.mean(dg * u, axis=-1, keepdims=True))
    return rows, jnp.sum(dn * u, axis=0, keepdims=True)


def gelu_parts(v):
    c = math.sqrt(2.0 / math.pi)
    t = jnp.tanh(c * (v + 0.044715 * v * v * v))
    value = 0.5 * v * (1.0 + t)
    slope = 0.5 * (1.0 + t) + 0.5 * v * (1.0 - t * t) * c * (1.0 + 3.0 * 0.044715 * v * v)
    return value, slope


def head_rows(values, h):
    lane = lax.broadcasted_iota(jnp.int32, values.shape, 1)
    return jnp.where(lane // DH == h, values, jnp.zeros_like(values))


def diagonal_sums(tile):
    rows, width = tile.shape
    while rows > 1:
        rows = rows // 2
        tile = tile[:rows] + pltpu.roll(tile[rows:], width - rows, 1)
    return tile


class Attention:
    def __init__(self, slots, shared, length, cols, causal):
        self.shared, self.cols, self.heads, self.causal = shared, cols, cols // DH, causal
        rows, turned = VM((length, cols), BF16), VM((4, cols, QB), BF16)
        slots.add(
            self, q=rows, k=rows, v=rows, ctx=rows, kt=turned, vt=turned,
            lse=VM((4, self.heads, 1, QB), F32), kcol=VM((length, 128), F32),
        )

    def bind(self, weights):
        self.w = weights

    def blk(self, b):
        return aligned(b * QB, QB)

    def wcols(self, first, count):
        return self.w[:, first * self.cols : (first + count) * self.cols]

    def mask(self, b, kb):
        sk = self.kcol[self.blk(kb), :]
        sk = jnp.concatenate([sk, sk], axis=1)
        return jnp.where(sk == self.shared.segq[b], 0.0, NEG)

    def score(self, k, q, madd, h, kind):
        s = nt(k, q) + madd
        if self.causal:
            s = s + self.shared.bias[kind, h]
        return s

    def kind(self, b, kb):
        return jnp.minimum(b - kb, 2) if self.causal else None

    def key_blocks(self, b):
        return b + 1 if self.causal else 4

    def project_kv(self, source):
        c = self.cols

        def one(b, carry):
            kv = nn(source[self.blk(b), :], self.wcols(1, 2))
            k, v = kv[:, :c], kv[:, c:]
            self.k[self.blk(b), :] = k.astype(BF16)
            self.v[self.blk(b), :] = v.astype(BF16)
            self.kt[b] = k.T.astype(BF16)
            self.vt[b] = v.T.astype(BF16)
            return carry

        lax.fori_loop(0, 4, one, 0)

    def project_q(self, source, b):
        self.q[self.blk(b), :] = nn(source[self.blk(b), :], self.wcols(0, 1)).astype(BF16)

    def out_part(self, dest, b):
        dest[self.blk(b), :] = nt(self.ctx[self.blk(b), :], self.wcols(3, 1)).astype(BF16)

    def rows_of(self, h):
        return slice(h * DH, (h + 1) * DH)

    def wide_of(self, h):
        return slice(h * QB, (h + 1) * QB)

    def forward(self, b):
        s_ = self.shared
        q = self.q[self.blk(b), :]
        for h in range(self.heads):
            s_.qm[self.wide_of(h), :] = head_rows(q, h)
        s_.peak[...] = jnp.full_like(s_.peak, NEG)
        s_.total[...] = jnp.zeros_like(s_.total)
        s_.oacc[...] = jnp.zeros_like(s_.oacc)

        def tile(kb, carry):
            madd = self.mask(b, kb)
            k = self.k[self.blk(kb), :]
            for h in range(self.heads):
                hs = self.rows_of(h)
                s = self.score(k, s_.qm[self.wide_of(h), :], madd, h, self.kind(b, kb))
                old = s_.peak[h]
                new = jnp.maximum(old, jnp.max(s, axis=0, keepdims=True))
                fade = jnp.exp(old - new)
                x = jnp.exp(s - new)
                s_.peak[h] = new
                s_.total[h] = s_.total[h] * fade + jnp.sum(x, axis=0, keepdims=True)
                s_.oacc[hs, :] = s_.oacc[hs, :] * fade + nn(self.vt[kb, hs, :], x.astype(BF16))
            return carry

        lax.fori_loop(0, self.key_blocks(b), tile, 0)
        for h in range(self.heads):
            hs = self.rows_of(h)
            s_.oacc[hs, :] = s_.oacc[hs, :] / s_.total[h]
            self.lse[b, h] = s_.peak[h] + jnp.log(s_.total[h])
        self.ctx[self.blk(b), :] = s_.oacc[...].T.astype(BF16)

    def backward(self, b, dctx):
        s_ = self.shared
        q = self.q[self.blk(b), :]
        prod = (dctx.astype(F32) * self.ctx[self.blk(b), :].astype(F32)).T
        for h in range(self.heads):
            s_.qm[self.wide_of(h), :] = head_rows(q, h)
            s_.dm[self.wide_of(h), :] = head_rows(dctx, h)
            s_.total[h] = jnp.sum(prod[self.rows_of(h), :], axis=0, keepdims=True)
        s_.oacc[...] = jnp.zeros_like(s_.oacc)

        def tile(kb, carry):
            madd = self.mask(b, kb)
            keys = self.blk(kb)
            k, v = self.k[keys, :], self.v[keys, :]
            kind = self.kind(b, kb)
            for h in range(self.heads):
                hs, wide = self.rows_of(h), self.wide_of(h)
                p = jnp.exp(self.score(k, s_.qm[wide, :], madd, h, kind) - self.lse[b, h])
                ds = p * (nt(v, s_.dm[wide, :]) - s_.total[h])
                if self.causal:
                    s_.gb[kind, h] += ds
                low = ds.astype(BF16)
                s_.pcat[:, wide] = p.astype(BF16)
                s_.dcat[:, wide] = low
                s_.oacc[hs, :] += nn(self.kt[kb, hs, :], low)
            s_.dva[keys, :] += nn(s_.pcat[...], s_.dm[...])
            s_.dka[keys, :] += nn(s_.dcat[...], s_.qm[...])
            return carry

        lax.fori_loop(0, self.key_blocks(b), tile, 0)
        return s_.oacc[...].T.astype(BF16)


def make_bias(s_, table, heads, ranges):
    lane = lax.broadcasted_iota(jnp.int32, (1, 2 * QB), 1)
    jj = lax.broadcasted_iota(jnp.int32, (QB, QB), 0)
    ii = lax.broadcasted_iota(jnp.int32, (QB, QB), 1)
    for h in range(heads):
        row = jnp.full((1, 2 * QB), table[h, NB - 1])
        for which, start, stop in reversed(ranges[:-1]):
            row = jnp.where(lane < stop, table[h, which], row)
        turned = pltpu.roll(jnp.broadcast_to(row, (QB, 2 * QB)), 0, 1, stride=1, stride_axis=0)
        s_.bias[0, h] = jnp.where(jj <= ii, turned[:, :QB], NEG)
        s_.bias[1, h] = turned[:, QB:]
        s_.bias[2, h] = jnp.full((QB, QB), table[h, NB - 1])
    s_.gb[...] = jnp.zeros_like(s_.gb)


def table_rows(s_, heads, ranges, n):
    near = [diagonal_sums(jnp.concatenate([s_.gb[0, h], s_.gb[1, h]], axis=1)) for h in range(heads)]
    near = jnp.concatenate(near + [jnp.zeros((8 - heads, 2 * QB), F32)], axis=0)
    lane = lax.broadcasted_iota(jnp.int32, (1, 128), 1)
    first = jnp.full((1, 128), 2 * QB, jnp.int32)
    after = jnp.zeros((1, 128), jnp.int32)
    for which, start, stop in ranges:
        first = jnp.where(lane == which, start, first)
        after = jnp.where(lane == which, stop, after)
    dist = lax.broadcasted_iota(jnp.int32, (2 * QB, 128), 0)
    pick = jnp.where(jnp.logical_and(dist >= first, dist < after), 1.0, 0.0)
    sums = lax.dot_general(
        near, pick, (((1,), (0,)), ((), ())), precision=lax.Precision.HIGHEST, preferred_element_type=F32
    )
    place = lax.broadcasted_iota(jnp.int32, (16, 128), 0)
    rows = jnp.zeros((16, 128), F32)
    for h in range(heads):
        far = jnp.sum(jnp.sum(s_.gb[2, h], axis=0, keepdims=True), axis=1, keepdims=True)
        line = sums[h : h + 1, :] + jnp.where(lane == NB - 1, far, 0.0)
        rows = jnp.where(place == n * heads + h, jnp.broadcast_to(line, (16, 128)), rows)
    return rows


def weight_grad(dest, column, left, right):
    width = right.shape[1]

    def one(m, carry):
        part = pl.ds(pl.multiple_of(m * 256, 256), 256)
        dest[part, column : column + width] = tn(left[:, part], right[...]).astype(BF16)
        return carry

    lax.fori_loop(0, left.shape[1] // 256, one, 0)


class Layer:
    def __init__(self, zy, sizes, ins, outs, slots):
        self.zy, self.sizes = zy, sizes
        rows, model, cols, hid, wrows, length = sizes
        heads = cols // DH
        self.heads = heads
        s_ = self.shared = SimpleNamespace()
        self.one = Attention(slots, s_, length, cols, True)
        self.two = Attention(slots, s_, length, cols, False)
        wide_rows, acc = VM((heads * QB, cols), BF16), VM((length, cols), F32)
        line, tiles, cat = VM((heads, 1, QB), F32), VM((3, heads, QB, QB), F32), VM((QB, heads * QB), BF16)
        slots.add(
            s_, segq=VM((4, 1, QB), F32), bias=tiles, gb=tiles, qm=wide_rows, dm=wide_rows, peak=line, total=line,
            oacc=VM((cols, QB), F32), pcat=cat, dcat=cat, dva=acc, dka=acc,
        )
        full, own, head_out = VM((length, model), BF16), VM((rows, model), F32), VM((length, cols), BF16)
        slots.add(
            self, full_self=full, full_mem=full, full_cross=full, full_ff=full, dy3=full, dy2=full, dy1=full,
            pa=full, pb=full, x_two=own, x_three=own, g=own, dq=head_out, dk=head_out, dv=head_out,
            hidden=VM((length, hid), BF16), dgu=VM((length, 2 * hid), BF16), small=VM((16, model), F32),
        )
        self.gathers = [RowGather(slots, rows) for _ in range(7)]
        self.g_self, self.g_mem, self.g_cross, self.g_ff, self.g_dy3, self.g_dy2, self.g_dy1 = self.gathers
        self.reduces = [RowReduce(slots, rows, model) for _ in range(7)]
        self.r_out1, self.r_out2, self.r_out3, self.r_dn3, self.r_dn2, self.r_mem, self.r_dn1 = self.reduces
        self.groups = [SimpleNamespace(width=w) for w in (4 * cols, 4 * cols, 3 * hid)]
        self.ws, self.wc, self.wf = self.groups
        for group in self.groups:
            if zy:
                both = VM((model, group.width), BF16)
                slots.add(group, w=both, gp=both)
                group.gather = WideGather(slots, wrows)
                group.reduce = WideReduce(slots, wrows, group.width, 384)
            else:
                outs.add(group, gp=((model, group.width), BF16))
                group.gather = group.reduce = Idle()
        if zy:
            self.ss = SmallSum(slots, 16, model)

    def blk(self, b):
        return aligned(b * QB, QB)

    def chunk(self, k, block=0):
        size = self.sizes[0] // ROW_CHUNKS
        return aligned(block * self.sizes[0] + k * size, size)

    def far_first(self, i):
        s = self.spot
        far = jnp.where(i < 2, 1 - s.x, s.x)
        return far * 2 + jnp.where(i % 2 == 0, 1 - s.c, s.c)

    def near_first(self, i):
        s = self.spot
        far = jnp.where(i < 2, s.x, 1 - s.x)
        return far * 2 + jnp.where(jnp.logical_or(i == 0, i == 3), s.c, 1 - s.c)

    def near_waits(self, i, gather):
        @pl.when(i == 1)
        def _():
            gather.have_sib()
            gather.forward(0, 1)

        @pl.when(i == 2)
        def _():
            gather.forward(1, ROW_CHUNKS)
            gather.have_xsib()

    def near_sends(self, i, reduce):
        @pl.when(i == 1)
        def _():
            reduce.send_own()

        @pl.when(i == 2)
        def _():
            reduce.send_far()

        @pl.when(i == 3)
        def _():
            reduce.cross()

    def at(self, i, *actions):
        for j, action in enumerate(actions):
            if action is not None:
                pl.when(i == j)(action)

    def pack(self, group, *shards):
        rows = self.sizes[4]
        parts = [ref[...].astype(F32) for ref in shards]
        parts = [p if p.shape[0] == rows else p.T for p in parts]
        group.w[aligned(self.spot.w * rows, rows), :] = jnp.concatenate(parts, axis=1).astype(BF16)

    def ff_block(self, b):
        f = self.sizes[3]
        step = f // 2
        w, blk = self.wf.w, self.blk(b)
        x, dy = self.full_ff[blk, :], self.dy3[blk, :]
        for j in range(0, f, step):
            gate = nn(x, w[:, j : j + step])
            up = nn(x, w[:, f + j : f + j + step])
            dh = nn(dy, w[:, 2 * f + j : 2 * f + j + step])
            value, slope = gelu_parts(gate)
            self.hidden[blk, j : j + step] = (value * up).astype(BF16)
            self.dgu[blk, j : j + step] = (dh * up * slope).astype(BF16)
            self.dgu[blk, f + j : f + j + step] = (dh * value).astype(BF16)
        self.pa[blk, :] = nt(self.dgu[blk, :], w[:, : 2 * f]).astype(BF16)

    def norm_backward(self, values, gain, reduce, base, done):
        gain_sum = jnp.zeros((1, self.sizes[1]), F32)
        for k in range(ROW_CHUNKS):
            rows = self.chunk(k)
            add, part = norm_back(values[rows, :].astype(F32), gain, reduce.total(k))
            gain_sum = gain_sum + part
            done(k, rows, base[rows, :].astype(F32) + add)
        return gain_sum

    def run(self):
        rows, model, cols, hid, wrows, length = self.sizes
        zy, heads, s_ = self.zy, self.heads, self.shared
        spot = self.spot = Spot(zy)
        one, two = self.one, self.two
        ws, wc, wf = self.groups
        greet(spot, zy)
        for gather, full in zip(
            self.gathers, (self.full_self, self.full_mem, self.full_cross, self.full_ff, self.dy3, self.dy2, self.dy1)
        ):
            gather.bind(spot, full)
        for reduce, part in zip(
            self.reduces, (self.pa, self.pb, self.pb, self.pa, self.pa, self.pb, self.pa)
        ):
            reduce.bind(spot, part)
        column = 0
        for group in self.groups:
            group.gather.bind(spot, group.w)
            group.reduce.bind(spot, group.gp, self.red if zy else None, column)
            column += group.width
        one.bind(ws.w)
        two.bind(wc.w)
        gain_s, gain_c, gain_f = (ref[...].reshape(1, model) for ref in (self.gain_s, self.gain_c, self.gain_f))

        if zy:
            self.pack(ws, self.sq, self.sk, self.sv, self.so)
        ws.gather.open()
        for k in range(ROW_CHUNKS):
            x = self.x[self.chunk(k), :].astype(F32)
            self.full_self[self.chunk(k, spot.n), :] = norm_rows(x, gain_s).astype(BF16)
            self.g_self.send(k)
        self.full_mem[self.blk(spot.n), :] = self.m[...]
        self.g_mem.send_all()
        if zy:
            self.pack(wc, self.cq, self.ck, self.cv, self.co)
            self.pack(wf, self.fg, self.fu, self.fd)
        ranges = bucket_ranges(2 * QB)
        for attention, ids in ((one, self.sid), (two, self.mid)):
            values = ids[...].astype(F32)
            attention.kcol[...] = jnp.broadcast_to(values, (128, length)).T
        for b in range(4):
            s_.segq[b] = self.sid[:, b * QB : (b + 1) * QB].astype(F32)
        make_bias(s_, self.table, heads, ranges)
        ws.gather.forward(1)
        self.g_self.forward(0, 2)
        ws.gather.forward(2)
        self.g_self.forward(2, 4)
        ws.gather.forward(3)
        wc.gather.open()
        self.g_self.have_sib()
        self.g_self.have_xsib()
        ws.gather.have()

        one.project_kv(self.full_self)

        def self_block(i, carry):
            b = self.far_first(i)
            one.project_q(self.full_self, b)
            one.forward(b)
            one.out_part(self.pa, b)

            def after_first():
                self.r_out1.send_far()
                wc.gather.forward(1)

            def after_second():
                self.r_out1.cross()
                self.g_mem.forward(0, 4)

            def after_third():
                self.r_out1.send_own()
                wc.gather.forward(2)

            self.at(i, after_first, after_second, after_third)
            return carry

        lax.fori_loop(0, 4, self_block, 0)
        wc.gather.forward(3)
        wf.gather.open()
        self.g_mem.have_sib()
        self.g_mem.have_xsib()
        wc.gather.have()
        two.project_kv(self.full_mem)
        wf.gather.forward(1)
        for k in range(ROW_CHUNKS):
            value = self.x[self.chunk(k), :].astype(F32) + self.r_out1.total(k)
            self.x_two[self.chunk(k), :] = value
            self.full_cross[self.chunk(k, spot.n), :] = norm_rows(value, gain_c).astype(BF16)
            self.g_cross.send(k)
        self.dy3[self.blk(spot.n), :] = self.cot[...]
        self.g_dy3.send_all()

        def cross_block(i, carry):
            b = self.near_first(i)
            self.near_waits(i, self.g_cross)
            two.project_q(self.full_cross, b)
            two.forward(b)
            two.out_part(self.pb, b)
            self.near_sends(i, self.r_out2)
            self.at(i, None, lambda: wf.gather.forward(2), None, lambda: wf.gather.forward(3))
            return carry

        lax.fori_loop(0, 4, cross_block, 0)
        self.g_dy3.forward(0, 4)
        for k in range(ROW_CHUNKS):
            value = self.x_two[self.chunk(k), :] + self.r_out2.total(k)
            self.x_three[self.chunk(k), :] = value
            self.full_ff[self.chunk(k, spot.n), :] = norm_rows(value, gain_f).astype(BF16)
            self.g_ff.send(k)
        self.r_out1.finish()
        self.r_out2.finish()
        self.g_dy3.have_sib()
        self.g_dy3.have_xsib()
        wf.gather.have()

        def ff_step(i, carry):
            b = self.near_first(i)
            self.near_waits(i, self.g_ff)
            self.ff_block(b)
            self.near_sends(i, self.r_dn3)
            return carry

        lax.fori_loop(0, 4, ff_step, 0)
        weight_grad(wf.gp, 0, self.full_ff, self.dgu)
        split = wf.reduce.chunks * 2 // 3
        for c in range(split):
            wf.reduce.open(c)

        def ff_out(b, carry):
            self.pb[self.blk(b), :] = nt(self.hidden[self.blk(b), :], wf.w[:, 2 * hid :]).astype(BF16)
            return carry

        lax.fori_loop(0, 4, ff_out, 0)
        self.r_out3.send_far()
        self.r_out3.send_own()
        weight_grad(wf.gp, 2 * hid, self.dy3, self.hidden)
        for c in range(split, wf.reduce.chunks):
            wf.reduce.open(c)

        def back_three(k, at, value):
            self.g[at, :] = value
            self.dy2[self.chunk(k, spot.n), :] = value.astype(BF16)
            self.g_dy2.send(k)

        gain_ff = self.norm_backward(self.x_three, gain_f, self.r_dn3, self.cot, back_three)
        self.small[14:15, :] = gain_ff
        self.r_out3.cross()

        self.r_dn3.finish()
        s_.dka[...] = jnp.zeros_like(s_.dka)
        s_.dva[...] = jnp.zeros_like(s_.dva)

        def cross_back(i, carry):
            b = self.near_first(i)
            blk = self.blk(b)
            self.near_waits(i, self.g_dy2)
            dctx = nn(self.dy2[blk, :], two.wcols(3, 1)).astype(BF16)
            dq = two.backward(b, dctx)
            self.dq[blk, :] = dq
            self.pa[blk, :] = nt(dq, two.wcols(0, 1)).astype(BF16)
            self.near_sends(i, self.r_dn2)
            if zy:
                self.at(i, lambda: wf.reduce.first(0), lambda: wf.reduce.first(1), None, lambda: wf.reduce.first(2))
            return carry

        lax.fori_loop(0, 4, cross_back, 0)
        for k in range(ROW_CHUNKS):
            value = self.x_three[self.chunk(k), :] + self.r_out3.total(k)
            self.result[self.chunk(k), :] = value.astype(BF16)
        self.r_out3.finish()
        self.dk[...] = s_.dka[...].astype(BF16)
        self.dv[...] = s_.dva[...].astype(BF16)

        def memory_part(b, carry):
            blk = self.blk(b)
            self.pb[blk, :] = (nt(self.dk[blk, :], two.wcols(1, 1)) + nt(self.dv[blk, :], two.wcols(2, 1))).astype(BF16)
            return carry

        lax.fori_loop(0, 4, memory_part, 0)
        self.r_mem.send_far()
        self.r_mem.send_own()
        if zy:
            wf.reduce.first(3)

        def back_two(k, at, value):
            self.g[at, :] = value
            self.dy1[self.chunk(k, spot.n), :] = value.astype(BF16)
            self.g_dy1.send(k)

        gain_cross = self.norm_backward(self.x_two, gain_c, self.r_dn2, self.g, back_two)
        self.small[13:14, :] = gain_cross
        self.r_mem.cross()
        weight_grad(wc.gp, 0, self.full_cross, self.dq)
        weight_grad(wc.gp, cols, self.full_mem, self.dk)
        wc.reduce.open(0)
        weight_grad(wc.gp, 2 * cols, self.full_mem, self.dv)
        weight_grad(wc.gp, 3 * cols, self.dy2, two.ctx)
        wc.reduce.open(1)

        s_.dka[...] = jnp.zeros_like(s_.dka)
        s_.dva[...] = jnp.zeros_like(s_.dva)

        def self_back(i, carry):
            b = self.near_first(i)
            blk = self.blk(b)
            self.near_waits(i, self.g_dy1)
            dctx = nn(self.dy1[blk, :], one.wcols(3, 1)).astype(BF16)
            self.dq[blk, :] = one.backward(b, dctx)

            def ff_totals():
                for c in range(wf.reduce.chunks):
                    wf.reduce.total(c)

            self.at(i, lambda: wc.reduce.first(0), ff_totals, lambda: wc.reduce.first(1))
            return carry

        lax.fori_loop(0, 4, self_back, 0)
        self.dk[...] = s_.dka[...].astype(BF16)
        self.dv[...] = s_.dva[...].astype(BF16)
        self.r_dn2.finish()

        def last_part(i, carry):
            blk = self.blk(self.far_first(i))
            self.pa[blk, :] = (
                nt(self.dq[blk, :], one.wcols(0, 1))
                + nt(self.dk[blk, :], one.wcols(1, 1))
                + nt(self.dv[blk, :], one.wcols(2, 1))
            ).astype(BF16)
            self.at(i, self.r_dn1.send_far, self.r_dn1.cross, self.r_dn1.send_own)
            return carry

        lax.fori_loop(0, 4, last_part, 0)
        weight_grad(ws.gp, 0, self.full_self, self.dq)
        weight_grad(ws.gp, cols, self.full_self, self.dk)
        ws.reduce.open(0)
        weight_grad(ws.gp, 2 * cols, self.full_self, self.dv)
        weight_grad(ws.gp, 3 * cols, self.dy1, one.ctx)
        ws.reduce.open(1)

        keep = self.small[13:15, :]
        self.small[...] = jnp.zeros_like(self.small)
        self.small[:, 0:128] = table_rows(s_, heads, ranges, spot.n)
        self.small[13:15, :] = keep
        wc.reduce.total(0)
        wc.reduce.total(1)
        ws.reduce.first(0)

        def back_one(k, at, value):
            self.gx[at, :] = value.astype(BF16)

        gain_self = self.norm_backward(self.x, gain_s, self.r_dn1, self.g, back_one)
        self.small[12:13, :] = gain_self
        ws.reduce.first(1)
        if zy:
            self.ss.run(spot, self.small[...], self.tot)
        else:
            self.tot[...] = self.small[...]
        for k in range(ROW_CHUNKS):
            self.gm[self.chunk(k), :] = self.r_mem.total(k).astype(BF16)
        ws.reduce.total(0)
        ws.reduce.total(1)

        for gather in self.gathers:
            gather.finish()
        self.r_mem.finish()
        self.r_dn1.finish()
        for group in self.groups:
            group.gather.finish()
            group.reduce.finish()


def deliver(red, tot, passed, sizes, heads):
    rows, model, cols, hid, wrows, length = sizes
    ins, outs = Slots(), Slots()
    packed, small = SimpleNamespace(), SimpleNamespace()
    ins.add(packed, ref=(red, VM))
    ins.add(small, ref=(tot, VM))
    sources, dests = [SimpleNamespace() for _ in passed], [SimpleNamespace() for _ in passed]
    for value, source, dest in zip(passed, sources, dests):
        ins.add(source, ref=(value, VM))
        outs.add(dest, ref=(value.shape, value.dtype))
    cuts, at = [], 0
    for width, turn in [(cols, False)] * 3 + [(cols, True)] + [(cols, False)] * 3 + [(cols, True)] + [(hid, False)] * 3:
        cut = SimpleNamespace(at=at, width=width, turn=turn)
        outs.add(cut, ref=((width, wrows) if turn else (wrows, width), F32))
        cuts.append(cut)
        at += width
    gains, table = [SimpleNamespace() for _ in range(3)], SimpleNamespace()
    for gain in gains:
        outs.add(gain, ref=((model,), F32))
    outs.add(table, ref=((4 * heads, NB), F32))

    def body():
        for source, dest in zip(sources, dests):
            dest.ref[...] = source.ref[...]
        for cut in cuts:
            part = packed.ref[:, cut.at : cut.at + cut.width]
            cut.ref[...] = part.T if cut.turn else part
        for i, gain in enumerate(gains):
            gain.ref[...] = small.ref[12 + i : 13 + i, :].reshape(model)
        table.ref[...] = small.ref[0 : 4 * heads, 0:NB]

    got = run_kernel(body, ins, outs, Slots(), None, "deliver")
    return got[:3], got[3:14], got[14:17], got[17]


def shards(
    zy, inputs, memory, segment_ids, memory_ids, self_gain, self_query, self_key, self_value, self_out, bias_table,
    cross_gain, cross_query, cross_key, cross_value, cross_out, ff_gain, ff_gate, ff_up, ff_down, cotangent,
):
    rows, model = inputs.shape
    length = segment_ids.shape[1]
    wrows, cols = self_query.shape
    hid = ff_gate.shape[1]
    heads = cols // DH
    assert segment_ids.shape[0] == 1 and rows == QB and length == 4 * QB == memory_ids.shape[1]
    sizes = (rows, model, cols, hid, wrows, length)
    ins, outs, slots = Slots(), Slots(), Slots()
    layer = Layer.__new__(Layer)
    outs.add(
        layer, result=((rows, model), BF16), gx=((rows, model), BF16), gm=((rows, model), BF16), tot=((16, model), F32)
    )
    if zy:
        outs.add(layer, red=((wrows, 8 * cols + 3 * hid), F32))
    layer.__init__(zy, sizes, ins, outs, slots)
    ins.add(
        layer, x=(inputs, VM), m=(memory, VM), cot=(cotangent, VM), sid=(segment_ids, VM), mid=(memory_ids, VM),
        gain_s=(self_gain, VM), gain_c=(cross_gain, VM), gain_f=(ff_gain, VM), table=(bias_table.T, pltpu.SMEM),
    )
    if zy:
        ins.add(
            layer, sq=(self_query, VM), sk=(self_key, VM), sv=(self_value, VM), so=(self_out, VM),
            cq=(cross_query, VM), ck=(cross_key, VM), cv=(cross_value, VM), co=(cross_out, VM),
            fg=(ff_gate, VM), fu=(ff_up, VM), fd=(ff_down.T, VM),
        )
    else:

        def whole(*parts):
            return lax.all_gather(jnp.concatenate(parts, axis=1), WIDE, axis=0, tiled=True)

        ins.add(layer.ws, w=(whole(self_query, self_key, self_value, self_out.T), VM))
        ins.add(layer.wc, w=(whole(cross_query, cross_key, cross_value, cross_out.T), VM))
        ins.add(layer.wf, w=(whole(ff_gate, ff_up, ff_down.T), VM))
    got = run_kernel(layer.run, ins, outs, slots, 0, "layer")
    if zy:
        total, red = got[3], got[4]
    else:
        packed = jnp.concatenate(got[4:7], axis=1)
        red = lax.psum_scatter(packed, WIDE, scatter_dimension=0, tiled=True).astype(F32)
        total = lax.psum(got[3], (WIDE, NARROW))
    row_outs, grads, gains, table = deliver(red, total, got[:3], sizes, heads)
    return (
        *row_outs,
        gains[0],
        *grads[0:4],
        table.T,
        gains[1],
        *grads[4:8],
        gains[2],
        grads[8],
        grads[9],
        grads[10].T,
    )


def solution(mesh):
    zy = mesh.shape[WIDE] == 8
    rows = P((WIDE, NARROW), None)
    w_in, w_out = P(WIDE, NARROW), P(NARROW, WIDE)
    placed = (
        rows, rows, P(WIDE, None), P(WIDE, None), P(),
        w_in, w_in, w_in, w_out, P(None, NARROW), P(),
        w_in, w_in, w_in, w_out, P(), w_in, w_in, w_out, rows,
    )
    outs = (
        rows, rows, rows, P(), w_in, w_in, w_in, w_out, P(), P(),
        w_in, w_in, w_in, w_out, P(), w_in, w_in, w_out,
    )

    def program(*args):
        return shards(zy, *args)

    return jax.shard_map(program, mesh=mesh, in_specs=placed, out_specs=outs, check_vma=False)
```

```python
import math
from types import SimpleNamespace

import jax
import jax.numpy as jnp
import numpy as np
from jax import lax
from jax.experimental import pallas as pl
from jax.experimental.pallas import tpu as pltpu
from jax.sharding import PartitionSpec as P

DH = 64
NB = 32
MAX_DIST = 128
EPS = 1e-06
NEG = -1e30
QB = 256
HALF = 128
ROW_CHUNKS = 4
WIDE = "wide"
NARROW = "narrow"
MESH = pl.DeviceIdType.MESH
F32 = jnp.float32
BF16 = jnp.bfloat16
VM = pltpu.VMEM
DMA = pltpu.SemaphoreType.DMA


def bucket_table(length, buckets, reach):
    exact_part = buckets // 2
    distance = np.arange(length)
    spread = (
        np.log(np.maximum(distance, exact_part) / exact_part)
        / np.log(reach / exact_part)
        * (buckets - exact_part)
    )
    far_bucket = np.minimum(exact_part + np.floor(spread).astype(np.int64), buckets - 1)
    return np.where(distance < exact_part, distance, far_bucket).astype(np.int32)


def bucket_ranges(length):
    table = bucket_table(length, NB, MAX_DIST)
    found = []
    for which in range(NB):
        places = np.nonzero(table == which)[0]
        if len(places):
            found.append((which, int(places[0]), int(places[-1]) + 1))
    return found


class Slots:
    def __init__(self):
        self.items = []

    def add(self, holder, **specs):
        for name, spec in specs.items():
            self.items.append((holder, name, spec))

    def fill(self, refs):
        for (holder, name, _), ref in zip(self.items, refs):
            setattr(holder, name, ref)


def run_kernel(body, ins, outs, scratch, cid, name):
    counts = len(ins.items), len(outs.items)

    def kernel(*refs):
        ins.fill(refs[: counts[0]])
        outs.fill(refs[counts[0] : counts[0] + counts[1]])
        scratch.fill(refs[counts[0] + counts[1] :])
        body()

    params = {} if cid is None else dict(collective_id=cid, has_side_effects=True)
    return pl.pallas_call(
        kernel,
        out_shape=[jax.ShapeDtypeStruct(*spec) for _, _, spec in outs.items],
        in_specs=[pl.BlockSpec(memory_space=spec[1]) for _, _, spec in ins.items],
        out_specs=[pl.BlockSpec(memory_space=VM) for _ in outs.items],
        scratch_shapes=[spec for _, _, spec in scratch.items],
        compiler_params=pltpu.CompilerParams(vmem_limit_bytes=66_900_000, **params),
        name=name,
    )(*[spec[0] for _, _, spec in ins.items])


class Spot:
    def __init__(self, wide_split):
        n = lax.axis_index(NARROW)
        self.n = n
        self.x = n // 2
        self.c = n % 2
        self.sib = self.x * 2 + (1 - self.c)
        self.xp = (1 - self.x) * 2 + self.c
        self.xsib = (1 - self.x) * 2 + (1 - self.c)
        if wide_split:
            w = lax.axis_index(WIDE)
            self.w = w
            self.z = w // 2
            self.y = w % 2
            self.yp = self.z * 2 + (1 - self.y)

    def at_n(self, n):
        return {NARROW: n}

    def at_w(self, w):
        return {WIDE: w}

    def at_z(self, z):
        return {WIDE: z * 2 + self.y}


def remote(src, dst, send, recv, dev):
    return pltpu.make_async_remote_copy(
        src_ref=src, dst_ref=dst, send_sem=send, recv_sem=recv, device_id=dev, device_id_type=MESH
    )


def greet(spot, zy):
    barrier = pltpu.get_barrier_semaphore()

    def hello(dev):
        pl.semaphore_signal(barrier, inc=1, device_id=dev, device_id_type=MESH)

    hello(spot.at_n(spot.sib))
    hello(spot.at_n(spot.xp))
    if zy:
        hello(spot.at_w(spot.yp))
        for step in range(1, 4):
            hello(spot.at_z((spot.z + step) % 4))
    pl.semaphore_wait(barrier, 6 if zy else 2)


def aligned(start, size):
    return pl.ds(pl.multiple_of(start, 16), size)


class RowGather:
    def __init__(self, slots, rows, chunks=ROW_CHUNKS):
        self.nrows, self.chunks, self.size = rows, chunks, rows // chunks
        sems = DMA((chunks,))
        slots.add(self, xs=sems, xr=sems, ss=sems, sr=sems, fs=sems, fr=sems)

    def bind(self, spot, full):
        self.spot, self.full = spot, full

    def hop(self, k, block, dev, send, recv):
        rows = self.full.at[aligned(block * self.nrows + k * self.size, self.size)]
        return remote(rows, rows, send.at[k], recv.at[k], self.spot.at_n(dev))

    def to_x(self, k):
        return self.hop(k, self.spot.n, self.spot.xp, self.xs, self.xr)

    def from_x(self, k):
        return self.hop(k, self.spot.xp, self.spot.xp, self.xs, self.xr)

    def to_sib(self, k):
        return self.hop(k, self.spot.n, self.spot.sib, self.ss, self.sr)

    def from_sib(self, k):
        return self.hop(k, self.spot.sib, self.spot.sib, self.ss, self.sr)

    def onward(self, k):
        return self.hop(k, self.spot.xp, self.spot.sib, self.fs, self.fr)

    def from_onward(self, k):
        return self.hop(k, self.spot.xsib, self.spot.sib, self.fs, self.fr)

    def send(self, k):
        self.to_x(k).start()
        self.to_sib(k).start()

    def send_all(self, first=0, after=ROW_CHUNKS):
        for k in range(first, after):
            self.send(k)

    def forward(self, first, after):
        for k in range(first, after):
            self.from_x(k).wait_recv()
            self.onward(k).start()

    def have_sib(self):
        for k in range(self.chunks):
            self.from_sib(k).wait_recv()

    def have_xsib(self, first, after):
        for k in range(first, after):
            self.from_onward(k).wait_recv()

    def finish(self):
        for k in range(self.chunks):
            self.to_x(k).wait_send()
            self.to_sib(k).wait_send()
            self.onward(k).wait_send()


class RowReduce:
    def __init__(self, slots, rows, cols, chunks=ROW_CHUNKS):
        self.nrows, self.ncols, self.chunks, self.size = rows, cols, chunks, rows // chunks
        sems, buf = DMA((chunks,)), VM((rows, cols), BF16)
        slots.add(self, as_=sems, ar=sems, bs=sems, br=sems, xs=sems, xr=sems, far=buf, own=buf, inn=buf)

    def bind(self, spot, part):
        self.spot, self.part = spot, part

    def buf(self, ref, k):
        return ref.at[pl.ds(k * self.size, self.size)]

    def mine(self, block, k):
        return self.part.at[aligned(block * self.nrows + k * self.size, self.size), pl.ds(0, self.ncols)]

    def far_sib(self, k):
        s = self.spot
        return remote(self.mine(s.xsib, k), self.buf(self.far, k), self.as_.at[k], self.ar.at[k], s.at_n(s.sib))

    def own_sib(self, k):
        s = self.spot
        return remote(self.mine(s.sib, k), self.buf(self.own, k), self.bs.at[k], self.br.at[k], s.at_n(s.sib))

    def across(self, k):
        s = self.spot
        return remote(self.buf(self.far, k), self.buf(self.inn, k), self.xs.at[k], self.xr.at[k], s.at_n(s.xp))

    def send_far(self, first=0, after=ROW_CHUNKS):
        for k in range(first, after):
            self.far_sib(k).start()

    def send_own(self):
        for k in range(self.chunks):
            self.own_sib(k).start()

    def cross(self, first=0, after=ROW_CHUNKS):
        for k in range(first, after):
            self.far_sib(k).wait_recv()
            here = self.buf(self.far, k)
            here[...] = (self.mine(self.spot.xp, k)[...].astype(F32) + here[...].astype(F32)).astype(BF16)
            self.across(k).start()

    def total(self, k):
        self.own_sib(k).wait_recv()
        self.across(k).wait_recv()
        value = self.mine(self.spot.n, k)[...].astype(F32) + self.buf(self.own, k)[...].astype(F32)
        return value + self.buf(self.inn, k)[...].astype(F32)

    def finish(self):
        for k in range(self.chunks):
            self.far_sib(k).wait_send()
            self.own_sib(k).wait_send()
            self.across(k).wait_send()


class WideGather:
    steps = (1, -1, 2, -2, 3, -3)

    def __init__(self, slots, rows, widths):
        self.nrows, self.widths, self.parts = rows, widths, range(len(widths))
        four = DMA((4, len(widths)))
        slots.add(self, zs=DMA((6, len(widths))), zr=four, ys=four, yr=four)

    def bind(self, spot, full):
        self.spot, self.full = spot, full

    def rows(self, z, y, part):
        cols = pl.ds(sum(self.widths[:part]), self.widths[part])
        return self.full.at[aligned((z * 2 + y) * self.nrows, self.nrows), cols]

    def along(self, i, part):
        s = self.spot
        rows = self.rows(s.z, s.y, part)
        return remote(rows, rows, self.zs.at[i, part], self.zr.at[s.z, part], s.at_z(s.z + self.steps[i]))

    def came(self, z, part):
        s = self.spot
        rows = self.rows(z, s.y, part)
        return remote(rows, rows, self.zs.at[0, part], self.zr.at[z, part], s.at_z(z))

    def over(self, z, part):
        s = self.spot
        rows = self.rows(z, s.y, part)
        return remote(rows, rows, self.ys.at[z, part], self.yr.at[z, part], s.at_w(s.yp))

    def crossed(self, z, part):
        s = self.spot
        rows = self.rows(z, 1 - s.y, part)
        return remote(rows, rows, self.ys.at[z, part], self.yr.at[z, part], s.at_w(s.yp))

    def when_inside(self, step, fn):
        there = self.spot.z + step

        @pl.when(there >= 0 if step < 0 else there <= 3)
        def _():
            fn(there)

    def open_y(self):
        for part in self.parts:
            self.over(self.spot.z, part).start()

    def open_z(self):
        for part in self.parts:
            for i, step in enumerate(self.steps):
                self.when_inside(step, lambda there: self.along(i, part).start())

    def forward(self, distance, *parts):
        for part in parts or self.parts:
            for step in (distance, -distance):

                def pass_on(there):
                    self.came(there, part).wait_recv()
                    self.over(there, part).start()

                self.when_inside(step, pass_on)

    def have(self, *parts):
        for part in parts or self.parts:
            for z in range(4):
                self.crossed(z, part).wait_recv()

    def finish(self):
        for part in self.parts:
            for z in range(4):
                self.over(z, part).wait_send()
            for i, step in enumerate(self.steps):
                self.when_inside(step, lambda there: self.along(i, part).wait_send())


class WideReduce:
    steps = (2, 3, 1, 0)

    def __init__(self, slots, rows, cols, width):
        self.nrows, self.width, self.chunks = rows, width, cols // width
        sems, buf = DMA((self.chunks, 4)), VM((4, rows, cols), BF16)
        slots.add(self, ys=sems, yr=sems, zs=sems, zr=sems, acc=buf, inn=buf)

    def bind(self, spot, part, out, out_col):
        self.spot, self.part, self.out, self.out_col = spot, part, out, out_col

    def cols(self, c):
        return pl.ds(c * self.width, self.width)

    def slab(self, c, z, y):
        return self.part.at[aligned((z * 2 + y) * self.nrows, self.nrows), self.cols(c)]

    def over(self, c, z):
        s = self.spot
        return remote(
            self.slab(c, z, 1 - s.y), self.acc.at[z, :, self.cols(c)], self.ys.at[c, z], self.yr.at[c, z], s.at_w(s.yp)
        )

    def along(self, c, z):
        s = self.spot
        return remote(
            self.acc.at[z, :, self.cols(c)], self.inn.at[s.z, :, self.cols(c)],
            self.zs.at[c, z], self.zr.at[c, s.z], s.at_z(z),
        )

    def came(self, c, z):
        here = self.inn.at[z, :, self.cols(c)]
        return remote(here, here, self.zs.at[c, z], self.zr.at[c, z], self.spot.at_z(z))

    def targets(self):
        return [(self.spot.z + step) % 4 for step in self.steps]

    def open(self, c):
        for z in self.targets():
            self.over(c, z).start()

    def first(self, c):
        for step, z in zip(self.steps, self.targets()):
            self.over(c, z).wait_recv()
            here = self.acc.at[z, :, self.cols(c)]
            here[...] = (self.slab(c, z, self.spot.y)[...].astype(F32) + here[...].astype(F32)).astype(BF16)
            if step:
                self.along(c, z).start()

    def total(self, c):
        value = self.acc[self.spot.z, :, self.cols(c)].astype(F32)
        for z in self.targets()[:3]:
            self.came(c, z).wait_recv()
            value = value + self.inn[z, :, self.cols(c)].astype(F32)
        self.out[:, pl.ds(self.out_col + c * self.width, self.width)] = value

    def finish(self):
        for c in range(self.chunks):
            for step, z in zip(self.steps, self.targets()):
                self.over(c, z).wait_send()
                if step:
                    self.along(c, z).wait_send()


class SmallSum:
    def __init__(self, slots, rows, cols):
        four = VM((4, rows, cols), F32)
        slots.add(
            self, ps=DMA((3,)), pr=DMA((3,)), zs=DMA((4,)), zr=DMA((4,)), held=four, inn=VM((3, rows, cols), F32), zin=four
        )

    def bind(self, spot):
        self.spot = spot

    def pair(self, i):
        s = self.spot
        dev = (s.at_n(s.sib), s.at_n(s.xp), s.at_w(s.yp))[i]
        return remote(self.held.at[i], self.inn.at[i], self.ps.at[i], self.pr.at[i], dev)

    def hop(self, step, landed):
        other = (self.spot.z + step) % 4
        return remote(
            self.held.at[3], self.zin.at[landed], self.zs.at[step], self.zr.at[landed], self.spot.at_z(other)
        )

    def begin(self, value):
        self.held[0] = value
        self.pair(0).start()

    def step(self, i):
        self.pair(i).wait_recv()
        self.held[i + 1] = self.held[i] + self.inn[i]
        if i < 2:
            self.pair(i + 1).start()
        else:
            self.zin[self.spot.z] = self.held[3]
            for step in range(1, 4):
                self.hop(step, self.spot.z).start()

    def end(self, out):
        for step in range(1, 4):
            self.hop(step, (self.spot.z + step) % 4).wait_recv()
        out[...] = ((self.zin[0] + self.zin[1]) + self.zin[2]) + self.zin[3]
        for i in range(3):
            self.pair(i).wait_send()
        for step in range(1, 4):
            self.hop(step, self.spot.z).wait_send()


class Idle:
    chunks = 0

    def bind(self, *args):
        pass

    open = open_y = open_z = forward = have = finish = first = total = bind


def nt(left, right):
    return lax.dot_general(left, right, (((1,), (1,)), ((), ())), preferred_element_type=F32)


def nn(left, right):
    return lax.dot_general(left, right, (((1,), (0,)), ((), ())), preferred_element_type=F32)


def tn(left, right):
    return lax.dot_general(left, right, (((0,), (0,)), ((), ())), preferred_element_type=F32)


def mean_square(values):
    return jnp.mean(values * values, axis=-1, keepdims=True)


def norm_rows(values, gain):
    return values * lax.rsqrt(mean_square(values) + EPS) * gain


def norm_back(values, gain, dn):
    r = lax.rsqrt(mean_square(values) + EPS)
    u = values * r
    dg = dn * gain
    rows = r * (dg - u * jnp.mean(dg * u, axis=-1, keepdims=True))
    return rows, jnp.sum(dn * u, axis=0, keepdims=True)


def gelu_parts(v):
    c = math.sqrt(2.0 / math.pi)
    t = jnp.tanh(c * (v + 0.044715 * v * v * v))
    value = 0.5 * v * (1.0 + t)
    slope = 0.5 * (1.0 + t) + 0.5 * v * (1.0 - t * t) * c * (1.0 + 3.0 * 0.044715 * v * v)
    return value, slope


def head_rows(values, h):
    lane = lax.broadcasted_iota(jnp.int32, values.shape, 1)
    return jnp.where(lane // DH == h, values, jnp.zeros_like(values))


def diagonal_sums(tile):
    rows, width = tile.shape
    while rows > 1:
        rows = rows // 2
        tile = tile[:rows] + pltpu.roll(tile[rows:], width - rows, 1)
    return tile


class Tile:
    def __init__(self, slot, first, second):
        self.slot, self.halves = slot, (first, second)

    def rows(self, half):
        return aligned(half * HALF, HALF)

    def load(self, ref):
        return jnp.concatenate([ref[self.rows(h), :] for h in self.halves], axis=0)

    def store(self, ref, value, at=0):
        for i, h in enumerate(self.halves):
            ref[self.rows(h), at : at + value.shape[1]] = value[i * HALF : (i + 1) * HALF]


class Attention:
    def __init__(self, slots, shared, length, cols, causal):
        self.shared, self.cols, self.heads, self.causal = shared, cols, cols // DH, causal
        rows, turned = VM((length, cols), BF16), VM((4, cols, QB), BF16)
        slots.add(
            self, q=rows, k=rows, v=rows, ctx=rows, kt=turned, vt=turned,
            lse=VM((4, self.heads, 1, QB), F32), kcol=VM((length, 128), F32),
        )

    def bind(self, weights):
        self.w = weights

    def blk(self, b):
        return aligned(b * QB, QB)

    def wcols(self, first, count):
        return self.w[:, first * self.cols : (first + count) * self.cols]

    def mask(self, t, kb):
        sk = self.kcol[self.blk(kb), :]
        sk = jnp.concatenate([sk, sk], axis=1)
        sq = jnp.concatenate([self.shared.segq[h] for h in t.halves], axis=1)
        return jnp.where(sk == sq, 0.0, NEG)

    def score(self, k, q, madd, h, kind):
        s = nt(k, q) + madd
        if self.causal:
            s = s + self.shared.bias[kind, h]
        return s

    def kind(self, t, kb):
        return jnp.minimum(t.slot - kb, 2) if self.causal else None

    def key_blocks(self, t):
        return (jnp.maximum(t.slot - 2, 0), t.slot + 1) if self.causal else (0, 4)

    def project_kv(self, source):
        c = self.cols

        def one(b, carry):
            kv = nn(source[self.blk(b), :], self.wcols(0, 2))
            k, v = kv[:, :c], kv[:, c:]
            self.k[self.blk(b), :] = k.astype(BF16)
            self.v[self.blk(b), :] = v.astype(BF16)
            self.kt[b] = k.T.astype(BF16)
            self.vt[b] = v.T.astype(BF16)
            return carry

        lax.fori_loop(0, 4, one, 0)

    def project_q(self, source, t):
        t.store(self.q, nn(t.load(source), self.wcols(2, 1)).astype(BF16))

    def out_part(self, dest, t):
        t.store(dest, nt(t.load(self.ctx), self.wcols(3, 1)).astype(BF16))

    def rows_of(self, h):
        return slice(h * DH, (h + 1) * DH)

    def wide_of(self, h):
        return slice(h * QB, (h + 1) * QB)

    def forward(self, t):
        s_ = self.shared
        q = t.load(self.q)
        for h in range(self.heads):
            s_.qm[self.wide_of(h), :] = head_rows(q, h)
        s_.peak[...] = jnp.full_like(s_.peak, NEG)
        s_.total[...] = jnp.zeros_like(s_.total)
        s_.oacc[...] = jnp.zeros_like(s_.oacc)

        def tile(kb, carry):
            madd = self.mask(t, kb)
            k = self.k[self.blk(kb), :]
            for h in range(self.heads):
                hs = self.rows_of(h)
                s = self.score(k, s_.qm[self.wide_of(h), :], madd, h, self.kind(t, kb))
                old = s_.peak[h]
                new = jnp.maximum(old, jnp.max(s, axis=0, keepdims=True))
                fade = jnp.exp(old - new)
                x = jnp.exp(s - new)
                s_.peak[h] = new
                s_.total[h] = s_.total[h] * fade + jnp.sum(x, axis=0, keepdims=True)
                s_.oacc[hs, :] = s_.oacc[hs, :] * fade + nn(self.vt[kb, hs, :], x.astype(BF16))
            return carry

        lax.fori_loop(*self.key_blocks(t), tile, 0)
        for h in range(self.heads):
            hs = self.rows_of(h)
            s_.oacc[hs, :] = s_.oacc[hs, :] / s_.total[h]
            self.lse[t.slot, h] = s_.peak[h] + jnp.log(s_.total[h])
        t.store(self.ctx, s_.oacc[...].T.astype(BF16))

    def backward(self, t, dctx):
        s_ = self.shared
        q = t.load(self.q)
        prod = (dctx.astype(F32) * t.load(self.ctx).astype(F32)).T
        for h in range(self.heads):
            s_.qm[self.wide_of(h), :] = head_rows(q, h)
            s_.dm[self.wide_of(h), :] = head_rows(dctx, h)
            s_.total[h] = jnp.sum(prod[self.rows_of(h), :], axis=0, keepdims=True)
        s_.oacc[...] = jnp.zeros_like(s_.oacc)

        def tile(kb, carry):
            madd = self.mask(t, kb)
            keys = self.blk(kb)
            k, v = self.k[keys, :], self.v[keys, :]
            kind = self.kind(t, kb)
            for h in range(self.heads):
                hs, wide = self.rows_of(h), self.wide_of(h)
                p = jnp.exp(self.score(k, s_.qm[wide, :], madd, h, kind) - self.lse[t.slot, h])
                ds = p * (nt(v, s_.dm[wide, :]) - s_.total[h])
                if self.causal:
                    s_.gb[kind, h] += ds
                low = ds.astype(BF16)
                s_.pcat[:, wide] = p.astype(BF16)
                s_.dcat[:, wide] = low
                s_.oacc[hs, :] += nn(self.kt[kb, hs, :], low)
            s_.dva[keys, :] += nn(s_.pcat[...], s_.dm[...])
            s_.dka[keys, :] += nn(s_.dcat[...], s_.qm[...])
            return carry

        lax.fori_loop(*self.key_blocks(t), tile, 0)
        return s_.oacc[...].T.astype(BF16)


def make_bias(s_, table, heads, ranges):
    lane = lax.broadcasted_iota(jnp.int32, (1, 2 * QB), 1)
    jj = lax.broadcasted_iota(jnp.int32, (QB, QB), 0)
    ii = lax.broadcasted_iota(jnp.int32, (QB, QB), 1)
    for h in range(heads):
        row = jnp.full((1, 2 * QB), table[h, NB - 1])
        for which, start, stop in reversed(ranges[:-1]):
            row = jnp.where(lane < stop, table[h, which], row)
        turned = pltpu.roll(jnp.broadcast_to(row, (QB, 2 * QB)), 0, 1, stride=1, stride_axis=0)
        s_.bias[0, h] = jnp.where(jj <= ii, turned[:, :QB], NEG)
        s_.bias[1, h] = turned[:, QB:]
        s_.bias[2, h] = jnp.full((QB, QB), table[h, NB - 1])
    s_.gb[...] = jnp.zeros_like(s_.gb)
    lane = lax.broadcasted_iota(jnp.int32, (1, 128), 1)
    first = jnp.full((1, 128), 2 * QB, jnp.int32)
    after = jnp.zeros((1, 128), jnp.int32)
    for which, start, stop in ranges:
        first = jnp.where(lane == which, start, first)
        after = jnp.where(lane == which, stop, after)
    dist = lax.broadcasted_iota(jnp.int32, (2 * QB, 128), 0)
    s_.pick[...] = jnp.where(jnp.logical_and(dist >= first, dist < after), 1.0, 0.0).astype(BF16)


def table_rows(s_, heads, n):
    near = [diagonal_sums(jnp.concatenate([s_.gb[0, h], s_.gb[1, h]], axis=1)) for h in range(heads)]
    near = jnp.concatenate(near + [jnp.zeros((8 - heads, 2 * QB), F32)], axis=0)
    sums = jnp.zeros((8, 128), F32)
    for _ in range(3):
        term = near.astype(BF16)
        sums = sums + nn(term, s_.pick[...])
        near = near - term.astype(F32)
    lane = lax.broadcasted_iota(jnp.int32, (1, 128), 1)
    place = lax.broadcasted_iota(jnp.int32, (16, 128), 0)
    rows = jnp.zeros((16, 128), F32)
    for h in range(heads):
        far = jnp.sum(jnp.sum(s_.gb[2, h], axis=0, keepdims=True), axis=1, keepdims=True)
        line = sums[h : h + 1, :] + jnp.where(lane == NB - 1, far, 0.0)
        rows = jnp.where(place == n * heads + h, jnp.broadcast_to(line, (16, 128)), rows)
    return rows


def weight_grad(dest, column, left, right, first, width):
    def one(m, carry):
        part = pl.ds(pl.multiple_of(m * 256, 256), 256)
        dest[part, column : column + width] = tn(left[:, part], right[:, first : first + width]).astype(BF16)
        return carry

    lax.fori_loop(0, left.shape[1] // 256, one, 0)


class Layer:
    def __init__(self, zy, sizes, ins, outs, slots):
        self.zy, self.sizes = zy, sizes
        rows, model, cols, hid, wrows, length = sizes
        heads = cols // DH
        self.heads = heads
        s_ = self.shared = SimpleNamespace()
        self.one = Attention(slots, s_, length, cols, True)
        self.two = Attention(slots, s_, length, cols, False)
        wide_rows, acc = VM((heads * QB, cols), BF16), VM((length, cols), F32)
        line, tiles, cat = VM((heads, 1, QB), F32), VM((3, heads, QB, QB), F32), VM((QB, heads * QB), BF16)
        slots.add(
            s_, segq=VM((length // HALF, 1, HALF), F32), bias=tiles, gb=tiles, qm=wide_rows, dm=wide_rows, peak=line, total=line,
            oacc=VM((cols, QB), F32), pcat=cat, dcat=cat, dva=acc, dka=acc, pick=VM((2 * QB, 128), BF16),
        )
        full, own = VM((length, model), BF16), VM((rows, model), F32)
        slots.add(
            self, full_self=full, full_mem=full, full_cross=full, full_ff=full, dy3=full, dy2=full, dy1=full,
            pa=full, pb=full, x_two=own, x_three=own, g=own, dkvq=VM((length, 3 * cols), BF16),
            hidden=VM((length, hid), BF16), dgu=VM((length, 2 * hid), BF16), small=VM((16, model), F32),
        )
        self.gathers = [RowGather(slots, rows) for _ in range(7)]
        self.g_self, self.g_mem, self.g_cross, self.g_ff, self.g_dy3, self.g_dy2, self.g_dy1 = self.gathers
        self.reduces = [RowReduce(slots, rows, model) for _ in range(7)]
        self.r_out1, self.r_out2, self.r_out3, self.r_dn3, self.r_dn2, self.r_mem, self.r_dn1 = self.reduces
        kinds = (
            (4 * cols, (2 * cols, 256, 4 * cols - 2 * cols - 256), 128),
            (4 * cols, (2 * cols, 2 * cols), 384),
            (3 * hid, (768, 3 * hid - 768), 384),
        )
        self.groups = [SimpleNamespace(width=w, parts=p, step=s) for w, p, s in kinds]
        self.ws, self.wc, self.wf = self.groups
        for group in self.groups:
            if zy:
                both = VM((model, group.width), BF16)
                slots.add(group, w=both, gp=both)
                group.gather = WideGather(slots, wrows, group.parts)
                group.reduce = WideReduce(slots, wrows, group.width, group.step)
            else:
                outs.add(group, gp=((model, group.width), BF16))
                group.gather = group.reduce = Idle()
        if zy:
            self.ss = SmallSum(slots, 16, model)

    def blk(self, b):
        return aligned(b * QB, QB)

    def chunk(self, k, block=0):
        size = self.sizes[0] // ROW_CHUNKS
        return aligned(block * self.sizes[0] + k * size, size)

    def far_first(self, i):
        s = self.spot
        far = jnp.where(i < 2, 1 - s.x, s.x)
        return far * 2 + jnp.where(i % 2 == 0, 1 - s.c, s.c)

    def near_tile(self, i):
        s = self.spot
        near = jnp.where(i == 0, s.n, s.sib)
        first = jnp.where(i < 2, 2 * near, 2 * s.xsib + i - 2)
        second = jnp.where(i < 2, 2 * near + 1, 2 * s.xp + i - 2)
        return Tile(i, first, second)

    def near_block(self, i):
        s = self.spot
        far = jnp.where(i < 2, s.x, 1 - s.x)
        return far * 2 + jnp.where(i % 2 == 0, s.c, 1 - s.c)

    def block_tile(self, b):
        return Tile(b, 2 * b, 2 * b + 1)

    def near_waits(self, i, gather):
        @pl.when(i == 1)
        def _():
            gather.have_sib()
            gather.forward(0, 1)

        @pl.when(i == 2)
        def _():
            gather.forward(1, 2)
            gather.have_xsib(0, 2)

        @pl.when(i == 3)
        def _():
            gather.forward(2, 4)
            gather.have_xsib(2, 4)

    def near_sends(self, i, reduce):
        @pl.when(i == 1)
        def _():
            reduce.send_own()

        @pl.when(i == 2)
        def _():
            reduce.send_far(0, 2)
            reduce.cross(0, 2)

        @pl.when(i == 3)
        def _():
            reduce.send_far(2, 4)
            reduce.cross(2, 4)

    def at(self, i, *actions):
        for j, action in enumerate(actions):
            if action is not None:
                pl.when(i == j)(action)

    def pack(self, group, *shards):
        rows = self.sizes[4]
        parts = [ref[...].astype(F32) for ref in shards]
        parts = [p if p.shape[0] == rows else p.T for p in parts]
        group.w[aligned(self.spot.w * rows, rows), :] = jnp.concatenate(parts, axis=1).astype(BF16)

    def ff_tile(self, t):
        f = self.sizes[3]
        step = f // 2
        w = self.wf.w
        x, dy = t.load(self.full_ff), t.load(self.dy3)
        for j in range(0, f, step):
            gate = nn(x, w[:, j : j + step])
            up = nn(x, w[:, f + j : f + j + step])
            dh = nn(dy, w[:, 2 * f + j : 2 * f + j + step])
            value, slope = gelu_parts(gate)
            t.store(self.hidden, (value * up).astype(BF16), j)
            t.store(self.dgu, (dh * up * slope).astype(BF16), j)
            t.store(self.dgu, (dh * value).astype(BF16), f + j)
        t.store(self.pa, nt(t.load(self.dgu), w[:, : 2 * f]).astype(BF16))

    def grads_kv(self):
        c = self.sizes[2]
        self.dkvq[:, : 2 * c] = jnp.concatenate(
            [self.shared.dka[...], self.shared.dva[...]], axis=1
        ).astype(BF16)

    def norm_backward(self, values, gain, reduce, base, done):
        gain_sum = jnp.zeros((1, self.sizes[1]), F32)
        for k in range(ROW_CHUNKS):
            rows = self.chunk(k)
            add, part = norm_back(values[rows, :].astype(F32), gain, reduce.total(k))
            gain_sum = gain_sum + part
            done(k, rows, base[rows, :].astype(F32) + add)
        return gain_sum

    def run(self):
        rows, model, cols, hid, wrows, length = self.sizes
        zy, heads, s_ = self.zy, self.heads, self.shared
        spot = self.spot = Spot(zy)
        one, two = self.one, self.two
        ws, wc, wf = self.groups
        greet(spot, zy)
        for gather, full in zip(
            self.gathers, (self.full_self, self.full_mem, self.full_cross, self.full_ff, self.dy3, self.dy2, self.dy1)
        ):
            gather.bind(spot, full)
        for reduce, part in zip(
            self.reduces, (self.pa, self.pb, self.pb, self.pa, self.pa, self.dgu, self.pa)
        ):
            reduce.bind(spot, part)
        column = 0
        for group in self.groups:
            group.gather.bind(spot, group.w)
            group.reduce.bind(spot, group.gp, self.red if zy else None, column)
            column += group.width
        one.bind(ws.w)
        two.bind(wc.w)
        gain_s, gain_c, gain_f = (ref[...].reshape(1, model) for ref in (self.gain_s, self.gain_c, self.gain_f))

        if zy:
            self.ss.bind(spot)
            self.pack(ws, self.sk, self.sv, self.sq, self.so)
        ws.gather.open_z()
        ws.gather.open_y()
        for k in range(ROW_CHUNKS):
            x = self.x[self.chunk(k), :].astype(F32)
            self.full_self[self.chunk(k, spot.n), :] = norm_rows(x, gain_s).astype(BF16)
            self.g_self.send(k)
        self.full_mem[self.blk(spot.n), :] = self.m[...]
        self.g_mem.send_all()
        self.dy3[self.blk(spot.n), :] = self.cot[...]
        self.g_dy3.send_all(0, 2)
        if zy:
            self.pack(wc, self.ck, self.cv, self.cq, self.co)
            self.pack(wf, self.fg, self.fu, self.fd)
        ranges = bucket_ranges(2 * QB)
        values = self.sid[...].astype(F32)
        one.kcol[...] = jnp.broadcast_to(values, (128, length)).T
        for h in range(length // HALF):
            s_.segq[h] = values[:, h * HALF : (h + 1) * HALF]
        make_bias(s_, self.table, heads, ranges)
        ws.gather.forward(1, 0)
        ws.gather.forward(2, 0)
        self.g_self.forward(0, 2)
        ws.gather.forward(3, 0)
        ws.gather.forward(1, 1)
        self.g_self.forward(2, 4)
        ws.gather.forward(2, 1)
        ws.gather.forward(3, 1)
        self.g_self.have_sib()
        self.g_self.have_xsib(0, 4)
        ws.gather.have(0)
        wc.gather.open_z()

        one.project_kv(self.full_self)
        for distance in (1, 2, 3):
            ws.gather.forward(distance, 2)
        wc.gather.open_y()
        ws.gather.have(1, 2)

        def self_block(i, carry):
            b = self.far_first(i)
            t = self.block_tile(b)
            one.project_q(self.full_self, t)
            one.forward(t)
            one.out_part(self.pa, t)

            def after_first():
                self.r_out1.send_far()
                wc.gather.forward(1)
                wf.gather.open_z()
                wc.gather.forward(2, 0)

            def after_second():
                self.r_out1.cross()
                self.g_mem.forward(0, 4)
                wc.gather.forward(3, 0)
                wc.gather.forward(2, 1)

            def after_third():
                self.r_out1.send_own()
                wc.gather.forward(3, 1)
                wf.gather.open_y()

            self.at(i, after_first, after_second, after_third)
            return carry

        lax.fori_loop(0, 4, self_block, 0)
        two.kcol[...] = jnp.broadcast_to(self.mid[...].astype(F32), (128, length)).T
        self.g_mem.have_sib()
        self.g_mem.have_xsib(0, 4)
        wc.gather.have()
        two.project_kv(self.full_mem)
        self.g_dy3.forward(0, 2)
        for k in range(ROW_CHUNKS):
            value = self.x[self.chunk(k), :].astype(F32) + self.r_out1.total(k)
            self.x_two[self.chunk(k), :] = value
            self.full_cross[self.chunk(k, spot.n), :] = norm_rows(value, gain_c).astype(BF16)
            self.g_cross.send(k)
        self.g_dy3.send_all(2, 4)
        wf.gather.forward(1, 0)

        def cross_block(i, carry):
            t = self.near_tile(i)
            self.near_waits(i, self.g_cross)
            two.project_q(self.full_cross, t)
            two.forward(t)
            two.out_part(self.pb, t)
            self.near_sends(i, self.r_out2)
            self.at(i, lambda: [wf.gather.forward(2, 0)] and None, lambda: [wf.gather.forward(3, 0), wf.gather.forward(1, 1)] and None, lambda: [wf.gather.forward(2, 1), wf.gather.forward(3, 1)] and None)
            return carry

        lax.fori_loop(0, 4, cross_block, 0)
        self.g_dy3.forward(2, 4)
        for k in range(ROW_CHUNKS):
            value = self.x_two[self.chunk(k), :] + self.r_out2.total(k)
            self.x_three[self.chunk(k), :] = value
            self.full_ff[self.chunk(k, spot.n), :] = norm_rows(value, gain_f).astype(BF16)
            self.g_ff.send(k)
        self.r_out1.finish()
        self.r_out2.finish()
        self.g_dy3.have_sib()
        self.g_dy3.have_xsib(0, 4)
        wf.gather.have()

        def ff_step(i, carry):
            self.near_waits(i, self.g_ff)
            self.ff_tile(self.near_tile(i))
            self.near_sends(i, self.r_dn3)
            return carry

        lax.fori_loop(0, 4, ff_step, 0)
        weight_grad(wf.gp, 0, self.full_ff, self.dgu, 0, 2 * hid)
        split = wf.reduce.chunks * 2 // 3
        for c in range(split):
            wf.reduce.open(c)

        def ff_out(b, carry):
            self.pb[self.blk(b), :] = nt(self.hidden[self.blk(b), :], wf.w[:, 2 * hid :]).astype(BF16)
            return carry

        lax.fori_loop(0, 4, ff_out, 0)
        self.r_out3.send_far()
        self.r_out3.send_own()
        weight_grad(wf.gp, 2 * hid, self.dy3, self.hidden, 0, hid)
        for c in range(split, wf.reduce.chunks):
            wf.reduce.open(c)

        def back_three(k, at, value):
            self.g[at, :] = value
            self.dy2[self.chunk(k, spot.n), :] = value.astype(BF16)
            self.g_dy2.send(k)

        gain_ff = self.norm_backward(self.x_three, gain_f, self.r_dn3, self.cot, back_three)
        self.small[14:15, :] = gain_ff
        self.r_out3.cross(0, 2)

        self.r_dn3.finish()
        s_.dka[...] = jnp.zeros_like(s_.dka)
        s_.dva[...] = jnp.zeros_like(s_.dva)

        def cross_back(i, carry):
            t = self.near_tile(i)
            self.near_waits(i, self.g_dy2)
            dctx = nn(t.load(self.dy2), two.wcols(3, 1)).astype(BF16)
            dq = two.backward(t, dctx)
            t.store(self.dkvq, dq, 2 * cols)
            t.store(self.pa, nt(dq, two.wcols(2, 1)).astype(BF16))
            self.near_sends(i, self.r_dn2)
            if zy:
                self.at(i, lambda: wf.reduce.first(0), lambda: wf.reduce.first(1), None, lambda: wf.reduce.first(2))
            return carry

        lax.fori_loop(0, 4, cross_back, 0)
        self.grads_kv()

        def memory_part(b, carry):
            blk = self.blk(b)
            self.dgu[blk, 0:model] = nt(self.dkvq[blk, : 2 * cols], two.wcols(0, 2)).astype(BF16)
            return carry

        lax.fori_loop(0, 4, memory_part, 0)
        self.r_mem.send_far()
        self.r_mem.send_own()
        if zy:
            wf.reduce.first(3)

        def back_two(k, at, value):
            self.g[at, :] = value
            self.dy1[self.chunk(k, spot.n), :] = value.astype(BF16)
            self.g_dy1.send(k)

        gain_cross = self.norm_backward(self.x_two, gain_c, self.r_dn2, self.g, back_two)
        self.small[13:14, :] = gain_cross
        self.r_out3.cross(2, 4)
        self.r_mem.cross()
        weight_grad(wc.gp, 0, self.full_mem, self.dkvq, 0, 2 * cols)
        wc.reduce.open(0)
        weight_grad(wc.gp, 2 * cols, self.full_cross, self.dkvq, 2 * cols, cols)
        weight_grad(wc.gp, 3 * cols, self.dy2, two.ctx, 0, cols)
        wc.reduce.open(1)

        s_.dka[...] = jnp.zeros_like(s_.dka)
        s_.dva[...] = jnp.zeros_like(s_.dva)

        def self_waits(i):
            @pl.when(i == 1)
            def _():
                self.g_dy1.have_sib()
                self.g_dy1.forward(0, 1)

            @pl.when(i == 2)
            def _():
                self.g_dy1.forward(1, 4)

            @pl.when(i == 3)
            def _():
                self.g_dy1.have_xsib(0, 4)

        def self_back(i, carry):
            b = self.near_block(i)
            t = self.block_tile(b)
            self_waits(i)
            dctx = nn(t.load(self.dy1), one.wcols(3, 1)).astype(BF16)
            t.store(self.dkvq, one.backward(t, dctx), 2 * cols)

            def ff_totals():
                for c in range(wf.reduce.chunks):
                    wf.reduce.total(c)

            self.at(i, lambda: wc.reduce.first(0), ff_totals, lambda: wc.reduce.first(1))
            return carry

        lax.fori_loop(0, 4, self_back, 0)
        self.grads_kv()
        self.r_dn2.finish()

        def last_part(i, carry):
            blk = self.blk(self.far_first(i))
            self.pa[blk, :] = nt(self.dkvq[blk, :], one.wcols(0, 3)).astype(BF16)
            return carry

        lax.fori_loop(0, 2, last_part, 0)
        self.r_dn1.send_far()
        weight_grad(ws.gp, 0, self.full_self, self.dkvq, 0, 3 * cols)
        weight_grad(ws.gp, 3 * cols, self.dy1, one.ctx, 0, cols)
        for c in range(ws.reduce.chunks):
            ws.reduce.open(c)
        self.r_dn1.cross()
        lax.fori_loop(2, 4, last_part, 0)
        self.r_dn1.send_own()

        def gain_part(b, total):
            blk = self.blk(b)
            both = self.full_self[blk, :].astype(F32) * self.pa[blk, :].astype(F32)
            return total + jnp.sum(both, axis=0, keepdims=True)

        gain_self = lax.fori_loop(0, 4, gain_part, jnp.zeros((1, model), F32)) / gain_s
        keep = self.small[13:15, :]
        self.small[...] = jnp.zeros_like(self.small)
        self.small[:, 0:128] = table_rows(s_, heads, spot.n)
        self.small[12:13, :] = gain_self
        self.small[13:15, :] = keep
        if zy:
            self.ss.begin(self.small[...])
        else:
            self.tot[...] = self.small[...]
        for k in range(ROW_CHUNKS):
            value = self.x_three[self.chunk(k), :] + self.r_out3.total(k)
            self.result[self.chunk(k), :] = value.astype(BF16)
        if zy:
            self.ss.step(0)
            ws.reduce.first(0)
            ws.reduce.first(1)
        for k in range(ROW_CHUNKS):
            self.gm[self.chunk(k), :] = self.r_mem.total(k).astype(BF16)
        for c in range(wc.reduce.chunks):
            wc.reduce.total(c)
        if zy:
            ws.reduce.first(2)

        def back_one(k, at, value):
            self.gx[at, :] = value.astype(BF16)
            if zy and k == 1:
                ws.reduce.first(3)
            if zy and k == 3:
                self.ss.step(1)

        self.norm_backward(self.x, gain_s, self.r_dn1, self.g, back_one)
        if zy:
            ws.reduce.first(4)
            self.ss.step(2)
            ws.reduce.first(5)
            for c in range(ws.reduce.chunks):
                ws.reduce.total(c)
            self.ss.end(self.tot)

        for gather in self.gathers:
            gather.finish()
        for reduce in (self.r_out3, self.r_mem, self.r_dn1):
            reduce.finish()
        for group in self.groups:
            group.gather.finish()
            group.reduce.finish()


def deliver(red, tot, passed, sizes, heads):
    rows, model, cols, hid, wrows, length = sizes
    ins, outs = Slots(), Slots()
    packed, small = SimpleNamespace(), SimpleNamespace()
    ins.add(packed, ref=(red, VM))
    ins.add(small, ref=(tot, VM))
    sources, dests = [SimpleNamespace() for _ in passed], [SimpleNamespace() for _ in passed]
    for value, source, dest in zip(passed, sources, dests):
        ins.add(source, ref=(value, VM))
        outs.add(dest, ref=(value.shape, value.dtype))
    places = [(i * cols, cols, i % 4 == 3) for i in (2, 0, 1, 3, 6, 4, 5, 7)]
    places += [(8 * cols + i * hid, hid, False) for i in range(3)]
    cuts = []
    for at, width, turn in places:
        cut = SimpleNamespace(at=at, width=width, turn=turn)
        outs.add(cut, ref=((width, wrows) if turn else (wrows, width), F32))
        cuts.append(cut)
    gains, table = [SimpleNamespace() for _ in range(3)], SimpleNamespace()
    for gain in gains:
        outs.add(gain, ref=((model,), F32))
    outs.add(table, ref=((4 * heads, NB), F32))

    def body():
        for source, dest in zip(sources, dests):
            dest.ref[...] = source.ref[...]
        for cut in cuts:
            part = packed.ref[:, cut.at : cut.at + cut.width]
            cut.ref[...] = part.T if cut.turn else part
        for i, gain in enumerate(gains):
            gain.ref[...] = small.ref[12 + i : 13 + i, :].reshape(model)
        table.ref[...] = small.ref[0 : 4 * heads, 0:NB]

    got = run_kernel(body, ins, outs, Slots(), None, "deliver")
    return got[:3], got[3:14], got[14:17], got[17]


def shards(
    zy, inputs, memory, segment_ids, memory_ids, self_gain, self_query, self_key, self_value, self_out, bias_table,
    cross_gain, cross_query, cross_key, cross_value, cross_out, ff_gain, ff_gate, ff_up, ff_down, cotangent,
):
    rows, model = inputs.shape
    length = segment_ids.shape[1]
    wrows, cols = self_query.shape
    hid = ff_gate.shape[1]
    heads = cols // DH
    assert segment_ids.shape[0] == 1 and rows == QB and length == 4 * QB == memory_ids.shape[1]
    sizes = (rows, model, cols, hid, wrows, length)
    ins, outs, slots = Slots(), Slots(), Slots()
    layer = Layer.__new__(Layer)
    outs.add(
        layer, result=((rows, model), BF16), gx=((rows, model), BF16), gm=((rows, model), BF16), tot=((16, model), F32)
    )
    if zy:
        outs.add(layer, red=((wrows, 8 * cols + 3 * hid), F32))
    layer.__init__(zy, sizes, ins, outs, slots)
    ins.add(
        layer, x=(inputs, VM), m=(memory, VM), cot=(cotangent, VM), sid=(segment_ids, VM), mid=(memory_ids, VM),
        gain_s=(self_gain, VM), gain_c=(cross_gain, VM), gain_f=(ff_gain, VM), table=(bias_table.T, pltpu.SMEM),
    )
    if zy:
        ins.add(
            layer, sq=(self_query, VM), sk=(self_key, VM), sv=(self_value, VM), so=(self_out, VM),
            cq=(cross_query, VM), ck=(cross_key, VM), cv=(cross_value, VM), co=(cross_out, VM),
            fg=(ff_gate, VM), fu=(ff_up, VM), fd=(ff_down.T, VM),
        )
    else:

        def whole(*parts):
            return lax.all_gather(jnp.concatenate(parts, axis=1), WIDE, axis=0, tiled=True)

        ins.add(layer.ws, w=(whole(self_key, self_value, self_query, self_out.T), VM))
        ins.add(layer.wc, w=(whole(cross_key, cross_value, cross_query, cross_out.T), VM))
        ins.add(layer.wf, w=(whole(ff_gate, ff_up, ff_down.T), VM))
    got = run_kernel(layer.run, ins, outs, slots, 0, "layer")
    if zy:
        total, red = got[3], got[4]
    else:
        packed = jnp.concatenate(got[4:7], axis=1)
        red = lax.psum_scatter(packed, WIDE, scatter_dimension=0, tiled=True).astype(F32)
        total = lax.psum(got[3], (WIDE, NARROW))
    row_outs, grads, gains, table = deliver(red, total, got[:3], sizes, heads)
    return (
        *row_outs,
        gains[0],
        *grads[0:4],
        table.T,
        gains[1],
        *grads[4:8],
        gains[2],
        grads[8],
        grads[9],
        grads[10].T,
    )


def solution(mesh):
    zy = mesh.shape[WIDE] == 8
    rows = P((WIDE, NARROW), None)
    w_in, w_out = P(WIDE, NARROW), P(NARROW, WIDE)
    placed = (
        rows, rows, P(WIDE, None), P(WIDE, None), P(),
        w_in, w_in, w_in, w_out, P(None, NARROW), P(),
        w_in, w_in, w_in, w_out, P(), w_in, w_in, w_out, rows,
    )
    outs = (
        rows, rows, rows, P(), w_in, w_in, w_in, w_out, P(), P(),
        w_in, w_in, w_in, w_out, P(), w_in, w_in, w_out,
    )

    def program(*args):
        return shards(zy, *args)

    return jax.shard_map(program, mesh=mesh, in_specs=placed, out_specs=outs, check_vma=False)
```

```python
import math
from types import SimpleNamespace

import jax
import jax.numpy as jnp
import numpy as np
from jax import lax
from jax.experimental import pallas as pl
from jax.experimental.pallas import tpu as pltpu
from jax.sharding import PartitionSpec as P

DH = 64
NB = 32
MAX_DIST = 128
EPS = 1e-06
NEG = -1e30
QB = 256
HALF = 128
ROW_CHUNKS = 4
WIDE = "wide"
NARROW = "narrow"
MESH = pl.DeviceIdType.MESH
F32 = jnp.float32
BF16 = jnp.bfloat16
VM = pltpu.VMEM
DMA = pltpu.SemaphoreType.DMA


def bucket_table(length, buckets, reach):
    exact_part = buckets // 2
    distance = np.arange(length)
    spread = (
        np.log(np.maximum(distance, exact_part) / exact_part)
        / np.log(reach / exact_part)
        * (buckets - exact_part)
    )
    far_bucket = np.minimum(exact_part + np.floor(spread).astype(np.int64), buckets - 1)
    return np.where(distance < exact_part, distance, far_bucket).astype(np.int32)


def bucket_ranges(length):
    table = bucket_table(length, NB, MAX_DIST)
    found = []
    for which in range(NB):
        places = np.nonzero(table == which)[0]
        if len(places):
            found.append((which, int(places[0]), int(places[-1]) + 1))
    return found


class Slots:
    def __init__(self):
        self.items = []

    def add(self, holder, **specs):
        for name, spec in specs.items():
            self.items.append((holder, name, spec))

    def fill(self, refs):
        for (holder, name, _), ref in zip(self.items, refs):
            setattr(holder, name, ref)


def run_kernel(body, ins, outs, scratch, cid, name):
    counts = len(ins.items), len(outs.items)

    def kernel(*refs):
        ins.fill(refs[: counts[0]])
        outs.fill(refs[counts[0] : counts[0] + counts[1]])
        scratch.fill(refs[counts[0] + counts[1] :])
        body()

    params = {} if cid is None else dict(collective_id=cid, has_side_effects=True)
    return pl.pallas_call(
        kernel,
        out_shape=[jax.ShapeDtypeStruct(*spec) for _, _, spec in outs.items],
        in_specs=[pl.BlockSpec(memory_space=spec[1]) for _, _, spec in ins.items],
        out_specs=[pl.BlockSpec(memory_space=VM) for _ in outs.items],
        scratch_shapes=[spec for _, _, spec in scratch.items],
        compiler_params=pltpu.CompilerParams(vmem_limit_bytes=66_900_000, **params),
        name=name,
    )(*[spec[0] for _, _, spec in ins.items])


class Spot:
    def __init__(self, wide_split):
        n = lax.axis_index(NARROW)
        self.n = n
        self.x = n // 2
        self.c = n % 2
        self.sib = self.x * 2 + (1 - self.c)
        self.xp = (1 - self.x) * 2 + self.c
        self.xsib = (1 - self.x) * 2 + (1 - self.c)
        if wide_split:
            w = lax.axis_index(WIDE)
            self.w = w
            self.z = w // 2
            self.y = w % 2
            self.yp = self.z * 2 + (1 - self.y)

    def at_n(self, n):
        return {NARROW: n}

    def at_w(self, w):
        return {WIDE: w}

    def at_z(self, z):
        return {WIDE: z * 2 + self.y}


def remote(src, dst, send, recv, dev):
    return pltpu.make_async_remote_copy(
        src_ref=src, dst_ref=dst, send_sem=send, recv_sem=recv, device_id=dev, device_id_type=MESH
    )


def greet(spot, zy):
    barrier = pltpu.get_barrier_semaphore()

    def hello(dev):
        pl.semaphore_signal(barrier, inc=1, device_id=dev, device_id_type=MESH)

    hello(spot.at_n(spot.sib))
    hello(spot.at_n(spot.xp))
    if zy:
        hello(spot.at_w(spot.yp))
        for step in range(1, 4):
            hello(spot.at_z((spot.z + step) % 4))
    pl.semaphore_wait(barrier, 6 if zy else 2)


def aligned(start, size):
    return pl.ds(pl.multiple_of(start, 16), size)


class RowGather:
    def __init__(self, slots, rows, chunks=ROW_CHUNKS):
        self.nrows, self.chunks, self.size = rows, chunks, rows // chunks
        sems = DMA((chunks,))
        slots.add(self, xs=sems, xr=sems, ss=sems, sr=sems, fs=sems, fr=sems)

    def bind(self, spot, full):
        self.spot, self.full = spot, full

    def hop(self, k, block, dev, send, recv):
        rows = self.full.at[aligned(block * self.nrows + k * self.size, self.size)]
        return remote(rows, rows, send.at[k], recv.at[k], self.spot.at_n(dev))

    def to_x(self, k):
        return self.hop(k, self.spot.n, self.spot.xp, self.xs, self.xr)

    def from_x(self, k):
        return self.hop(k, self.spot.xp, self.spot.xp, self.xs, self.xr)

    def to_sib(self, k):
        return self.hop(k, self.spot.n, self.spot.sib, self.ss, self.sr)

    def from_sib(self, k):
        return self.hop(k, self.spot.sib, self.spot.sib, self.ss, self.sr)

    def onward(self, k):
        return self.hop(k, self.spot.xp, self.spot.sib, self.fs, self.fr)

    def from_onward(self, k):
        return self.hop(k, self.spot.xsib, self.spot.sib, self.fs, self.fr)

    def send(self, k):
        self.to_x(k).start()
        self.to_sib(k).start()

    def send_all(self, first=0, after=ROW_CHUNKS):
        for k in range(first, after):
            self.send(k)

    def forward(self, first, after):
        for k in range(first, after):
            self.from_x(k).wait_recv()
            self.onward(k).start()

    def have_sib(self):
        for k in range(self.chunks):
            self.from_sib(k).wait_recv()

    def have_xsib(self, first, after):
        for k in range(first, after):
            self.from_onward(k).wait_recv()

    def finish(self):
        for k in range(self.chunks):
            self.to_x(k).wait_send()
            self.to_sib(k).wait_send()
            self.onward(k).wait_send()


class RowReduce:
    def __init__(self, slots, rows, cols, chunks=ROW_CHUNKS):
        self.nrows, self.ncols, self.chunks, self.size = rows, cols, chunks, rows // chunks
        sems, buf = DMA((chunks,)), VM((rows, cols), BF16)
        slots.add(self, as_=sems, ar=sems, bs=sems, br=sems, xs=sems, xr=sems, far=buf, own=buf, inn=buf)

    def bind(self, spot, part):
        self.spot, self.part = spot, part

    def buf(self, ref, k):
        return ref.at[pl.ds(k * self.size, self.size)]

    def mine(self, block, k):
        return self.part.at[aligned(block * self.nrows + k * self.size, self.size), pl.ds(0, self.ncols)]

    def far_sib(self, k):
        s = self.spot
        return remote(self.mine(s.xsib, k), self.buf(self.far, k), self.as_.at[k], self.ar.at[k], s.at_n(s.sib))

    def own_sib(self, k):
        s = self.spot
        return remote(self.mine(s.sib, k), self.buf(self.own, k), self.bs.at[k], self.br.at[k], s.at_n(s.sib))

    def across(self, k):
        s = self.spot
        return remote(self.buf(self.far, k), self.buf(self.inn, k), self.xs.at[k], self.xr.at[k], s.at_n(s.xp))

    def send_far(self, first=0, after=ROW_CHUNKS):
        for k in range(first, after):
            self.far_sib(k).start()

    def send_own(self):
        for k in range(self.chunks):
            self.own_sib(k).start()

    def cross(self, first=0, after=ROW_CHUNKS):
        for k in range(first, after):
            self.far_sib(k).wait_recv()
            here = self.buf(self.far, k)
            here[...] = (self.mine(self.spot.xp, k)[...].astype(F32) + here[...].astype(F32)).astype(BF16)
            self.across(k).start()

    def total(self, k):
        self.own_sib(k).wait_recv()
        self.across(k).wait_recv()
        value = self.mine(self.spot.n, k)[...].astype(F32) + self.buf(self.own, k)[...].astype(F32)
        return value + self.buf(self.inn, k)[...].astype(F32)

    def finish(self):
        for k in range(self.chunks):
            self.far_sib(k).wait_send()
            self.own_sib(k).wait_send()
            self.across(k).wait_send()


class WideGather:
    steps = (1, -1, 2, -2, 3, -3)

    def __init__(self, slots, rows, widths):
        self.nrows, self.widths, self.parts = rows, widths, range(len(widths))
        four = DMA((4, len(widths)))
        slots.add(self, zs=DMA((6, len(widths))), zr=four, ys=four, yr=four)

    def bind(self, spot, full):
        self.spot, self.full = spot, full

    def rows(self, z, y, part):
        cols = pl.ds(sum(self.widths[:part]), self.widths[part])
        return self.full.at[aligned((z * 2 + y) * self.nrows, self.nrows), cols]

    def along(self, i, part):
        s = self.spot
        rows = self.rows(s.z, s.y, part)
        return remote(rows, rows, self.zs.at[i, part], self.zr.at[s.z, part], s.at_z(s.z + self.steps[i]))

    def came(self, z, part):
        s = self.spot
        rows = self.rows(z, s.y, part)
        return remote(rows, rows, self.zs.at[0, part], self.zr.at[z, part], s.at_z(z))

    def over(self, z, part):
        s = self.spot
        rows = self.rows(z, s.y, part)
        return remote(rows, rows, self.ys.at[z, part], self.yr.at[z, part], s.at_w(s.yp))

    def crossed(self, z, part):
        s = self.spot
        rows = self.rows(z, 1 - s.y, part)
        return remote(rows, rows, self.ys.at[z, part], self.yr.at[z, part], s.at_w(s.yp))

    def when_inside(self, step, fn):
        there = self.spot.z + step

        @pl.when(there >= 0 if step < 0 else there <= 3)
        def _():
            fn(there)

    def open_y(self):
        for part in self.parts:
            self.over(self.spot.z, part).start()

    def open_z(self):
        for part in self.parts:
            for i, step in enumerate(self.steps):
                self.when_inside(step, lambda there: self.along(i, part).start())

    def forward(self, distance, *parts):
        for part in parts or self.parts:
            for step in (distance, -distance):

                def pass_on(there):
                    self.came(there, part).wait_recv()
                    self.over(there, part).start()

                self.when_inside(step, pass_on)

    def have(self, *parts):
        for part in parts or self.parts:
            for z in range(4):
                self.crossed(z, part).wait_recv()

    def finish(self):
        for part in self.parts:
            for z in range(4):
                self.over(z, part).wait_send()
            for i, step in enumerate(self.steps):
                self.when_inside(step, lambda there: self.along(i, part).wait_send())


class WideReduce:
    steps = (2, 3, 1, 0)

    def __init__(self, slots, rows, cols, width):
        self.nrows, self.width, self.chunks = rows, width, cols // width
        sems, buf = DMA((self.chunks, 4)), VM((4, rows, cols), BF16)
        slots.add(self, ys=sems, yr=sems, zs=sems, zr=sems, acc=buf, inn=buf)

    def bind(self, spot, part, out, out_col):
        self.spot, self.part, self.out, self.out_col = spot, part, out, out_col

    def cols(self, c):
        return pl.ds(c * self.width, self.width)

    def slab(self, c, z, y):
        return self.part.at[aligned((z * 2 + y) * self.nrows, self.nrows), self.cols(c)]

    def over(self, c, z):
        s = self.spot
        return remote(
            self.slab(c, z, 1 - s.y), self.acc.at[z, :, self.cols(c)], self.ys.at[c, z], self.yr.at[c, z], s.at_w(s.yp)
        )

    def along(self, c, z):
        s = self.spot
        return remote(
            self.acc.at[z, :, self.cols(c)], self.inn.at[s.z, :, self.cols(c)],
            self.zs.at[c, z], self.zr.at[c, s.z], s.at_z(z),
        )

    def came(self, c, z):
        here = self.inn.at[z, :, self.cols(c)]
        return remote(here, here, self.zs.at[c, z], self.zr.at[c, z], self.spot.at_z(z))

    def targets(self):
        return [(self.spot.z + step) % 4 for step in self.steps]

    def open(self, c):
        for z in self.targets():
            self.over(c, z).start()

    def first(self, c):
        for step, z in zip(self.steps, self.targets()):
            self.over(c, z).wait_recv()
            here = self.acc.at[z, :, self.cols(c)]
            here[...] = (self.slab(c, z, self.spot.y)[...].astype(F32) + here[...].astype(F32)).astype(BF16)
            if step:
                self.along(c, z).start()

    def total(self, c):
        value = self.acc[self.spot.z, :, self.cols(c)].astype(F32)
        for z in self.targets()[:3]:
            self.came(c, z).wait_recv()
            value = value + self.inn[z, :, self.cols(c)].astype(F32)
        self.out[:, pl.ds(self.out_col + c * self.width, self.width)] = value

    def finish(self):
        for c in range(self.chunks):
            for step, z in zip(self.steps, self.targets()):
                self.over(c, z).wait_send()
                if step:
                    self.along(c, z).wait_send()


class SmallSum:
    def __init__(self, slots, rows, cols):
        four = VM((4, rows, cols), F32)
        slots.add(
            self, ps=DMA((3,)), pr=DMA((3,)), zs=DMA((4,)), zr=DMA((4,)), held=four, inn=VM((3, rows, cols), F32), zin=four
        )

    def bind(self, spot):
        self.spot = spot

    def pair(self, i):
        s = self.spot
        dev = (s.at_n(s.sib), s.at_n(s.xp), s.at_w(s.yp))[i]
        return remote(self.held.at[i], self.inn.at[i], self.ps.at[i], self.pr.at[i], dev)

    def hop(self, step, landed):
        other = (self.spot.z + step) % 4
        return remote(
            self.held.at[3], self.zin.at[landed], self.zs.at[step], self.zr.at[landed], self.spot.at_z(other)
        )

    def begin(self, value):
        self.held[0] = value
        self.pair(0).start()

    def step(self, i):
        self.pair(i).wait_recv()
        self.held[i + 1] = self.held[i] + self.inn[i]
        if i < 2:
            self.pair(i + 1).start()
        else:
            self.zin[self.spot.z] = self.held[3]
            for step in range(1, 4):
                self.hop(step, self.spot.z).start()

    def end(self, out):
        for step in range(1, 4):
            self.hop(step, (self.spot.z + step) % 4).wait_recv()
        out[...] = ((self.zin[0] + self.zin[1]) + self.zin[2]) + self.zin[3]
        for i in range(3):
            self.pair(i).wait_send()
        for step in range(1, 4):
            self.hop(step, self.spot.z).wait_send()


class Idle:
    chunks = 0

    def bind(self, *args):
        pass

    open = open_y = open_z = forward = have = finish = first = total = bind


def nt(left, right):
    return lax.dot_general(left, right, (((1,), (1,)), ((), ())), preferred_element_type=F32)


def nn(left, right):
    return lax.dot_general(left, right, (((1,), (0,)), ((), ())), preferred_element_type=F32)


def tn(left, right):
    return lax.dot_general(left, right, (((0,), (0,)), ((), ())), preferred_element_type=F32)


def mean_square(values):
    return jnp.mean(values * values, axis=-1, keepdims=True)


def norm_rows(values, gain):
    return values * lax.rsqrt(mean_square(values) + EPS) * gain


def norm_back(values, gain, dn):
    r = lax.rsqrt(mean_square(values) + EPS)
    u = values * r
    dg = dn * gain
    rows = r * (dg - u * jnp.mean(dg * u, axis=-1, keepdims=True))
    return rows, jnp.sum(dn * u, axis=0, keepdims=True)


def gelu_parts(v):
    c = math.sqrt(2.0 / math.pi)
    t = jnp.tanh(c * (v + 0.044715 * v * v * v))
    value = 0.5 * v * (1.0 + t)
    slope = 0.5 * (1.0 + t) + 0.5 * v * (1.0 - t * t) * c * (1.0 + 3.0 * 0.044715 * v * v)
    return value, slope


def head_rows(values, h, heads):
    lane = lax.broadcasted_iota(jnp.int32, values.shape, 1) // DH
    return jnp.where(jnp.logical_or(lane == h, lane >= heads), values, jnp.zeros_like(values))


def document_columns(query_ref, key_ref, ids, first):
    column = jnp.broadcast_to(ids[...].astype(F32), (128, ids.shape[1])).T[:, :DH]
    lane = lax.broadcasted_iota(jnp.int32, column.shape, 1)
    same = column == lane.astype(F32)
    if query_ref is not None:
        for ref in query_ref:
            ref[:, first : first + DH] = jnp.where(same, 1.0, 0.0).astype(BF16)
    if key_ref is not None:
        other = jnp.logical_and(jnp.logical_not(same), lane < 4)
        key_ref[:, first : first + DH] = jnp.where(other, NEG, 0.0).astype(BF16)


def diagonal_sums(tile):
    rows, width = tile.shape
    while rows > 1:
        rows = rows // 2
        tile = tile[:rows] + pltpu.roll(tile[rows:], width - rows, 1)
    return tile


class Tile:
    def __init__(self, slot, first, second):
        self.slot, self.halves = slot, (first, second)

    def rows(self, half):
        return aligned(half * HALF, HALF)

    def load(self, ref):
        return jnp.concatenate([ref[self.rows(h), :] for h in self.halves], axis=0)

    def store(self, ref, value, at=0):
        for i, h in enumerate(self.halves):
            ref[self.rows(h), at : at + value.shape[1]] = value[i * HALF : (i + 1) * HALF]


class Attention:
    def __init__(self, slots, shared, length, cols, causal):
        self.shared, self.cols, self.heads, self.causal = shared, cols, cols // DH, causal
        rows, marked, turned = VM((length, cols), BF16), VM((length, cols + DH), BF16), VM((4, cols, QB), BF16)
        slots.add(
            self, q=marked, k=marked, v=rows, ctx=rows, kt=turned, vt=turned, lse=VM((4, self.heads, 1, QB), F32)
        )

    def bind(self, weights, pcat, dcat):
        self.w, self.pcat, self.dcat = weights, pcat, dcat

    def blk(self, b):
        return aligned(b * QB, QB)

    def wcols(self, first, count):
        return self.w[:, first * self.cols : (first + count) * self.cols]

    def window(self, t, body):
        if not self.causal:
            body(0, 4)
            return
        for count in (1, 2, 3):
            pl.when(jnp.minimum(t.slot + 1, 3) == count)(lambda: body(t.slot + 1 - count, count))

    def keys(self, first, count):
        return aligned(first * QB, count * QB)

    def score(self, k, h, count):
        s = nt(k, self.shared.qm[self.wide_of(h), :])
        if self.causal:
            s = s + jnp.concatenate([self.shared.bias[self.kind(j, count), h] for j in range(count)], axis=0)
        return s

    def kind(self, j, count):
        return min(count - 1 - j, 2)

    def over_keys(self, turned, first, count, hs, right):
        parts = [nn(turned[first + j, hs, :], right[j * QB : (j + 1) * QB]) for j in range(count)]
        return sum(parts[1:], parts[0])

    def project_kv(self, source):
        c = self.cols

        def one(b, carry):
            kv = nn(source[self.blk(b), :], self.wcols(0, 2))
            k, v = kv[:, :c], kv[:, c:]
            self.k[self.blk(b), :c] = k.astype(BF16)
            self.v[self.blk(b), :] = v.astype(BF16)
            self.kt[b] = k.T.astype(BF16)
            self.vt[b] = v.T.astype(BF16)
            return carry

        lax.fori_loop(0, 4, one, 0)

    def project_q(self, source, t):
        t.store(self.q, nn(t.load(source), self.wcols(2, 1)).astype(BF16))

    def out_part(self, dest, t):
        t.store(dest, nt(t.load(self.ctx), self.wcols(3, 1)).astype(BF16))

    def rows_of(self, h):
        return slice(h * DH, (h + 1) * DH)

    def wide_of(self, h):
        return slice(h * QB, (h + 1) * QB)

    def forward(self, t):
        s_ = self.shared
        q = t.load(self.q)
        for h in range(self.heads):
            s_.qm[self.wide_of(h), :] = head_rows(q, h, self.heads)

        def attend(first, count):
            k = self.k[self.keys(first, count), :]
            for h in range(self.heads):
                hs = self.rows_of(h)
                s = self.score(k, h, count)
                peak = jnp.max(s, axis=0, keepdims=True)
                x = jnp.exp(s - peak)
                total = jnp.sum(x, axis=0, keepdims=True)
                s_.oacc[hs, :] = self.over_keys(self.vt, first, count, hs, x.astype(BF16)) / total
                self.lse[t.slot, h] = peak + jnp.log(total)

        self.window(t, attend)
        t.store(self.ctx, s_.oacc[...].T.astype(BF16))

    def backward(self, t, dctx):
        s_ = self.shared
        q = t.load(self.q)
        prod = (dctx.astype(F32) * t.load(self.ctx).astype(F32)).T
        for h in range(self.heads):
            s_.qm[self.wide_of(h), :] = head_rows(q, h, self.heads)
            s_.dm[self.wide_of(h), :] = head_rows(dctx, h, self.heads)
            s_.delta[h] = jnp.sum(prod[self.rows_of(h), :], axis=0, keepdims=True)

        def attend(first, count):
            keys, span = self.keys(first, count), count * QB
            k, v = self.k[keys, :], self.v[keys, :]
            for h in range(self.heads):
                hs, wide = self.rows_of(h), self.wide_of(h)
                p = jnp.exp(self.score(k, h, count) - self.lse[t.slot, h])
                ds = p * (nt(v, s_.dm[wide, :]) - s_.delta[h])
                if self.causal:
                    for j in range(count):
                        s_.gb[self.kind(j, count), h] += ds[j * QB : (j + 1) * QB]
                low = ds.astype(BF16)
                self.pcat[:span, wide] = p.astype(BF16)
                self.dcat[:span, wide] = low
                s_.oacc[hs, :] = self.over_keys(self.kt, first, count, hs, low)
            s_.dva[keys, :] += nn(self.pcat[:span, :], s_.dm[...])
            s_.dka[keys, :] += nn(self.dcat[:span, :], s_.qm[...])

        self.window(t, attend)
        return s_.oacc[...].T.astype(BF16)


def make_bias(s_, table, heads, ranges):
    lane = lax.broadcasted_iota(jnp.int32, (1, 2 * QB), 1)
    jj = lax.broadcasted_iota(jnp.int32, (QB, QB), 0)
    ii = lax.broadcasted_iota(jnp.int32, (QB, QB), 1)
    for h in range(heads):
        row = jnp.full((1, 2 * QB), table[h, NB - 1])
        for which, start, stop in reversed(ranges[:-1]):
            row = jnp.where(lane < stop, table[h, which], row)
        turned = pltpu.roll(jnp.broadcast_to(row, (QB, 2 * QB)), 0, 1, stride=1, stride_axis=0)
        s_.bias[0, h] = jnp.where(jj <= ii, turned[:, :QB], NEG)
        s_.bias[1, h] = turned[:, QB:]
        s_.bias[2, h] = jnp.full((QB, QB), table[h, NB - 1])
    s_.gb[...] = jnp.zeros_like(s_.gb)
    lane = lax.broadcasted_iota(jnp.int32, (1, 128), 1)
    first = jnp.full((1, 128), 2 * QB, jnp.int32)
    after = jnp.zeros((1, 128), jnp.int32)
    for which, start, stop in ranges:
        first = jnp.where(lane == which, start, first)
        after = jnp.where(lane == which, stop, after)
    dist = lax.broadcasted_iota(jnp.int32, (2 * QB, 128), 0)
    s_.pick[...] = jnp.where(jnp.logical_and(dist >= first, dist < after), 1.0, 0.0).astype(BF16)


def table_rows(s_, heads, n):
    near = [diagonal_sums(jnp.concatenate([s_.gb[0, h], s_.gb[1, h]], axis=1)) for h in range(heads)]
    near = jnp.concatenate(near + [jnp.zeros((8 - heads, 2 * QB), F32)], axis=0)
    sums = jnp.zeros((8, 128), F32)
    for _ in range(3):
        term = near.astype(BF16)
        sums = sums + nn(term, s_.pick[...])
        near = near - term.astype(F32)
    lane = lax.broadcasted_iota(jnp.int32, (1, 128), 1)
    place = lax.broadcasted_iota(jnp.int32, (16, 128), 0)
    rows = jnp.zeros((16, 128), F32)
    for h in range(heads):
        far = jnp.sum(jnp.sum(s_.gb[2, h], axis=0, keepdims=True), axis=1, keepdims=True)
        line = sums[h : h + 1, :] + jnp.where(lane == NB - 1, far, 0.0)
        rows = jnp.where(place == n * heads + h, jnp.broadcast_to(line, (16, 128)), rows)
    return rows


def weight_grad(dest, column, left, right, first, width):
    def one(m, carry):
        part = pl.ds(pl.multiple_of(m * 256, 256), 256)
        dest[part, column : column + width] = tn(left[:, part], right[:, first : first + width]).astype(BF16)
        return carry

    lax.fori_loop(0, left.shape[1] // 256, one, 0)


class Layer:
    def __init__(self, zy, sizes, ins, outs, slots):
        self.zy, self.sizes = zy, sizes
        rows, model, cols, hid, wrows, length = sizes
        heads = cols // DH
        self.heads = heads
        s_ = self.shared = SimpleNamespace()
        self.one = Attention(slots, s_, length, cols, True)
        self.two = Attention(slots, s_, length, cols, False)
        wide_rows, acc = VM((heads * QB, cols), BF16), VM((length, cols), F32)
        marked, marked_acc = VM((heads * QB, cols + DH), BF16), VM((length, cols + DH), F32)
        line, tiles = VM((heads, 1, QB), F32), VM((3, heads, QB, QB), F32)
        slots.add(
            s_, bias=tiles, gb=tiles, qm=marked, dm=wide_rows, delta=line,
            oacc=VM((cols, QB), F32), dva=acc, dka=marked_acc, pick=VM((2 * QB, 128), BF16),
        )
        full, own = VM((length, model), BF16), VM((rows, model), F32)
        slots.add(
            self, full_self=full, full_mem=full, full_cross=full, full_ff=full, dy3=full, dy2=full, dy1=full,
            pa=full, pb=full, x_two=own, x_three=own, g=own, dkvq=VM((length, 3 * cols), BF16),
            hidden=VM((length, hid), BF16), cat=VM((length, heads * QB), BF16), dgu=VM((length, 2 * hid), BF16), small=VM((16, model), F32),
        )
        self.gathers = [RowGather(slots, rows) for _ in range(7)]
        self.g_self, self.g_mem, self.g_cross, self.g_ff, self.g_dy3, self.g_dy2, self.g_dy1 = self.gathers
        self.reduces = [RowReduce(slots, rows, model) for _ in range(7)]
        self.r_out1, self.r_out2, self.r_out3, self.r_dn3, self.r_dn2, self.r_mem, self.r_dn1 = self.reduces
        kinds = (
            (4 * cols, (2 * cols, 256, 4 * cols - 2 * cols - 256), 128),
            (4 * cols, (2 * cols, 2 * cols), 384),
            (3 * hid, (768, 3 * hid - 768), 384),
        )
        self.groups = [SimpleNamespace(width=w, parts=p, step=s) for w, p, s in kinds]
        self.ws, self.wc, self.wf = self.groups
        for group in self.groups:
            if zy:
                both = VM((model, group.width), BF16)
                slots.add(group, w=both, gp=both)
                group.gather = WideGather(slots, wrows, group.parts)
                group.reduce = WideReduce(slots, wrows, group.width, group.step)
            else:
                outs.add(group, gp=((model, group.width), BF16))
                group.gather = group.reduce = Idle()
        if zy:
            self.ss = SmallSum(slots, 16, model)

    def blk(self, b):
        return aligned(b * QB, QB)

    def chunk(self, k, block=0):
        size = self.sizes[0] // ROW_CHUNKS
        return aligned(block * self.sizes[0] + k * size, size)

    def far_first(self, i):
        s = self.spot
        far = jnp.where(i < 2, 1 - s.x, s.x)
        return far * 2 + jnp.where(i % 2 == 0, 1 - s.c, s.c)

    def near_tile(self, i):
        s = self.spot
        near = jnp.where(i == 0, s.n, s.sib)
        first = jnp.where(i < 2, 2 * near, 2 * s.xsib + i - 2)
        second = jnp.where(i < 2, 2 * near + 1, 2 * s.xp + i - 2)
        return Tile(i, first, second)

    def near_block(self, i):
        s = self.spot
        far = jnp.where(i < 2, s.x, 1 - s.x)
        return far * 2 + jnp.where(i % 2 == 0, s.c, 1 - s.c)

    def block_tile(self, b):
        return Tile(b, 2 * b, 2 * b + 1)

    def near_waits(self, i, gather):
        @pl.when(i == 1)
        def _():
            gather.have_sib()
            gather.forward(0, 1)

        @pl.when(i == 2)
        def _():
            gather.forward(1, 2)
            gather.have_xsib(0, 2)

        @pl.when(i == 3)
        def _():
            gather.forward(2, 4)
            gather.have_xsib(2, 4)

    def near_sends(self, i, reduce):
        @pl.when(i == 1)
        def _():
            reduce.send_own()

        @pl.when(i == 2)
        def _():
            reduce.send_far(0, 2)
            reduce.cross(0, 2)

        @pl.when(i == 3)
        def _():
            reduce.send_far(2, 4)
            reduce.cross(2, 4)

    def at(self, i, *actions):
        for j, action in enumerate(actions):
            if action is not None:
                pl.when(i == j)(action)

    def pack(self, group, *shards):
        rows = self.sizes[4]
        parts = [ref[...].astype(F32) for ref in shards]
        parts = [p if p.shape[0] == rows else p.T for p in parts]
        group.w[aligned(self.spot.w * rows, rows), :] = jnp.concatenate(parts, axis=1).astype(BF16)

    def ff_tile(self, t):
        f = self.sizes[3]
        step = f // 2
        w = self.wf.w
        x, dy = t.load(self.full_ff), t.load(self.dy3)
        for j in range(0, f, step):
            gate = nn(x, w[:, j : j + step])
            up = nn(x, w[:, f + j : f + j + step])
            dh = nn(dy, w[:, 2 * f + j : 2 * f + j + step])
            value, slope = gelu_parts(gate)
            t.store(self.hidden, (value * up).astype(BF16), j)
            t.store(self.dgu, (dh * up * slope).astype(BF16), j)
            t.store(self.dgu, (dh * value).astype(BF16), f + j)
        t.store(self.pa, nt(t.load(self.dgu), w[:, : 2 * f]).astype(BF16))

    def grads_kv(self):
        c = self.sizes[2]
        self.dkvq[:, : 2 * c] = jnp.concatenate(
            [self.shared.dka[:, :c], self.shared.dva[...]], axis=1
        ).astype(BF16)

    def norm_backward(self, values, gain, reduce, base, done):
        gain_sum = jnp.zeros((1, self.sizes[1]), F32)
        for k in range(ROW_CHUNKS):
            rows = self.chunk(k)
            add, part = norm_back(values[rows, :].astype(F32), gain, reduce.total(k))
            gain_sum = gain_sum + part
            done(k, rows, base[rows, :].astype(F32) + add)
        return gain_sum

    def run(self):
        rows, model, cols, hid, wrows, length = self.sizes
        zy, heads, s_ = self.zy, self.heads, self.shared
        spot = self.spot = Spot(zy)
        one, two = self.one, self.two
        ws, wc, wf = self.groups
        greet(spot, zy)
        for gather, full in zip(
            self.gathers, (self.full_self, self.full_mem, self.full_cross, self.full_ff, self.dy3, self.dy2, self.dy1)
        ):
            gather.bind(spot, full)
        for reduce, part in zip(
            self.reduces, (self.pa, self.pb, self.pb, self.pa, self.pa, self.dgu, self.pa)
        ):
            reduce.bind(spot, part)
        column = 0
        for group in self.groups:
            group.gather.bind(spot, group.w)
            group.reduce.bind(spot, group.gp, self.red if zy else None, column)
            column += group.width
        width = heads * QB
        one.bind(ws.w, self.full_mem, self.cat)
        two.bind(wc.w, self.dgu.at[:, :width], self.cat)
        gain_s, gain_c, gain_f = (ref[...].reshape(1, model) for ref in (self.gain_s, self.gain_c, self.gain_f))

        if zy:
            self.ss.bind(spot)
            self.pack(ws, self.sk, self.sv, self.sq, self.so)
        ws.gather.open_z()
        ws.gather.open_y()
        for k in range(ROW_CHUNKS):
            x = self.x[self.chunk(k), :].astype(F32)
            self.full_self[self.chunk(k, spot.n), :] = norm_rows(x, gain_s).astype(BF16)
            self.g_self.send(k)
        self.full_mem[self.blk(spot.n), :] = self.m[...]
        self.g_mem.send_all()
        self.dy3[self.blk(spot.n), :] = self.cot[...]
        self.g_dy3.send_all(0, 2)
        if zy:
            self.pack(wc, self.ck, self.cv, self.cq, self.co)
            self.pack(wf, self.fg, self.fu, self.fd)
        ranges = bucket_ranges(2 * QB)
        document_columns((one.q, two.q), one.k, self.sid, cols)
        make_bias(s_, self.table, heads, ranges)
        ws.gather.forward(1, 0)
        ws.gather.forward(2, 0)
        self.g_self.forward(0, 2)
        ws.gather.forward(3, 0)
        ws.gather.forward(1, 1)
        self.g_self.forward(2, 4)
        ws.gather.forward(2, 1)
        ws.gather.forward(3, 1)
        self.g_self.have_sib()
        self.g_self.have_xsib(0, 4)
        ws.gather.have(0)
        wc.gather.open_z()

        one.project_kv(self.full_self)
        for distance in (1, 2, 3):
            ws.gather.forward(distance, 2)
        wc.gather.open_y()
        ws.gather.have(1, 2)

        def self_block(i, carry):
            b = self.far_first(i)
            t = self.block_tile(b)
            one.project_q(self.full_self, t)
            one.forward(t)
            one.out_part(self.pa, t)

            def after_first():
                self.r_out1.send_far()
                wc.gather.forward(1)
                wf.gather.open_z()
                wc.gather.forward(2, 0)

            def after_second():
                self.r_out1.cross()
                self.g_mem.forward(0, 4)
                wc.gather.forward(3, 0)
                wc.gather.forward(2, 1)

            def after_third():
                self.r_out1.send_own()
                wc.gather.forward(3, 1)
                wf.gather.open_y()

            self.at(i, after_first, after_second, after_third)
            return carry

        lax.fori_loop(0, 4, self_block, 0)
        document_columns(None, two.k, self.mid, cols)
        self.g_mem.have_sib()
        self.g_mem.have_xsib(0, 4)
        wc.gather.have()
        two.project_kv(self.full_mem)
        self.g_dy3.forward(0, 2)
        for k in range(ROW_CHUNKS):
            value = self.x[self.chunk(k), :].astype(F32) + self.r_out1.total(k)
            self.x_two[self.chunk(k), :] = value
            self.full_cross[self.chunk(k, spot.n), :] = norm_rows(value, gain_c).astype(BF16)
            self.g_cross.send(k)
        self.g_dy3.send_all(2, 4)
        wf.gather.forward(1, 0)

        def cross_block(i, carry):
            t = self.near_tile(i)
            self.near_waits(i, self.g_cross)
            two.project_q(self.full_cross, t)
            two.forward(t)
            two.out_part(self.pb, t)
            self.near_sends(i, self.r_out2)
            self.at(i, lambda: [wf.gather.forward(2, 0)] and None, lambda: [wf.gather.forward(3, 0), wf.gather.forward(1, 1)] and None, lambda: [wf.gather.forward(2, 1), wf.gather.forward(3, 1)] and None)
            return carry

        lax.fori_loop(0, 4, cross_block, 0)
        self.g_dy3.forward(2, 4)
        for k in range(ROW_CHUNKS):
            value = self.x_two[self.chunk(k), :] + self.r_out2.total(k)
            self.x_three[self.chunk(k), :] = value
            self.full_ff[self.chunk(k, spot.n), :] = norm_rows(value, gain_f).astype(BF16)
            self.g_ff.send(k)
        self.r_out1.finish()
        self.r_out2.finish()
        self.g_dy3.have_sib()
        self.g_dy3.have_xsib(0, 4)
        wf.gather.have()

        def ff_step(i, carry):
            self.near_waits(i, self.g_ff)
            self.ff_tile(self.near_tile(i))
            self.near_sends(i, self.r_dn3)
            return carry

        lax.fori_loop(0, 4, ff_step, 0)
        weight_grad(wf.gp, 0, self.full_ff, self.dgu, 0, 2 * hid)
        split = wf.reduce.chunks * 2 // 3
        for c in range(split):
            wf.reduce.open(c)

        def ff_out(b, carry):
            self.pb[self.blk(b), :] = nt(self.hidden[self.blk(b), :], wf.w[:, 2 * hid :]).astype(BF16)
            return carry

        lax.fori_loop(0, 4, ff_out, 0)
        self.r_out3.send_far()
        self.r_out3.send_own()
        weight_grad(wf.gp, 2 * hid, self.dy3, self.hidden, 0, hid)
        for c in range(split, wf.reduce.chunks):
            wf.reduce.open(c)

        def back_three(k, at, value):
            self.g[at, :] = value
            self.dy2[self.chunk(k, spot.n), :] = value.astype(BF16)
            self.g_dy2.send(k)

        gain_ff = self.norm_backward(self.x_three, gain_f, self.r_dn3, self.cot, back_three)
        self.small[14:15, :] = gain_ff
        self.r_out3.cross(0, 2)

        self.r_dn3.finish()
        s_.dka[...] = jnp.zeros_like(s_.dka)
        s_.dva[...] = jnp.zeros_like(s_.dva)

        def cross_back(i, carry):
            t = self.near_tile(i)
            self.near_waits(i, self.g_dy2)
            dctx = nn(t.load(self.dy2), two.wcols(3, 1)).astype(BF16)
            dq = two.backward(t, dctx)
            t.store(self.dkvq, dq, 2 * cols)
            t.store(self.pa, nt(dq, two.wcols(2, 1)).astype(BF16))
            self.near_sends(i, self.r_dn2)
            if zy:
                self.at(i, lambda: wf.reduce.first(0), lambda: wf.reduce.first(1), None, lambda: wf.reduce.first(2))
            return carry

        lax.fori_loop(0, 4, cross_back, 0)
        self.grads_kv()

        def memory_part(b, carry):
            blk = self.blk(b)
            self.dgu[blk, 0:model] = nt(self.dkvq[blk, : 2 * cols], two.wcols(0, 2)).astype(BF16)
            return carry

        lax.fori_loop(0, 4, memory_part, 0)
        self.r_mem.send_far()
        self.r_mem.send_own()
        if zy:
            wf.reduce.first(3)

        def back_two(k, at, value):
            self.g[at, :] = value
            self.dy1[self.chunk(k, spot.n), :] = value.astype(BF16)
            self.g_dy1.send(k)

        gain_cross = self.norm_backward(self.x_two, gain_c, self.r_dn2, self.g, back_two)
        self.small[13:14, :] = gain_cross
        self.r_out3.cross(2, 4)
        self.r_mem.cross()
        weight_grad(wc.gp, 0, self.full_mem, self.dkvq, 0, 2 * cols)
        wc.reduce.open(0)
        weight_grad(wc.gp, 2 * cols, self.full_cross, self.dkvq, 2 * cols, cols)
        weight_grad(wc.gp, 3 * cols, self.dy2, two.ctx, 0, cols)
        wc.reduce.open(1)

        self.g_mem.finish()
        s_.dka[...] = jnp.zeros_like(s_.dka)
        s_.dva[...] = jnp.zeros_like(s_.dva)

        def self_waits(i):
            @pl.when(i == 1)
            def _():
                self.g_dy1.have_sib()
                self.g_dy1.forward(0, 1)

            @pl.when(i == 2)
            def _():
                self.g_dy1.forward(1, 4)

            @pl.when(i == 3)
            def _():
                self.g_dy1.have_xsib(0, 4)

        def self_back(i, carry):
            b = self.near_block(i)
            t = self.block_tile(b)
            self_waits(i)
            dctx = nn(t.load(self.dy1), one.wcols(3, 1)).astype(BF16)
            t.store(self.dkvq, one.backward(t, dctx), 2 * cols)

            def ff_totals():
                for c in range(wf.reduce.chunks):
                    wf.reduce.total(c)

            self.at(i, lambda: wc.reduce.first(0), ff_totals, lambda: wc.reduce.first(1))
            return carry

        lax.fori_loop(0, 4, self_back, 0)
        self.grads_kv()
        self.r_dn2.finish()

        def last_part(i, carry):
            blk = self.blk(self.far_first(i))
            self.pa[blk, :] = nt(self.dkvq[blk, :], one.wcols(0, 3)).astype(BF16)
            return carry

        lax.fori_loop(0, 2, last_part, 0)
        self.r_dn1.send_far()
        weight_grad(ws.gp, 0, self.full_self, self.dkvq, 0, 3 * cols)
        weight_grad(ws.gp, 3 * cols, self.dy1, one.ctx, 0, cols)
        for c in range(ws.reduce.chunks):
            ws.reduce.open(c)
        self.r_dn1.cross()
        lax.fori_loop(2, 4, last_part, 0)
        self.r_dn1.send_own()

        def gain_part(b, total):
            blk = self.blk(b)
            both = self.full_self[blk, :].astype(F32) * self.pa[blk, :].astype(F32)
            return total + jnp.sum(both, axis=0, keepdims=True)

        gain_self = lax.fori_loop(0, 4, gain_part, jnp.zeros((1, model), F32)) / gain_s
        keep = self.small[13:15, :]
        self.small[...] = jnp.zeros_like(self.small)
        self.small[:, 0:128] = table_rows(s_, heads, spot.n)
        self.small[12:13, :] = gain_self
        self.small[13:15, :] = keep
        if zy:
            self.ss.begin(self.small[...])
        else:
            self.tot[...] = self.small[...]
        for k in range(ROW_CHUNKS):
            value = self.x_three[self.chunk(k), :] + self.r_out3.total(k)
            self.result[self.chunk(k), :] = value.astype(BF16)
        if zy:
            self.ss.step(0)
            ws.reduce.first(0)
            ws.reduce.first(1)
        for k in range(ROW_CHUNKS):
            self.gm[self.chunk(k), :] = self.r_mem.total(k).astype(BF16)
        for c in range(wc.reduce.chunks):
            wc.reduce.total(c)
        if zy:
            ws.reduce.first(2)

        def back_one(k, at, value):
            self.gx[at, :] = value.astype(BF16)
            if zy and k == 1:
                ws.reduce.first(3)
            if zy and k == 3:
                self.ss.step(1)

        self.norm_backward(self.x, gain_s, self.r_dn1, self.g, back_one)
        if zy:
            ws.reduce.first(4)
            self.ss.step(2)
            ws.reduce.first(5)
            for c in range(ws.reduce.chunks):
                ws.reduce.total(c)
            self.ss.end(self.tot)

        for gather in self.gathers:
            if gather is not self.g_mem:
                gather.finish()
        for reduce in (self.r_out3, self.r_mem, self.r_dn1):
            reduce.finish()
        for group in self.groups:
            group.gather.finish()
            group.reduce.finish()


def deliver(red, tot, passed, sizes, heads):
    rows, model, cols, hid, wrows, length = sizes
    ins, outs = Slots(), Slots()
    packed, small = SimpleNamespace(), SimpleNamespace()
    ins.add(packed, ref=(red, VM))
    ins.add(small, ref=(tot, VM))
    sources, dests = [SimpleNamespace() for _ in passed], [SimpleNamespace() for _ in passed]
    for value, source, dest in zip(passed, sources, dests):
        ins.add(source, ref=(value, VM))
        outs.add(dest, ref=(value.shape, value.dtype))
    places = [(i * cols, cols, i % 4 == 3) for i in (2, 0, 1, 3, 6, 4, 5, 7)]
    places += [(8 * cols + i * hid, hid, False) for i in range(3)]
    cuts = []
    for at, width, turn in places:
        cut = SimpleNamespace(at=at, width=width, turn=turn)
        outs.add(cut, ref=((width, wrows) if turn else (wrows, width), F32))
        cuts.append(cut)
    gains, table = [SimpleNamespace() for _ in range(3)], SimpleNamespace()
    for gain in gains:
        outs.add(gain, ref=((model,), F32))
    outs.add(table, ref=((4 * heads, NB), F32))

    def body():
        for source, dest in zip(sources, dests):
            dest.ref[...] = source.ref[...]
        for cut in cuts:
            part = packed.ref[:, cut.at : cut.at + cut.width]
            cut.ref[...] = part.T if cut.turn else part
        for i, gain in enumerate(gains):
            gain.ref[...] = small.ref[12 + i : 13 + i, :].reshape(model)
        table.ref[...] = small.ref[0 : 4 * heads, 0:NB]

    got = run_kernel(body, ins, outs, Slots(), None, "deliver")
    return got[:3], got[3:14], got[14:17], got[17]


def shards(
    zy, inputs, memory, segment_ids, memory_ids, self_gain, self_query, self_key, self_value, self_out, bias_table,
    cross_gain, cross_query, cross_key, cross_value, cross_out, ff_gain, ff_gate, ff_up, ff_down, cotangent,
):
    rows, model = inputs.shape
    length = segment_ids.shape[1]
    wrows, cols = self_query.shape
    hid = ff_gate.shape[1]
    heads = cols // DH
    assert segment_ids.shape[0] == 1 and rows == QB and length == 4 * QB == memory_ids.shape[1]
    sizes = (rows, model, cols, hid, wrows, length)
    ins, outs, slots = Slots(), Slots(), Slots()
    layer = Layer.__new__(Layer)
    outs.add(
        layer, result=((rows, model), BF16), gx=((rows, model), BF16), gm=((rows, model), BF16), tot=((16, model), F32)
    )
    if zy:
        outs.add(layer, red=((wrows, 8 * cols + 3 * hid), F32))
    layer.__init__(zy, sizes, ins, outs, slots)
    ins.add(
        layer, x=(inputs, VM), m=(memory, VM), cot=(cotangent, VM), sid=(segment_ids, VM), mid=(memory_ids, VM),
        gain_s=(self_gain, VM), gain_c=(cross_gain, VM), gain_f=(ff_gain, VM), table=(bias_table.T, pltpu.SMEM),
    )
    if zy:
        ins.add(
            layer, sq=(self_query, VM), sk=(self_key, VM), sv=(self_value, VM), so=(self_out, VM),
            cq=(cross_query, VM), ck=(cross_key, VM), cv=(cross_value, VM), co=(cross_out, VM),
            fg=(ff_gate, VM), fu=(ff_up, VM), fd=(ff_down.T, VM),
        )
    else:

        def whole(*parts):
            return lax.all_gather(jnp.concatenate(parts, axis=1), WIDE, axis=0, tiled=True)

        ins.add(layer.ws, w=(whole(self_key, self_value, self_query, self_out.T), VM))
        ins.add(layer.wc, w=(whole(cross_key, cross_value, cross_query, cross_out.T), VM))
        ins.add(layer.wf, w=(whole(ff_gate, ff_up, ff_down.T), VM))
    got = run_kernel(layer.run, ins, outs, slots, 0, "layer")
    if zy:
        total, red = got[3], got[4]
    else:
        packed = jnp.concatenate(got[4:7], axis=1)
        red = lax.psum_scatter(packed, WIDE, scatter_dimension=0, tiled=True).astype(F32)
        total = lax.psum(got[3], (WIDE, NARROW))
    row_outs, grads, gains, table = deliver(red, total, got[:3], sizes, heads)
    return (
        *row_outs,
        gains[0],
        *grads[0:4],
        table.T,
        gains[1],
        *grads[4:8],
        gains[2],
        grads[8],
        grads[9],
        grads[10].T,
    )


def solution(mesh):
    zy = mesh.shape[WIDE] == 8
    rows = P((WIDE, NARROW), None)
    w_in, w_out = P(WIDE, NARROW), P(NARROW, WIDE)
    placed = (
        rows, rows, P(WIDE, None), P(WIDE, None), P(),
        w_in, w_in, w_in, w_out, P(None, NARROW), P(),
        w_in, w_in, w_in, w_out, P(), w_in, w_in, w_out, rows,
    )
    outs = (
        rows, rows, rows, P(), w_in, w_in, w_in, w_out, P(), P(),
        w_in, w_in, w_in, w_out, P(), w_in, w_in, w_out,
    )

    def program(*args):
        return shards(zy, *args)

    return jax.shard_map(program, mesh=mesh, in_specs=placed, out_specs=outs, check_vma=False)
```

```python
import math
from types import SimpleNamespace

import jax
import jax.numpy as jnp
import numpy as np
from jax import lax
from jax.experimental import pallas as pl
from jax.experimental.pallas import tpu as pltpu
from jax.sharding import PartitionSpec as P

DH = 64
NB = 32
MAX_DIST = 128
EPS = 1e-06
NEG = -1e30
QB = 256
HALF = 128
ROW_CHUNKS = 4
WIDE = "wide"
NARROW = "narrow"
MESH = pl.DeviceIdType.MESH
F32 = jnp.float32
BF16 = jnp.bfloat16
VM = pltpu.VMEM
DMA = pltpu.SemaphoreType.DMA


def bucket_table(length, buckets, reach):
    exact_part = buckets // 2
    distance = np.arange(length)
    spread = (
        np.log(np.maximum(distance, exact_part) / exact_part)
        / np.log(reach / exact_part)
        * (buckets - exact_part)
    )
    far_bucket = np.minimum(exact_part + np.floor(spread).astype(np.int64), buckets - 1)
    return np.where(distance < exact_part, distance, far_bucket).astype(np.int32)


def bucket_ranges(length):
    table = bucket_table(length, NB, MAX_DIST)
    found = []
    for which in range(NB):
        places = np.nonzero(table == which)[0]
        if len(places):
            found.append((which, int(places[0]), int(places[-1]) + 1))
    return found


class Slots:
    def __init__(self):
        self.items = []

    def add(self, holder, **specs):
        for name, spec in specs.items():
            self.items.append((holder, name, spec))

    def fill(self, refs):
        for (holder, name, _), ref in zip(self.items, refs):
            setattr(holder, name, ref)


def run_kernel(body, ins, outs, scratch, cid, name):
    counts = len(ins.items), len(outs.items)

    def kernel(*refs):
        ins.fill(refs[: counts[0]])
        outs.fill(refs[counts[0] : counts[0] + counts[1]])
        scratch.fill(refs[counts[0] + counts[1] :])
        body()

    params = {} if cid is None else dict(collective_id=cid, has_side_effects=True)
    return pl.pallas_call(
        kernel,
        out_shape=[jax.ShapeDtypeStruct(*spec) for _, _, spec in outs.items],
        in_specs=[pl.BlockSpec(memory_space=spec[1]) for _, _, spec in ins.items],
        out_specs=[pl.BlockSpec(memory_space=VM) for _ in outs.items],
        scratch_shapes=[spec for _, _, spec in scratch.items],
        compiler_params=pltpu.CompilerParams(vmem_limit_bytes=66_900_000, **params),
        name=name,
    )(*[spec[0] for _, _, spec in ins.items])


class Spot:
    def __init__(self, wide_split):
        n = lax.axis_index(NARROW)
        self.n = n
        self.x = n // 2
        self.c = n % 2
        self.sib = self.x * 2 + (1 - self.c)
        self.xp = (1 - self.x) * 2 + self.c
        self.xsib = (1 - self.x) * 2 + (1 - self.c)
        if wide_split:
            w = lax.axis_index(WIDE)
            self.w = w
            self.z = w // 2
            self.y = w % 2
            self.yp = self.z * 2 + (1 - self.y)

    def at_n(self, n):
        return {NARROW: n}

    def at_w(self, w):
        return {WIDE: w}

    def at_z(self, z):
        return {WIDE: z * 2 + self.y}


def remote(src, dst, send, recv, dev):
    return pltpu.make_async_remote_copy(
        src_ref=src, dst_ref=dst, send_sem=send, recv_sem=recv, device_id=dev, device_id_type=MESH
    )


def greet(spot, zy):
    barrier = pltpu.get_barrier_semaphore()

    def hello(dev):
        pl.semaphore_signal(barrier, inc=1, device_id=dev, device_id_type=MESH)

    hello(spot.at_n(spot.sib))
    hello(spot.at_n(spot.xp))
    if zy:
        hello(spot.at_w(spot.yp))
        for step in range(1, 4):
            hello(spot.at_z((spot.z + step) % 4))
    pl.semaphore_wait(barrier, 6 if zy else 2)


def aligned(start, size):
    return pl.ds(pl.multiple_of(start, 16), size)


class RowGather:
    def __init__(self, slots, rows, chunks=ROW_CHUNKS):
        self.nrows, self.chunks, self.size = rows, chunks, rows // chunks
        sems = DMA((chunks,))
        slots.add(self, xs=sems, xr=sems, ss=sems, sr=sems, fs=sems, fr=sems)

    def bind(self, spot, full):
        self.spot, self.full = spot, full

    def hop(self, k, block, dev, send, recv):
        rows = self.full.at[aligned(block * self.nrows + k * self.size, self.size)]
        return remote(rows, rows, send.at[k], recv.at[k], self.spot.at_n(dev))

    def to_x(self, k):
        return self.hop(k, self.spot.n, self.spot.xp, self.xs, self.xr)

    def from_x(self, k):
        return self.hop(k, self.spot.xp, self.spot.xp, self.xs, self.xr)

    def to_sib(self, k):
        return self.hop(k, self.spot.n, self.spot.sib, self.ss, self.sr)

    def from_sib(self, k):
        return self.hop(k, self.spot.sib, self.spot.sib, self.ss, self.sr)

    def onward(self, k):
        return self.hop(k, self.spot.xp, self.spot.sib, self.fs, self.fr)

    def from_onward(self, k):
        return self.hop(k, self.spot.xsib, self.spot.sib, self.fs, self.fr)

    def send(self, k):
        self.to_x(k).start()
        self.to_sib(k).start()

    def send_all(self, first=0, after=ROW_CHUNKS):
        for k in range(first, after):
            self.send(k)

    def forward(self, first, after):
        for k in range(first, after):
            self.from_x(k).wait_recv()
            self.onward(k).start()

    def have_sib(self):
        for k in range(self.chunks):
            self.from_sib(k).wait_recv()

    def have_xsib(self, first, after):
        for k in range(first, after):
            self.from_onward(k).wait_recv()

    def finish(self):
        for k in range(self.chunks):
            self.to_x(k).wait_send()
            self.to_sib(k).wait_send()
            self.onward(k).wait_send()


class RowReduce:
    def __init__(self, slots, rows, cols, chunks=ROW_CHUNKS):
        self.nrows, self.ncols, self.chunks, self.size = rows, cols, chunks, rows // chunks
        sems, buf = DMA((chunks,)), VM((rows, cols), BF16)
        slots.add(self, as_=sems, ar=sems, bs=sems, br=sems, xs=sems, xr=sems, far=buf, own=buf, inn=buf)

    def bind(self, spot, part):
        self.spot, self.part = spot, part

    def buf(self, ref, k):
        return ref.at[pl.ds(k * self.size, self.size)]

    def mine(self, block, k):
        return self.part.at[aligned(block * self.nrows + k * self.size, self.size), pl.ds(0, self.ncols)]

    def far_sib(self, k):
        s = self.spot
        return remote(self.mine(s.xsib, k), self.buf(self.far, k), self.as_.at[k], self.ar.at[k], s.at_n(s.sib))

    def own_sib(self, k):
        s = self.spot
        return remote(self.mine(s.sib, k), self.buf(self.own, k), self.bs.at[k], self.br.at[k], s.at_n(s.sib))

    def across(self, k):
        s = self.spot
        return remote(self.buf(self.far, k), self.buf(self.inn, k), self.xs.at[k], self.xr.at[k], s.at_n(s.xp))

    def send_far(self, first=0, after=ROW_CHUNKS):
        for k in range(first, after):
            self.far_sib(k).start()

    def send_own(self):
        for k in range(self.chunks):
            self.own_sib(k).start()

    def cross(self, first=0, after=ROW_CHUNKS):
        for k in range(first, after):
            self.far_sib(k).wait_recv()
            here = self.buf(self.far, k)
            here[...] = (self.mine(self.spot.xp, k)[...].astype(F32) + here[...].astype(F32)).astype(BF16)
            self.across(k).start()

    def total(self, k):
        self.own_sib(k).wait_recv()
        self.across(k).wait_recv()
        value = self.mine(self.spot.n, k)[...].astype(F32) + self.buf(self.own, k)[...].astype(F32)
        return value + self.buf(self.inn, k)[...].astype(F32)

    def finish(self):
        for k in range(self.chunks):
            self.far_sib(k).wait_send()
            self.own_sib(k).wait_send()
            self.across(k).wait_send()


class WideGather:
    steps = (1, -1, 2, -2, 3, -3)

    def __init__(self, slots, rows, widths):
        self.nrows, self.widths, self.parts = rows, widths, range(len(widths))
        four = DMA((4, len(widths)))
        slots.add(self, zs=DMA((6, len(widths))), zr=four, ys=four, yr=four)

    def bind(self, spot, full):
        self.spot, self.full = spot, full

    def rows(self, z, y, part):
        cols = pl.ds(sum(self.widths[:part]), self.widths[part])
        return self.full.at[aligned((z * 2 + y) * self.nrows, self.nrows), cols]

    def along(self, i, part):
        s = self.spot
        rows = self.rows(s.z, s.y, part)
        return remote(rows, rows, self.zs.at[i, part], self.zr.at[s.z, part], s.at_z(s.z + self.steps[i]))

    def came(self, z, part):
        s = self.spot
        rows = self.rows(z, s.y, part)
        return remote(rows, rows, self.zs.at[0, part], self.zr.at[z, part], s.at_z(z))

    def over(self, z, part):
        s = self.spot
        rows = self.rows(z, s.y, part)
        return remote(rows, rows, self.ys.at[z, part], self.yr.at[z, part], s.at_w(s.yp))

    def crossed(self, z, part):
        s = self.spot
        rows = self.rows(z, 1 - s.y, part)
        return remote(rows, rows, self.ys.at[z, part], self.yr.at[z, part], s.at_w(s.yp))

    def when_inside(self, step, fn):
        there = self.spot.z + step

        @pl.when(there >= 0 if step < 0 else there <= 3)
        def _():
            fn(there)

    def open_y(self):
        for part in self.parts:
            self.over(self.spot.z, part).start()

    def open_z(self):
        for part in self.parts:
            for i, step in enumerate(self.steps):
                self.when_inside(step, lambda there: self.along(i, part).start())

    def forward(self, distance, *parts):
        for part in parts or self.parts:
            for step in (distance, -distance):

                def pass_on(there):
                    self.came(there, part).wait_recv()
                    self.over(there, part).start()

                self.when_inside(step, pass_on)

    def have(self, *parts):
        for part in parts or self.parts:
            for z in range(4):
                self.crossed(z, part).wait_recv()

    def finish(self):
        for part in self.parts:
            for z in range(4):
                self.over(z, part).wait_send()
            for i, step in enumerate(self.steps):
                self.when_inside(step, lambda there: self.along(i, part).wait_send())


class WideReduce:
    steps = (2, 3, 1, 0)

    def __init__(self, slots, rows, cols, width):
        self.nrows, self.width, self.chunks = rows, width, cols // width
        sems, buf = DMA((self.chunks, 4)), VM((4, rows, cols), BF16)
        slots.add(self, ys=sems, yr=sems, zs=sems, zr=sems, acc=buf, inn=buf)

    def bind(self, spot, part, out, out_col):
        self.spot, self.part, self.out, self.out_col = spot, part, out, out_col

    def cols(self, c):
        return pl.ds(c * self.width, self.width)

    def slab(self, c, z, y):
        return self.part.at[aligned((z * 2 + y) * self.nrows, self.nrows), self.cols(c)]

    def over(self, c, z):
        s = self.spot
        return remote(
            self.slab(c, z, 1 - s.y), self.acc.at[z, :, self.cols(c)], self.ys.at[c, z], self.yr.at[c, z], s.at_w(s.yp)
        )

    def along(self, c, z):
        s = self.spot
        return remote(
            self.acc.at[z, :, self.cols(c)], self.inn.at[s.z, :, self.cols(c)],
            self.zs.at[c, z], self.zr.at[c, s.z], s.at_z(z),
        )

    def came(self, c, z):
        here = self.inn.at[z, :, self.cols(c)]
        return remote(here, here, self.zs.at[c, z], self.zr.at[c, z], self.spot.at_z(z))

    def targets(self):
        return [(self.spot.z + step) % 4 for step in self.steps]

    def open(self, c):
        for z in self.targets():
            self.over(c, z).start()

    def first(self, c):
        for step, z in zip(self.steps, self.targets()):
            self.over(c, z).wait_recv()
            here = self.acc.at[z, :, self.cols(c)]
            here[...] = (self.slab(c, z, self.spot.y)[...].astype(F32) + here[...].astype(F32)).astype(BF16)
            if step:
                self.along(c, z).start()

    def total(self, c):
        value = self.acc[self.spot.z, :, self.cols(c)].astype(F32)
        for z in self.targets()[:3]:
            self.came(c, z).wait_recv()
            value = value + self.inn[z, :, self.cols(c)].astype(F32)
        self.out[:, pl.ds(self.out_col + c * self.width, self.width)] = value

    def finish(self):
        for c in range(self.chunks):
            for step, z in zip(self.steps, self.targets()):
                self.over(c, z).wait_send()
                if step:
                    self.along(c, z).wait_send()


class SmallSum:
    def __init__(self, slots, rows, cols):
        four = VM((4, rows, cols), F32)
        slots.add(
            self, ps=DMA((3,)), pr=DMA((3,)), zs=DMA((4,)), zr=DMA((4,)), held=four, inn=VM((3, rows, cols), F32), zin=four
        )

    def bind(self, spot):
        self.spot = spot

    def pair(self, i):
        s = self.spot
        source, dev = ((0, s.at_n(s.sib)), (2, s.at_n(s.xp)), (3, s.at_w(s.yp)))[i]
        return remote(self.held.at[source], self.inn.at[i], self.ps.at[i], self.pr.at[i], dev)

    def hop(self, step, landed):
        other = (self.spot.z + step) % 4
        return remote(
            self.held.at[1], self.zin.at[landed], self.zs.at[step], self.zr.at[landed], self.spot.at_z(other)
        )

    def begin(self, value):
        self.held[0] = value
        self.pair(0).start()

    def to_z(self):
        self.pair(0).wait_recv()
        self.held[1] = self.held[0] + self.inn[0]
        self.zin[self.spot.z] = self.held[1]
        for step in range(1, 4):
            self.hop(step, self.spot.z).start()

    def to_x(self):
        for step in range(1, 4):
            self.hop(step, (self.spot.z + step) % 4).wait_recv()
        self.held[2] = ((self.zin[0] + self.zin[1]) + self.zin[2]) + self.zin[3]
        self.pair(1).start()

    def to_y(self):
        self.pair(1).wait_recv()
        self.held[3] = self.held[2] + self.inn[1]
        self.pair(2).start()

    def end(self, out):
        self.pair(2).wait_recv()
        out[...] = self.held[3] + self.inn[2]
        for i in range(3):
            self.pair(i).wait_send()
        for step in range(1, 4):
            self.hop(step, self.spot.z).wait_send()


class Idle:
    chunks = 0

    def bind(self, *args):
        pass

    open = open_y = open_z = forward = have = finish = first = total = bind


def nt(left, right):
    return lax.dot_general(left, right, (((1,), (1,)), ((), ())), preferred_element_type=F32)


def nn(left, right):
    return lax.dot_general(left, right, (((1,), (0,)), ((), ())), preferred_element_type=F32)


def tn(left, right):
    return lax.dot_general(left, right, (((0,), (0,)), ((), ())), preferred_element_type=F32)


def mean_square(values):
    return jnp.mean(values * values, axis=-1, keepdims=True)


def norm_rows(values, gain):
    return values * lax.rsqrt(mean_square(values) + EPS) * gain


def norm_back(values, gain, dn):
    r = lax.rsqrt(mean_square(values) + EPS)
    u = values * r
    dg = dn * gain
    rows = r * (dg - u * jnp.mean(dg * u, axis=-1, keepdims=True))
    return rows, jnp.sum(dn * u, axis=0, keepdims=True)


def gelu_parts(v):
    c = math.sqrt(2.0 / math.pi)
    t = jnp.tanh(c * (v + 0.044715 * v * v * v))
    value = 0.5 * v * (1.0 + t)
    slope = 0.5 * (1.0 + t) + 0.5 * v * (1.0 - t * t) * c * (1.0 + 3.0 * 0.044715 * v * v)
    return value, slope


def head_rows(values, h, heads):
    lane = lax.broadcasted_iota(jnp.int32, values.shape, 1) // DH
    return jnp.where(jnp.logical_or(lane == h, lane >= heads), values, jnp.zeros_like(values))


def document_columns(query_ref, key_ref, ids, first):
    column = jnp.broadcast_to(ids[...].astype(F32), (128, ids.shape[1])).T[:, :DH]
    lane = lax.broadcasted_iota(jnp.int32, column.shape, 1)
    same = column == lane.astype(F32)
    if query_ref is not None:
        for ref in query_ref:
            ref[:, first : first + DH] = jnp.where(same, 1.0, 0.0).astype(BF16)
    if key_ref is not None:
        other = jnp.logical_and(jnp.logical_not(same), lane < 4)
        key_ref[:, first : first + DH] = jnp.where(other, NEG, 0.0).astype(BF16)


def diagonal_sums(tile):
    rows, width = tile.shape
    while rows > 1:
        rows = rows // 2
        tile = tile[:rows] + pltpu.roll(tile[rows:], width - rows, 1)
    return tile


class Tile:
    def __init__(self, slot, first, second):
        self.slot, self.halves = slot, (first, second)

    def rows(self, half):
        return aligned(half * HALF, HALF)

    def load(self, ref):
        return jnp.concatenate([ref[self.rows(h), :] for h in self.halves], axis=0)

    def store(self, ref, value, at=0):
        for i, h in enumerate(self.halves):
            ref[self.rows(h), at : at + value.shape[1]] = value[i * HALF : (i + 1) * HALF]


class Attention:
    def __init__(self, slots, shared, length, cols, causal):
        self.shared, self.cols, self.heads, self.causal = shared, cols, cols // DH, causal
        rows, marked, turned = VM((length, cols), BF16), VM((length, cols + DH), BF16), VM((4, cols, QB), BF16)
        slots.add(
            self, q=marked, k=marked, v=rows, ctx=rows, kt=turned, vt=turned, lse=VM((4, self.heads, 1, QB), F32)
        )

    def bind(self, weights, pcat, dcat):
        self.w, self.pcat, self.dcat = weights, pcat, dcat

    def blk(self, b):
        return aligned(b * QB, QB)

    def wcols(self, first, count):
        return self.w[:, first * self.cols : (first + count) * self.cols]

    def window(self, t, body):
        if not self.causal:
            body(0, 4)
            return
        for count in (1, 2, 3):
            pl.when(jnp.minimum(t.slot + 1, 3) == count)(lambda: body(t.slot + 1 - count, count))

    def keys(self, first, count):
        return aligned(first * QB, count * QB)

    def score(self, k, h, count):
        s = nt(k, self.shared.qm[self.wide_of(h), :])
        if self.causal:
            s = s + jnp.concatenate([self.shared.bias[self.kind(j, count), h] for j in range(count)], axis=0)
        return s

    def kind(self, j, count):
        return min(count - 1 - j, 2)

    def over_keys(self, turned, first, count, hs, right):
        parts = [nn(turned[first + j, hs, :], right[j * QB : (j + 1) * QB]) for j in range(count)]
        return sum(parts[1:], parts[0])

    def project_kv(self, source):
        c = self.cols

        def one(b, carry):
            kv = nn(source[self.blk(b), :], self.wcols(0, 2))
            k, v = kv[:, :c], kv[:, c:]
            self.k[self.blk(b), :c] = k.astype(BF16)
            self.v[self.blk(b), :] = v.astype(BF16)
            self.kt[b] = k.T.astype(BF16)
            self.vt[b] = v.T.astype(BF16)
            return carry

        lax.fori_loop(0, 4, one, 0)

    def project_q(self, source, t):
        t.store(self.q, nn(t.load(source), self.wcols(2, 1)).astype(BF16))

    def out_part(self, dest, t):
        t.store(dest, nt(t.load(self.ctx), self.wcols(3, 1)).astype(BF16))

    def rows_of(self, h):
        return slice(h * DH, (h + 1) * DH)

    def wide_of(self, h):
        return slice(h * QB, (h + 1) * QB)

    def forward(self, t):
        s_ = self.shared
        q = t.load(self.q)
        for h in range(self.heads):
            s_.qm[self.wide_of(h), :] = head_rows(q, h, self.heads)

        def attend(first, count):
            k = self.k[self.keys(first, count), :]
            for h in range(self.heads):
                hs = self.rows_of(h)
                s = self.score(k, h, count)
                peak = jnp.max(s, axis=0, keepdims=True)
                x = jnp.exp(s - peak)
                total = jnp.sum(x, axis=0, keepdims=True)
                s_.oacc[hs, :] = self.over_keys(self.vt, first, count, hs, x.astype(BF16)) / total
                self.lse[t.slot, h] = peak + jnp.log(total)

        self.window(t, attend)
        t.store(self.ctx, s_.oacc[...].T.astype(BF16))

    def backward(self, t, dctx):
        s_ = self.shared
        q = t.load(self.q)
        prod = (dctx.astype(F32) * t.load(self.ctx).astype(F32)).T
        for h in range(self.heads):
            s_.qm[self.wide_of(h), :] = head_rows(q, h, self.heads)
            s_.dm[self.wide_of(h), :] = head_rows(dctx, h, self.heads)
            s_.delta[h] = jnp.sum(prod[self.rows_of(h), :], axis=0, keepdims=True)

        def attend(first, count):
            keys, span = self.keys(first, count), count * QB
            k, v = self.k[keys, :], self.v[keys, :]
            for h in range(self.heads):
                hs, wide = self.rows_of(h), self.wide_of(h)
                p = jnp.exp(self.score(k, h, count) - self.lse[t.slot, h])
                ds = p * (nt(v, s_.dm[wide, :]) - s_.delta[h])
                if self.causal:
                    for j in range(count):
                        s_.gb[self.kind(j, count), h] += ds[j * QB : (j + 1) * QB]
                low = ds.astype(BF16)
                self.pcat[:span, wide] = p.astype(BF16)
                self.dcat[:span, wide] = low
                s_.oacc[hs, :] = self.over_keys(self.kt, first, count, hs, low)
            s_.dva[keys, :] += nn(self.pcat[:span, :], s_.dm[...])
            s_.dka[keys, :] += nn(self.dcat[:span, :], s_.qm[...])

        self.window(t, attend)
        return s_.oacc[...].T.astype(BF16)


def make_bias(s_, table, heads, ranges):
    lane = lax.broadcasted_iota(jnp.int32, (1, 2 * QB), 1)
    jj = lax.broadcasted_iota(jnp.int32, (QB, QB), 0)
    ii = lax.broadcasted_iota(jnp.int32, (QB, QB), 1)
    for h in range(heads):
        row = jnp.full((1, 2 * QB), table[h, NB - 1])
        for which, start, stop in reversed(ranges[:-1]):
            row = jnp.where(lane < stop, table[h, which], row)
        turned = pltpu.roll(jnp.broadcast_to(row, (QB, 2 * QB)), 0, 1, stride=1, stride_axis=0)
        s_.bias[0, h] = jnp.where(jj <= ii, turned[:, :QB], NEG)
        s_.bias[1, h] = turned[:, QB:]
        s_.bias[2, h] = jnp.full((QB, QB), table[h, NB - 1])
    s_.gb[...] = jnp.zeros_like(s_.gb)
    lane = lax.broadcasted_iota(jnp.int32, (1, 128), 1)
    first = jnp.full((1, 128), 2 * QB, jnp.int32)
    after = jnp.zeros((1, 128), jnp.int32)
    for which, start, stop in ranges:
        first = jnp.where(lane == which, start, first)
        after = jnp.where(lane == which, stop, after)
    dist = lax.broadcasted_iota(jnp.int32, (2 * QB, 128), 0)
    s_.pick[...] = jnp.where(jnp.logical_and(dist >= first, dist < after), 1.0, 0.0).astype(BF16)


def table_rows(s_, heads, n):
    near = [diagonal_sums(jnp.concatenate([s_.gb[0, h], s_.gb[1, h]], axis=1)) for h in range(heads)]
    near = jnp.concatenate(near + [jnp.zeros((8 - heads, 2 * QB), F32)], axis=0)
    sums = jnp.zeros((8, 128), F32)
    for _ in range(3):
        term = near.astype(BF16)
        sums = sums + nn(term, s_.pick[...])
        near = near - term.astype(F32)
    lane = lax.broadcasted_iota(jnp.int32, (1, 128), 1)
    place = lax.broadcasted_iota(jnp.int32, (16, 128), 0)
    rows = jnp.zeros((16, 128), F32)
    for h in range(heads):
        far = jnp.sum(jnp.sum(s_.gb[2, h], axis=0, keepdims=True), axis=1, keepdims=True)
        line = sums[h : h + 1, :] + jnp.where(lane == NB - 1, far, 0.0)
        rows = jnp.where(place == n * heads + h, jnp.broadcast_to(line, (16, 128)), rows)
    return rows


def weight_grad(dest, column, left, right, first, width):
    def one(m, carry):
        part = pl.ds(pl.multiple_of(m * 256, 256), 256)
        dest[part, column : column + width] = tn(left[:, part], right[:, first : first + width]).astype(BF16)
        return carry

    lax.fori_loop(0, left.shape[1] // 256, one, 0)


class Layer:
    def __init__(self, zy, sizes, ins, outs, slots):
        self.zy, self.sizes = zy, sizes
        rows, model, cols, hid, wrows, length = sizes
        heads = cols // DH
        self.heads = heads
        s_ = self.shared = SimpleNamespace()
        self.one = Attention(slots, s_, length, cols, True)
        self.two = Attention(slots, s_, length, cols, False)
        wide_rows, acc = VM((heads * QB, cols), BF16), VM((length, cols), F32)
        marked, marked_acc = VM((heads * QB, cols + DH), BF16), VM((length, cols + DH), F32)
        line, tiles = VM((heads, 1, QB), F32), VM((3, heads, QB, QB), F32)
        slots.add(
            s_, bias=tiles, gb=tiles, qm=marked, dm=wide_rows, delta=line,
            oacc=VM((cols, QB), F32), dva=acc, dka=marked_acc, pick=VM((2 * QB, 128), BF16),
        )
        full, own = VM((length, model), BF16), VM((rows, model), F32)
        slots.add(
            self, full_self=full, full_mem=full, full_cross=full, full_ff=full, dy3=full, dy2=full, dy1=full,
            pa=full, pb=full, x_two=own, x_three=own, g=own, dkvq=VM((length, 3 * cols), BF16),
            hidden=VM((length, hid), BF16), cat=VM((length, heads * QB), BF16), dgu=VM((length, 2 * hid), BF16), small=VM((16, model), F32),
        )
        self.gathers = [RowGather(slots, rows) for _ in range(7)]
        self.g_self, self.g_mem, self.g_cross, self.g_ff, self.g_dy3, self.g_dy2, self.g_dy1 = self.gathers
        self.reduces = [RowReduce(slots, rows, model) for _ in range(7)]
        self.r_out1, self.r_out2, self.r_out3, self.r_dn3, self.r_dn2, self.r_mem, self.r_dn1 = self.reduces
        kinds = (
            (4 * cols, (2 * cols, 256, 4 * cols - 2 * cols - 256), 128),
            (4 * cols, (2 * cols, 2 * cols), 384),
            (3 * hid, (768, 3 * hid - 768), 384),
        )
        self.groups = [SimpleNamespace(width=w, parts=p, step=s) for w, p, s in kinds]
        self.ws, self.wc, self.wf = self.groups
        for group in self.groups:
            if zy:
                both = VM((model, group.width), BF16)
                slots.add(group, w=both, gp=both)
                group.gather = WideGather(slots, wrows, group.parts)
                group.reduce = WideReduce(slots, wrows, group.width, group.step)
            else:
                outs.add(group, gp=((model, group.width), BF16))
                group.gather = group.reduce = Idle()
        if zy:
            self.ss = SmallSum(slots, 16, model)

    def blk(self, b):
        return aligned(b * QB, QB)

    def chunk(self, k, block=0):
        size = self.sizes[0] // ROW_CHUNKS
        return aligned(block * self.sizes[0] + k * size, size)

    def far_first(self, i):
        s = self.spot
        far = jnp.where(i < 2, 1 - s.x, s.x)
        return far * 2 + jnp.where(i % 2 == 0, 1 - s.c, s.c)

    def near_tile(self, i):
        s = self.spot
        near = jnp.where(i == 0, s.n, s.sib)
        first = jnp.where(i < 2, 2 * near, 2 * s.xsib + i - 2)
        second = jnp.where(i < 2, 2 * near + 1, 2 * s.xp + i - 2)
        return Tile(i, first, second)

    def near_block(self, i):
        s = self.spot
        far = jnp.where(i < 2, s.x, 1 - s.x)
        return far * 2 + jnp.where(i % 2 == 0, s.c, 1 - s.c)

    def block_tile(self, b):
        return Tile(b, 2 * b, 2 * b + 1)

    def near_waits(self, i, gather):
        @pl.when(i == 1)
        def _():
            gather.have_sib()
            gather.forward(0, 1)

        @pl.when(i == 2)
        def _():
            gather.forward(1, 2)
            gather.have_xsib(0, 2)

        @pl.when(i == 3)
        def _():
            gather.forward(2, 4)
            gather.have_xsib(2, 4)

    def near_sends(self, i, reduce):
        @pl.when(i == 1)
        def _():
            reduce.send_own()

        @pl.when(i == 2)
        def _():
            reduce.send_far(0, 2)
            reduce.cross(0, 2)

        @pl.when(i == 3)
        def _():
            reduce.send_far(2, 4)
            reduce.cross(2, 4)

    def at(self, i, *actions):
        for j, action in enumerate(actions):
            if action is not None:
                pl.when(i == j)(action)

    def pack(self, group, *shards):
        rows = self.sizes[4]
        parts = [ref[...].astype(F32) for ref in shards]
        parts = [p if p.shape[0] == rows else p.T for p in parts]
        group.w[aligned(self.spot.w * rows, rows), :] = jnp.concatenate(parts, axis=1).astype(BF16)

    def ff_tile(self, t):
        f = self.sizes[3]
        step = f // 2
        w = self.wf.w
        x, dy = t.load(self.full_ff), t.load(self.dy3)
        for j in range(0, f, step):
            gate = nn(x, w[:, j : j + step])
            up = nn(x, w[:, f + j : f + j + step])
            dh = nn(dy, w[:, 2 * f + j : 2 * f + j + step])
            value, slope = gelu_parts(gate)
            t.store(self.hidden, (value * up).astype(BF16), j)
            t.store(self.dgu, (dh * up * slope).astype(BF16), j)
            t.store(self.dgu, (dh * value).astype(BF16), f + j)
        t.store(self.pa, nt(t.load(self.dgu), w[:, : 2 * f]).astype(BF16))

    def grads_kv(self):
        c = self.sizes[2]
        self.dkvq[:, : 2 * c] = jnp.concatenate(
            [self.shared.dka[:, :c], self.shared.dva[...]], axis=1
        ).astype(BF16)

    def norm_backward(self, values, gain, reduce, base, done):
        gain_sum = jnp.zeros((1, self.sizes[1]), F32)
        for k in range(ROW_CHUNKS):
            rows = self.chunk(k)
            add, part = norm_back(values[rows, :].astype(F32), gain, reduce.total(k))
            gain_sum = gain_sum + part
            done(k, rows, base[rows, :].astype(F32) + add)
        return gain_sum

    def run(self):
        rows, model, cols, hid, wrows, length = self.sizes
        zy, heads, s_ = self.zy, self.heads, self.shared
        spot = self.spot = Spot(zy)
        one, two = self.one, self.two
        ws, wc, wf = self.groups
        greet(spot, zy)
        for gather, full in zip(
            self.gathers, (self.full_self, self.full_mem, self.full_cross, self.full_ff, self.dy3, self.dy2, self.dy1)
        ):
            gather.bind(spot, full)
        for reduce, part in zip(
            self.reduces, (self.pa, self.pb, self.pb, self.pa, self.pa, self.dgu, self.pa)
        ):
            reduce.bind(spot, part)
        column = 0
        for group in self.groups:
            group.gather.bind(spot, group.w)
            group.reduce.bind(spot, group.gp, self.red if zy else None, column)
            column += group.width
        width = heads * QB
        one.bind(ws.w, self.full_mem, self.cat)
        two.bind(wc.w, self.dgu.at[:, :width], self.cat)
        gain_s, gain_c, gain_f = (ref[...].reshape(1, model) for ref in (self.gain_s, self.gain_c, self.gain_f))

        if zy:
            self.ss.bind(spot)
            self.pack(ws, self.sk, self.sv, self.sq, self.so)
        ws.gather.open_z()
        ws.gather.open_y()
        for k in range(ROW_CHUNKS):
            x = self.x[self.chunk(k), :].astype(F32)
            self.full_self[self.chunk(k, spot.n), :] = norm_rows(x, gain_s).astype(BF16)
            self.g_self.send(k)
        self.full_mem[self.blk(spot.n), :] = self.m[...]
        self.g_mem.send_all()
        self.dy3[self.blk(spot.n), :] = self.cot[...]
        self.g_dy3.send_all(0, 2)
        if zy:
            self.pack(wc, self.ck, self.cv, self.cq, self.co)
            self.pack(wf, self.fg, self.fu, self.fd)
        ranges = bucket_ranges(2 * QB)
        document_columns((one.q, two.q), one.k, self.sid, cols)
        make_bias(s_, self.table, heads, ranges)
        ws.gather.forward(1, 0)
        ws.gather.forward(2, 0)
        self.g_self.forward(0, 2)
        ws.gather.forward(3, 0)
        ws.gather.forward(1, 1)
        self.g_self.forward(2, 4)
        ws.gather.forward(2, 1)
        ws.gather.forward(3, 1)
        wc.gather.open_z()
        self.g_self.have_sib()
        self.g_self.have_xsib(0, 4)
        ws.gather.have(0)

        one.project_kv(self.full_self)
        for distance in (1, 2, 3):
            ws.gather.forward(distance, 2)
        wc.gather.open_y()
        ws.gather.have(1, 2)

        def self_block(i, carry):
            b = self.far_first(i)
            t = self.block_tile(b)
            one.project_q(self.full_self, t)
            one.forward(t)
            one.out_part(self.pa, t)

            def after_first():
                self.r_out1.send_far()
                wc.gather.forward(1)
                wf.gather.open_z()
                wc.gather.forward(2, 0)

            def after_second():
                self.r_out1.cross()
                self.g_mem.forward(0, 4)
                wc.gather.forward(3, 0)
                wc.gather.forward(2, 1)

            def after_third():
                self.r_out1.send_own()
                wc.gather.forward(3, 1)
                wf.gather.open_y()

            self.at(i, after_first, after_second, after_third)
            return carry

        lax.fori_loop(0, 4, self_block, 0)
        document_columns(None, two.k, self.mid, cols)
        self.g_mem.have_sib()
        self.g_mem.have_xsib(0, 4)
        wc.gather.have()
        two.project_kv(self.full_mem)
        self.g_dy3.forward(0, 2)
        for k in range(ROW_CHUNKS):
            value = self.x[self.chunk(k), :].astype(F32) + self.r_out1.total(k)
            self.x_two[self.chunk(k), :] = value
            self.full_cross[self.chunk(k, spot.n), :] = norm_rows(value, gain_c).astype(BF16)
            self.g_cross.send(k)
        self.g_dy3.send_all(2, 4)
        wf.gather.forward(1, 0)

        def cross_block(i, carry):
            t = self.near_tile(i)
            self.near_waits(i, self.g_cross)
            two.project_q(self.full_cross, t)
            two.forward(t)
            two.out_part(self.pb, t)
            self.near_sends(i, self.r_out2)
            self.at(i, lambda: [wf.gather.forward(2, 0)] and None, lambda: [wf.gather.forward(3, 0), wf.gather.forward(1, 1)] and None, lambda: [wf.gather.forward(2, 1), wf.gather.forward(3, 1)] and None)
            return carry

        lax.fori_loop(0, 4, cross_block, 0)
        self.g_dy3.forward(2, 4)
        for k in range(ROW_CHUNKS):
            value = self.x_two[self.chunk(k), :] + self.r_out2.total(k)
            self.x_three[self.chunk(k), :] = value
            self.full_ff[self.chunk(k, spot.n), :] = norm_rows(value, gain_f).astype(BF16)
            self.g_ff.send(k)
        self.r_out1.finish()
        self.r_out2.finish()
        self.g_dy3.have_sib()
        self.g_dy3.have_xsib(0, 4)
        wf.gather.have()

        def ff_step(i, carry):
            self.near_waits(i, self.g_ff)
            self.ff_tile(self.near_tile(i))
            self.near_sends(i, self.r_dn3)
            return carry

        lax.fori_loop(0, 4, ff_step, 0)
        weight_grad(wf.gp, 0, self.full_ff, self.dgu, 0, 2 * hid)
        split = wf.reduce.chunks * 2 // 3
        for c in range(split):
            wf.reduce.open(c)

        def ff_out(b, carry):
            self.pb[self.blk(b), :] = nt(self.hidden[self.blk(b), :], wf.w[:, 2 * hid :]).astype(BF16)
            return carry

        lax.fori_loop(0, 4, ff_out, 0)
        self.r_out3.send_far()
        self.r_out3.send_own()
        weight_grad(wf.gp, 2 * hid, self.dy3, self.hidden, 0, hid)
        for c in range(split, wf.reduce.chunks):
            wf.reduce.open(c)

        def back_three(k, at, value):
            self.g[at, :] = value
            self.dy2[self.chunk(k, spot.n), :] = value.astype(BF16)
            self.g_dy2.send(k)

        gain_ff = self.norm_backward(self.x_three, gain_f, self.r_dn3, self.cot, back_three)
        self.small[14:15, :] = gain_ff
        self.r_out3.cross(0, 2)

        self.r_dn3.finish()
        s_.dka[...] = jnp.zeros_like(s_.dka)
        s_.dva[...] = jnp.zeros_like(s_.dva)

        def cross_back(i, carry):
            t = self.near_tile(i)
            self.near_waits(i, self.g_dy2)
            dctx = nn(t.load(self.dy2), two.wcols(3, 1)).astype(BF16)
            dq = two.backward(t, dctx)
            t.store(self.dkvq, dq, 2 * cols)
            t.store(self.pa, nt(dq, two.wcols(2, 1)).astype(BF16))
            self.near_sends(i, self.r_dn2)
            if zy:
                self.at(i, lambda: wf.reduce.first(0), lambda: wf.reduce.first(1), None, lambda: wf.reduce.first(2))
            return carry

        lax.fori_loop(0, 4, cross_back, 0)
        self.grads_kv()

        def memory_part(b, carry):
            blk = self.blk(b)
            self.dgu[blk, 0:model] = nt(self.dkvq[blk, : 2 * cols], two.wcols(0, 2)).astype(BF16)
            return carry

        lax.fori_loop(0, 4, memory_part, 0)
        self.r_mem.send_far()
        self.r_mem.send_own()
        if zy:
            wf.reduce.first(3)

        def back_two(k, at, value):
            self.g[at, :] = value
            self.dy1[self.chunk(k, spot.n), :] = value.astype(BF16)
            self.g_dy1.send(k)

        gain_cross = self.norm_backward(self.x_two, gain_c, self.r_dn2, self.g, back_two)
        self.small[13:14, :] = gain_cross
        self.r_out3.cross(2, 4)
        self.r_mem.cross()
        weight_grad(wc.gp, 0, self.full_mem, self.dkvq, 0, 2 * cols)
        wc.reduce.open(0)
        weight_grad(wc.gp, 2 * cols, self.full_cross, self.dkvq, 2 * cols, cols)
        weight_grad(wc.gp, 3 * cols, self.dy2, two.ctx, 0, cols)
        wc.reduce.open(1)

        self.g_mem.finish()
        s_.dka[...] = jnp.zeros_like(s_.dka)
        s_.dva[...] = jnp.zeros_like(s_.dva)

        def self_waits(i):
            @pl.when(i == 1)
            def _():
                self.g_dy1.have_sib()
                self.g_dy1.forward(0, 1)

            @pl.when(i == 2)
            def _():
                self.g_dy1.forward(1, 4)

            @pl.when(i == 3)
            def _():
                self.g_dy1.have_xsib(0, 4)

        def self_back(i, carry):
            b = self.near_block(i)
            t = self.block_tile(b)
            self_waits(i)
            dctx = nn(t.load(self.dy1), one.wcols(3, 1)).astype(BF16)
            t.store(self.dkvq, one.backward(t, dctx), 2 * cols)

            def ff_totals():
                for c in range(wf.reduce.chunks):
                    wf.reduce.total(c)

            self.at(i, None, lambda: wc.reduce.first(0), ff_totals, lambda: wc.reduce.first(1))
            return carry

        lax.fori_loop(0, 4, self_back, 0)
        self.grads_kv()
        self.r_dn2.finish()

        def last_part(i, carry):
            blk = self.blk(self.far_first(i))
            self.pa[blk, :] = nt(self.dkvq[blk, :], one.wcols(0, 3)).astype(BF16)
            return carry

        lax.fori_loop(0, 2, last_part, 0)
        self.r_dn1.send_far()
        weight_grad(ws.gp, 0, self.full_self, self.dkvq, 0, 3 * cols)
        weight_grad(ws.gp, 3 * cols, self.dy1, one.ctx, 0, cols)
        for c in range(ws.reduce.chunks):
            ws.reduce.open(c)
        self.r_dn1.cross()
        lax.fori_loop(2, 4, last_part, 0)
        self.r_dn1.send_own()

        def gain_part(b, total):
            blk = self.blk(b)
            both = self.full_self[blk, :].astype(F32) * self.pa[blk, :].astype(F32)
            return total + jnp.sum(both, axis=0, keepdims=True)

        gain_self = lax.fori_loop(0, 4, gain_part, jnp.zeros((1, model), F32)) / gain_s
        keep = self.small[13:15, :]
        self.small[...] = jnp.zeros_like(self.small)
        self.small[:, 0:128] = table_rows(s_, heads, spot.n)
        self.small[12:13, :] = gain_self
        self.small[13:15, :] = keep
        if zy:
            self.ss.begin(self.small[...])
        else:
            self.tot[...] = self.small[...]
        for k in range(ROW_CHUNKS):
            value = self.x_three[self.chunk(k), :] + self.r_out3.total(k)
            self.result[self.chunk(k), :] = value.astype(BF16)
        if zy:
            self.ss.to_z()
            ws.reduce.first(0)
            ws.reduce.first(1)
            self.ss.to_x()
        for k in range(ROW_CHUNKS):
            self.gm[self.chunk(k), :] = self.r_mem.total(k).astype(BF16)
        for c in range(wc.reduce.chunks):
            wc.reduce.total(c)
        if zy:
            ws.reduce.first(2)

        def back_one(k, at, value):
            self.gx[at, :] = value.astype(BF16)
            if zy and k == 1:
                ws.reduce.first(3)

        self.norm_backward(self.x, gain_s, self.r_dn1, self.g, back_one)
        if zy:
            self.ss.to_y()
            ws.reduce.first(4)
            ws.reduce.first(5)
            for c in range(ws.reduce.chunks):
                ws.reduce.total(c)
            self.ss.end(self.tot)

        for gather in self.gathers:
            if gather is not self.g_mem:
                gather.finish()
        for reduce in (self.r_out3, self.r_mem, self.r_dn1):
            reduce.finish()
        for group in self.groups:
            group.gather.finish()
            group.reduce.finish()


def deliver(red, tot, passed, sizes, heads):
    rows, model, cols, hid, wrows, length = sizes
    ins, outs = Slots(), Slots()
    packed, small = SimpleNamespace(), SimpleNamespace()
    ins.add(packed, ref=(red, VM))
    ins.add(small, ref=(tot, VM))
    sources, dests = [SimpleNamespace() for _ in passed], [SimpleNamespace() for _ in passed]
    for value, source, dest in zip(passed, sources, dests):
        ins.add(source, ref=(value, VM))
        outs.add(dest, ref=(value.shape, value.dtype))
    places = [(i * cols, cols, i % 4 == 3) for i in (2, 0, 1, 3, 6, 4, 5, 7)]
    places += [(8 * cols + i * hid, hid, False) for i in range(3)]
    cuts = []
    for at, width, turn in places:
        cut = SimpleNamespace(at=at, width=width, turn=turn)
        outs.add(cut, ref=((width, wrows) if turn else (wrows, width), F32))
        cuts.append(cut)
    gains, table = [SimpleNamespace() for _ in range(3)], SimpleNamespace()
    for gain in gains:
        outs.add(gain, ref=((model,), F32))
    outs.add(table, ref=((4 * heads, NB), F32))

    def body():
        for source, dest in zip(sources, dests):
            dest.ref[...] = source.ref[...]
        for cut in cuts:
            part = packed.ref[:, cut.at : cut.at + cut.width]
            cut.ref[...] = part.T if cut.turn else part
        for i, gain in enumerate(gains):
            gain.ref[...] = small.ref[12 + i : 13 + i, :].reshape(model)
        table.ref[...] = small.ref[0 : 4 * heads, 0:NB]

    got = run_kernel(body, ins, outs, Slots(), None, "deliver")
    return got[:3], got[3:14], got[14:17], got[17]


def shards(
    zy, inputs, memory, segment_ids, memory_ids, self_gain, self_query, self_key, self_value, self_out, bias_table,
    cross_gain, cross_query, cross_key, cross_value, cross_out, ff_gain, ff_gate, ff_up, ff_down, cotangent,
):
    rows, model = inputs.shape
    length = segment_ids.shape[1]
    wrows, cols = self_query.shape
    hid = ff_gate.shape[1]
    heads = cols // DH
    assert segment_ids.shape[0] == 1 and rows == QB and length == 4 * QB == memory_ids.shape[1]
    sizes = (rows, model, cols, hid, wrows, length)
    ins, outs, slots = Slots(), Slots(), Slots()
    layer = Layer.__new__(Layer)
    outs.add(
        layer, result=((rows, model), BF16), gx=((rows, model), BF16), gm=((rows, model), BF16), tot=((16, model), F32)
    )
    if zy:
        outs.add(layer, red=((wrows, 8 * cols + 3 * hid), F32))
    layer.__init__(zy, sizes, ins, outs, slots)
    ins.add(
        layer, x=(inputs, VM), m=(memory, VM), cot=(cotangent, VM), sid=(segment_ids, VM), mid=(memory_ids, VM),
        gain_s=(self_gain, VM), gain_c=(cross_gain, VM), gain_f=(ff_gain, VM), table=(bias_table.T, pltpu.SMEM),
    )
    if zy:
        ins.add(
            layer, sq=(self_query, VM), sk=(self_key, VM), sv=(self_value, VM), so=(self_out, VM),
            cq=(cross_query, VM), ck=(cross_key, VM), cv=(cross_value, VM), co=(cross_out, VM),
            fg=(ff_gate, VM), fu=(ff_up, VM), fd=(ff_down.T, VM),
        )
    else:

        def whole(*parts):
            return lax.all_gather(jnp.concatenate(parts, axis=1), WIDE, axis=0, tiled=True)

        ins.add(layer.ws, w=(whole(self_key, self_value, self_query, self_out.T), VM))
        ins.add(layer.wc, w=(whole(cross_key, cross_value, cross_query, cross_out.T), VM))
        ins.add(layer.wf, w=(whole(ff_gate, ff_up, ff_down.T), VM))
    got = run_kernel(layer.run, ins, outs, slots, 0, "layer")
    if zy:
        total, red = got[3], got[4]
    else:
        packed = jnp.concatenate(got[4:7], axis=1)
        red = lax.psum_scatter(packed, WIDE, scatter_dimension=0, tiled=True).astype(F32)
        total = lax.psum(got[3], (WIDE, NARROW))
    row_outs, grads, gains, table = deliver(red, total, got[:3], sizes, heads)
    return (
        *row_outs,
        gains[0],
        *grads[0:4],
        table.T,
        gains[1],
        *grads[4:8],
        gains[2],
        grads[8],
        grads[9],
        grads[10].T,
    )


def solution(mesh):
    zy = mesh.shape[WIDE] == 8
    rows = P((WIDE, NARROW), None)
    w_in, w_out = P(WIDE, NARROW), P(NARROW, WIDE)
    placed = (
        rows, rows, P(WIDE, None), P(WIDE, None), P(),
        w_in, w_in, w_in, w_out, P(None, NARROW), P(),
        w_in, w_in, w_in, w_out, P(), w_in, w_in, w_out, rows,
    )
    outs = (
        rows, rows, rows, P(), w_in, w_in, w_in, w_out, P(), P(),
        w_in, w_in, w_in, w_out, P(), w_in, w_in, w_out,
    )

    def program(*args):
        return shards(zy, *args)

    return jax.shard_map(program, mesh=mesh, in_specs=placed, out_specs=outs, check_vma=False)
```

```python
import math
from types import SimpleNamespace

import jax
import jax.numpy as jnp
import numpy as np
from jax import lax
from jax.experimental import pallas as pl
from jax.experimental.pallas import tpu as pltpu
from jax.sharding import PartitionSpec as P

DH = 64
NB = 32
MAX_DIST = 128
EPS = 1e-06
NEG = -1e30
QB = 256
HALF = 128
ROW_CHUNKS = 4
WIDE = "wide"
NARROW = "narrow"
MESH = pl.DeviceIdType.MESH
F32 = jnp.float32
BF16 = jnp.bfloat16
VM = pltpu.VMEM
DMA = pltpu.SemaphoreType.DMA


def bucket_table(length, buckets, reach):
    exact_part = buckets // 2
    distance = np.arange(length)
    spread = (
        np.log(np.maximum(distance, exact_part) / exact_part)
        / np.log(reach / exact_part)
        * (buckets - exact_part)
    )
    far_bucket = np.minimum(exact_part + np.floor(spread).astype(np.int64), buckets - 1)
    return np.where(distance < exact_part, distance, far_bucket).astype(np.int32)


def bucket_ranges(length):
    table = bucket_table(length, NB, MAX_DIST)
    found = []
    for which in range(NB):
        places = np.nonzero(table == which)[0]
        if len(places):
            found.append((which, int(places[0]), int(places[-1]) + 1))
    return found


class Slots:
    def __init__(self):
        self.items = []

    def add(self, holder, **specs):
        for name, spec in specs.items():
            self.items.append((holder, name, spec))

    def fill(self, refs):
        for (holder, name, _), ref in zip(self.items, refs):
            setattr(holder, name, ref)


def run_kernel(body, ins, outs, scratch, cid, name):
    counts = len(ins.items), len(outs.items)

    def kernel(*refs):
        ins.fill(refs[: counts[0]])
        outs.fill(refs[counts[0] : counts[0] + counts[1]])
        scratch.fill(refs[counts[0] + counts[1] :])
        body()

    params = {} if cid is None else dict(collective_id=cid, has_side_effects=True)
    return pl.pallas_call(
        kernel,
        out_shape=[jax.ShapeDtypeStruct(*spec) for _, _, spec in outs.items],
        in_specs=[pl.BlockSpec(memory_space=spec[1]) for _, _, spec in ins.items],
        out_specs=[pl.BlockSpec(memory_space=VM) for _ in outs.items],
        scratch_shapes=[spec for _, _, spec in scratch.items],
        compiler_params=pltpu.CompilerParams(vmem_limit_bytes=66_900_000, **params),
        name=name,
    )(*[spec[0] for _, _, spec in ins.items])


class Spot:
    def __init__(self, wide_split):
        n = lax.axis_index(NARROW)
        self.n = n
        self.x = n // 2
        self.c = n % 2
        self.sib = self.x * 2 + (1 - self.c)
        self.xp = (1 - self.x) * 2 + self.c
        self.xsib = (1 - self.x) * 2 + (1 - self.c)
        if wide_split:
            w = lax.axis_index(WIDE)
            self.w = w
            self.z = w // 2
            self.y = w % 2
            self.yp = self.z * 2 + (1 - self.y)

    def at_n(self, n):
        return {NARROW: n}

    def at_w(self, w):
        return {WIDE: w}

    def at_z(self, z):
        return {WIDE: z * 2 + self.y}


def remote(src, dst, send, recv, dev):
    return pltpu.make_async_remote_copy(
        src_ref=src, dst_ref=dst, send_sem=send, recv_sem=recv, device_id=dev, device_id_type=MESH
    )


def greet(spot, zy):
    barrier = pltpu.get_barrier_semaphore()

    def hello(dev):
        pl.semaphore_signal(barrier, inc=1, device_id=dev, device_id_type=MESH)

    hello(spot.at_n(spot.sib))
    hello(spot.at_n(spot.xp))
    if zy:
        hello(spot.at_w(spot.yp))
        for step in range(1, 4):
            hello(spot.at_z((spot.z + step) % 4))
    pl.semaphore_wait(barrier, 6 if zy else 2)


def aligned(start, size):
    return pl.ds(pl.multiple_of(start, 16), size)


class RowGather:
    def __init__(self, slots, rows, chunks=ROW_CHUNKS):
        self.nrows, self.chunks, self.size = rows, chunks, rows // chunks
        sems = DMA((chunks,))
        slots.add(self, xs=sems, xr=sems, ss=sems, sr=sems, fs=sems, fr=sems)

    def bind(self, spot, full):
        self.spot, self.full = spot, full

    def hop(self, k, block, dev, send, recv):
        rows = self.full.at[aligned(block * self.nrows + k * self.size, self.size)]
        return remote(rows, rows, send.at[k], recv.at[k], self.spot.at_n(dev))

    def to_x(self, k):
        return self.hop(k, self.spot.n, self.spot.xp, self.xs, self.xr)

    def from_x(self, k):
        return self.hop(k, self.spot.xp, self.spot.xp, self.xs, self.xr)

    def to_sib(self, k):
        return self.hop(k, self.spot.n, self.spot.sib, self.ss, self.sr)

    def from_sib(self, k):
        return self.hop(k, self.spot.sib, self.spot.sib, self.ss, self.sr)

    def onward(self, k):
        return self.hop(k, self.spot.xp, self.spot.sib, self.fs, self.fr)

    def from_onward(self, k):
        return self.hop(k, self.spot.xsib, self.spot.sib, self.fs, self.fr)

    def send(self, k):
        self.to_x(k).start()
        self.to_sib(k).start()

    def send_all(self, first=0, after=ROW_CHUNKS):
        for k in range(first, after):
            self.send(k)

    def forward(self, first, after):
        for k in range(first, after):
            self.from_x(k).wait_recv()
            self.onward(k).start()

    def have_sib(self):
        for k in range(self.chunks):
            self.from_sib(k).wait_recv()

    def have_xsib(self, first, after):
        for k in range(first, after):
            self.from_onward(k).wait_recv()

    def finish(self):
        for k in range(self.chunks):
            self.to_x(k).wait_send()
            self.to_sib(k).wait_send()
            self.onward(k).wait_send()


class RowReduce:
    def __init__(self, slots, rows, cols, chunks=ROW_CHUNKS):
        self.nrows, self.ncols, self.chunks, self.size = rows, cols, chunks, rows // chunks
        sems, buf = DMA((chunks,)), VM((rows, cols), BF16)
        slots.add(self, as_=sems, ar=sems, bs=sems, br=sems, xs=sems, xr=sems, far=buf, own=buf, inn=buf)

    def bind(self, spot, part):
        self.spot, self.part = spot, part

    def buf(self, ref, k):
        return ref.at[pl.ds(k * self.size, self.size)]

    def mine(self, block, k):
        return self.part.at[aligned(block * self.nrows + k * self.size, self.size), pl.ds(0, self.ncols)]

    def far_sib(self, k):
        s = self.spot
        return remote(self.mine(s.xsib, k), self.buf(self.far, k), self.as_.at[k], self.ar.at[k], s.at_n(s.sib))

    def own_sib(self, k):
        s = self.spot
        return remote(self.mine(s.sib, k), self.buf(self.own, k), self.bs.at[k], self.br.at[k], s.at_n(s.sib))

    def across(self, k):
        s = self.spot
        return remote(self.buf(self.far, k), self.buf(self.inn, k), self.xs.at[k], self.xr.at[k], s.at_n(s.xp))

    def send_far(self, first=0, after=ROW_CHUNKS):
        for k in range(first, after):
            self.far_sib(k).start()

    def send_own(self):
        for k in range(self.chunks):
            self.own_sib(k).start()

    def cross(self, first=0, after=ROW_CHUNKS):
        for k in range(first, after):
            self.far_sib(k).wait_recv()
            here = self.buf(self.far, k)
            here[...] = (self.mine(self.spot.xp, k)[...].astype(F32) + here[...].astype(F32)).astype(BF16)
            self.across(k).start()

    def total(self, k):
        self.own_sib(k).wait_recv()
        self.across(k).wait_recv()
        value = self.mine(self.spot.n, k)[...].astype(F32) + self.buf(self.own, k)[...].astype(F32)
        return value + self.buf(self.inn, k)[...].astype(F32)

    def finish(self):
        for k in range(self.chunks):
            self.far_sib(k).wait_send()
            self.own_sib(k).wait_send()
            self.across(k).wait_send()


class WideGather:
    steps = (1, -1, 2, -2, 3, -3)

    def __init__(self, slots, rows, widths):
        self.nrows, self.widths, self.parts = rows, widths, range(len(widths))
        four = DMA((4, len(widths)))
        slots.add(self, zs=DMA((6, len(widths))), zr=four, ys=four, yr=four)

    def bind(self, spot, full):
        self.spot, self.full = spot, full

    def rows(self, z, y, part):
        cols = pl.ds(sum(self.widths[:part]), self.widths[part])
        return self.full.at[aligned((z * 2 + y) * self.nrows, self.nrows), cols]

    def along(self, i, part):
        s = self.spot
        rows = self.rows(s.z, s.y, part)
        return remote(rows, rows, self.zs.at[i, part], self.zr.at[s.z, part], s.at_z(s.z + self.steps[i]))

    def came(self, z, part):
        s = self.spot
        rows = self.rows(z, s.y, part)
        return remote(rows, rows, self.zs.at[0, part], self.zr.at[z, part], s.at_z(z))

    def over(self, z, part):
        s = self.spot
        rows = self.rows(z, s.y, part)
        return remote(rows, rows, self.ys.at[z, part], self.yr.at[z, part], s.at_w(s.yp))

    def crossed(self, z, part):
        s = self.spot
        rows = self.rows(z, 1 - s.y, part)
        return remote(rows, rows, self.ys.at[z, part], self.yr.at[z, part], s.at_w(s.yp))

    def when_inside(self, step, fn):
        there = self.spot.z + step

        @pl.when(there >= 0 if step < 0 else there <= 3)
        def _():
            fn(there)

    def open_y(self):
        for part in self.parts:
            self.over(self.spot.z, part).start()

    def open_z(self):
        for part in self.parts:
            for i, step in enumerate(self.steps):
                self.when_inside(step, lambda there: self.along(i, part).start())

    def forward(self, distance, *parts):
        for part in parts or self.parts:
            for step in (distance, -distance):

                def pass_on(there):
                    self.came(there, part).wait_recv()
                    self.over(there, part).start()

                self.when_inside(step, pass_on)

    def have(self, *parts):
        for part in parts or self.parts:
            for z in range(4):
                self.crossed(z, part).wait_recv()

    def finish(self):
        for part in self.parts:
            for z in range(4):
                self.over(z, part).wait_send()
            for i, step in enumerate(self.steps):
                self.when_inside(step, lambda there: self.along(i, part).wait_send())


class WideReduce:
    steps = (2, 3, 1, 0)

    def __init__(self, slots, rows, cols, width):
        self.nrows, self.width, self.chunks = rows, width, cols // width
        sems, buf = DMA((self.chunks, 4)), VM((4, rows, cols), BF16)
        slots.add(self, ys=sems, yr=sems, zs=sems, zr=sems, acc=buf, inn=buf)

    def bind(self, spot, part, out, out_col):
        self.spot, self.part, self.out, self.out_col = spot, part, out, out_col

    def cols(self, c):
        return pl.ds(c * self.width, self.width)

    def slab(self, c, z, y):
        return self.part.at[aligned((z * 2 + y) * self.nrows, self.nrows), self.cols(c)]

    def over(self, c, z):
        s = self.spot
        return remote(
            self.slab(c, z, 1 - s.y), self.acc.at[z, :, self.cols(c)], self.ys.at[c, z], self.yr.at[c, z], s.at_w(s.yp)
        )

    def along(self, c, z):
        s = self.spot
        return remote(
            self.acc.at[z, :, self.cols(c)], self.inn.at[s.z, :, self.cols(c)],
            self.zs.at[c, z], self.zr.at[c, s.z], s.at_z(z),
        )

    def came(self, c, z):
        here = self.inn.at[z, :, self.cols(c)]
        return remote(here, here, self.zs.at[c, z], self.zr.at[c, z], self.spot.at_z(z))

    def targets(self):
        return [(self.spot.z + step) % 4 for step in self.steps]

    def open(self, c):
        for z in self.targets():
            self.over(c, z).start()

    def first(self, c):
        for step, z in zip(self.steps, self.targets()):
            self.over(c, z).wait_recv()
            here = self.acc.at[z, :, self.cols(c)]
            here[...] = (self.slab(c, z, self.spot.y)[...].astype(F32) + here[...].astype(F32)).astype(BF16)
            if step:
                self.along(c, z).start()

    def total(self, c):
        value = self.acc[self.spot.z, :, self.cols(c)].astype(F32)
        for z in self.targets()[:3]:
            self.came(c, z).wait_recv()
            value = value + self.inn[z, :, self.cols(c)].astype(F32)
        self.out[:, pl.ds(self.out_col + c * self.width, self.width)] = value

    def finish(self):
        for c in range(self.chunks):
            for step, z in zip(self.steps, self.targets()):
                self.over(c, z).wait_send()
                if step:
                    self.along(c, z).wait_send()


class SmallSum:
    def __init__(self, slots, rows, cols):
        four = VM((4, rows, cols), F32)
        slots.add(
            self, ps=DMA((3,)), pr=DMA((3,)), zs=DMA((4,)), zr=DMA((4,)), held=four, inn=VM((3, rows, cols), F32), zin=four
        )

    def bind(self, spot):
        self.spot = spot

    def pair(self, i):
        s = self.spot
        source, dev = ((0, s.at_n(s.sib)), (2, s.at_n(s.xp)), (3, s.at_w(s.yp)))[i]
        return remote(self.held.at[source], self.inn.at[i], self.ps.at[i], self.pr.at[i], dev)

    def hop(self, step, landed):
        other = (self.spot.z + step) % 4
        return remote(
            self.held.at[1], self.zin.at[landed], self.zs.at[step], self.zr.at[landed], self.spot.at_z(other)
        )

    def begin(self, value):
        self.held[0] = value
        self.pair(0).start()

    def to_z(self):
        self.pair(0).wait_recv()
        self.held[1] = self.held[0] + self.inn[0]
        self.zin[self.spot.z] = self.held[1]
        for step in range(1, 4):
            self.hop(step, self.spot.z).start()

    def to_x(self):
        for step in range(1, 4):
            self.hop(step, (self.spot.z + step) % 4).wait_recv()
        self.held[2] = ((self.zin[0] + self.zin[1]) + self.zin[2]) + self.zin[3]
        self.pair(1).start()

    def to_y(self):
        self.pair(1).wait_recv()
        self.held[3] = self.held[2] + self.inn[1]
        self.pair(2).start()

    def end(self, out):
        self.pair(2).wait_recv()
        out[...] = self.held[3] + self.inn[2]
        for i in range(3):
            self.pair(i).wait_send()
        for step in range(1, 4):
            self.hop(step, self.spot.z).wait_send()


class Idle:
    chunks = 0

    def bind(self, *args):
        pass

    open = open_y = open_z = forward = have = finish = first = total = bind


def nt(left, right):
    return lax.dot_general(left, right, (((1,), (1,)), ((), ())), preferred_element_type=F32)


def nn(left, right):
    return lax.dot_general(left, right, (((1,), (0,)), ((), ())), preferred_element_type=F32)


def tn(left, right):
    return lax.dot_general(left, right, (((0,), (0,)), ((), ())), preferred_element_type=F32)


def mean_square(values):
    return jnp.mean(values * values, axis=-1, keepdims=True)


def norm_rows(values, gain):
    return values * lax.rsqrt(mean_square(values) + EPS) * gain


def norm_back(values, gain, dn):
    r = lax.rsqrt(mean_square(values) + EPS)
    u = values * r
    dg = dn * gain
    rows = r * (dg - u * jnp.mean(dg * u, axis=-1, keepdims=True))
    return rows, jnp.sum(dn * u, axis=0, keepdims=True)


def gelu_parts(v):
    c = math.sqrt(2.0 / math.pi)
    t = jnp.tanh(c * (v + 0.044715 * v * v * v))
    value = 0.5 * v * (1.0 + t)
    slope = 0.5 * (1.0 + t) + 0.5 * v * (1.0 - t * t) * c * (1.0 + 3.0 * 0.044715 * v * v)
    return value, slope


def head_rows(values, h, heads):
    lane = lax.broadcasted_iota(jnp.int32, values.shape, 1) // DH
    return jnp.where(jnp.logical_or(lane == h, lane >= heads), values, jnp.zeros_like(values))


def document_columns(query_ref, key_ref, ids, first):
    column = jnp.broadcast_to(ids[...].astype(F32), (128, ids.shape[1])).T[:, :DH]
    lane = lax.broadcasted_iota(jnp.int32, column.shape, 1)
    same = column == lane.astype(F32)
    if query_ref is not None:
        for ref in query_ref:
            ref[:, first : first + DH] = jnp.where(same, 1.0, 0.0).astype(BF16)
    if key_ref is not None:
        other = jnp.logical_and(jnp.logical_not(same), lane < 4)
        key_ref[:, first : first + DH] = jnp.where(other, NEG, 0.0).astype(BF16)


def diagonal_sums(tile):
    rows, width = tile.shape
    while rows > 1:
        rows = rows // 2
        tile = tile[:rows] + pltpu.roll(tile[rows:], width - rows, 1)
    return tile


class Tile:
    def __init__(self, slot, first, second):
        self.slot, self.halves = slot, (first, second)

    def rows(self, half):
        return aligned(half * HALF, HALF)

    def load(self, ref):
        return jnp.concatenate([ref[self.rows(h), :] for h in self.halves], axis=0)

    def store(self, ref, value, at=0):
        for i, h in enumerate(self.halves):
            ref[self.rows(h), at : at + value.shape[1]] = value[i * HALF : (i + 1) * HALF]


class Attention:
    def __init__(self, slots, shared, length, cols, causal):
        self.shared, self.cols, self.heads, self.causal = shared, cols, cols // DH, causal
        rows, marked, turned = VM((length, cols), BF16), VM((length, cols + DH), BF16), VM((4, cols, QB), BF16)
        slots.add(
            self, q=marked, k=marked, v=rows, ctx=rows, kt=turned, vt=turned, lse=VM((4, self.heads, 1, QB), F32)
        )

    def bind(self, weights, pcat, dcat):
        self.w, self.pcat, self.dcat = weights, pcat, dcat

    def blk(self, b):
        return aligned(b * QB, QB)

    def wcols(self, first, count):
        return self.w[:, first * self.cols : (first + count) * self.cols]

    def window(self, t, body):
        if not self.causal:
            body(0, 4)
            return
        for count in (1, 2, 3):
            pl.when(jnp.minimum(t.slot + 1, 3) == count)(lambda: body(t.slot + 1 - count, count))

    def keys(self, first, count):
        return aligned(first * QB, count * QB)

    def score(self, k, h, count):
        s = nt(k, self.shared.qm[self.wide_of(h), :])
        if self.causal:
            s = s + jnp.concatenate([self.shared.bias[self.kind(j, count), h] for j in range(count)], axis=0)
        return s

    def kind(self, j, count):
        return min(count - 1 - j, 2)

    def over_keys(self, turned, first, count, hs, right):
        parts = [nn(turned[first + j, hs, :], right[j * QB : (j + 1) * QB]) for j in range(count)]
        return sum(parts[1:], parts[0])

    def project_kv(self, source):
        c = self.cols

        def one(b, carry):
            kv = nn(source[self.blk(b), :], self.wcols(0, 2))
            k, v = kv[:, :c], kv[:, c:]
            self.k[self.blk(b), :c] = k.astype(BF16)
            self.v[self.blk(b), :] = v.astype(BF16)
            self.kt[b] = k.T.astype(BF16)
            self.vt[b] = v.T.astype(BF16)
            return carry

        lax.fori_loop(0, 4, one, 0)

    def project_q(self, source, t):
        t.store(self.q, nn(t.load(source), self.wcols(2, 1)).astype(BF16))

    def out_part(self, dest, t):
        t.store(dest, nt(t.load(self.ctx), self.wcols(3, 1)).astype(BF16))

    def rows_of(self, h):
        return slice(h * DH, (h + 1) * DH)

    def wide_of(self, h):
        return slice(h * QB, (h + 1) * QB)

    def forward(self, t):
        s_ = self.shared
        q = t.load(self.q)
        for h in range(self.heads):
            s_.qm[self.wide_of(h), :] = head_rows(q, h, self.heads)

        def attend(first, count):
            k = self.k[self.keys(first, count), :]
            for h in range(self.heads):
                hs = self.rows_of(h)
                s = self.score(k, h, count)
                peak = jnp.max(s, axis=0, keepdims=True)
                x = jnp.exp(s - peak)
                total = jnp.sum(x, axis=0, keepdims=True)
                s_.oacc[hs, :] = self.over_keys(self.vt, first, count, hs, x.astype(BF16)) / total
                self.lse[t.slot, h] = peak + jnp.log(total)

        self.window(t, attend)
        t.store(self.ctx, s_.oacc[...].T.astype(BF16))

    def backward(self, t, dctx):
        s_ = self.shared
        q = t.load(self.q)
        prod = (dctx.astype(F32) * t.load(self.ctx).astype(F32)).T
        for h in range(self.heads):
            s_.qm[self.wide_of(h), :] = head_rows(q, h, self.heads)
            s_.dm[self.wide_of(h), :] = head_rows(dctx, h, self.heads)
            s_.delta[h] = jnp.sum(prod[self.rows_of(h), :], axis=0, keepdims=True)

        def attend(first, count):
            keys, span = self.keys(first, count), count * QB
            k, v = self.k[keys, :], self.v[keys, :]
            for h in range(self.heads):
                hs, wide = self.rows_of(h), self.wide_of(h)
                p = jnp.exp(self.score(k, h, count) - self.lse[t.slot, h])
                ds = p * (nt(v, s_.dm[wide, :]) - s_.delta[h])
                if self.causal:
                    for j in range(count):
                        s_.gb[self.kind(j, count), h] += ds[j * QB : (j + 1) * QB]
                low = ds.astype(BF16)
                self.pcat[:span, wide] = p.astype(BF16)
                self.dcat[:span, wide] = low
                s_.oacc[hs, :] = self.over_keys(self.kt, first, count, hs, low)
            s_.dva[keys, :] += nn(self.pcat[:span, :], s_.dm[...])
            s_.dka[keys, :] += nn(self.dcat[:span, :], s_.qm[...])

        self.window(t, attend)
        return s_.oacc[...].T.astype(BF16)


def make_bias(s_, table, heads, ranges):
    lane = lax.broadcasted_iota(jnp.int32, (1, 2 * QB), 1)
    jj = lax.broadcasted_iota(jnp.int32, (QB, QB), 0)
    ii = lax.broadcasted_iota(jnp.int32, (QB, QB), 1)
    for h in range(heads):
        row = jnp.full((1, 2 * QB), table[h, NB - 1])
        for which, start, stop in reversed(ranges[:-1]):
            row = jnp.where(lane < stop, table[h, which], row)
        turned = pltpu.roll(jnp.broadcast_to(row, (QB, 2 * QB)), 0, 1, stride=1, stride_axis=0)
        s_.bias[0, h] = jnp.where(jj <= ii, turned[:, :QB], NEG)
        s_.bias[1, h] = turned[:, QB:]
        s_.bias[2, h] = jnp.full((QB, QB), table[h, NB - 1])
    s_.gb[...] = jnp.zeros_like(s_.gb)
    lane = lax.broadcasted_iota(jnp.int32, (1, 128), 1)
    first = jnp.full((1, 128), 2 * QB, jnp.int32)
    after = jnp.zeros((1, 128), jnp.int32)
    for which, start, stop in ranges:
        first = jnp.where(lane == which, start, first)
        after = jnp.where(lane == which, stop, after)
    dist = lax.broadcasted_iota(jnp.int32, (2 * QB, 128), 0)
    s_.pick[...] = jnp.where(jnp.logical_and(dist >= first, dist < after), 1.0, 0.0).astype(BF16)


def table_rows(s_, heads, n):
    near = [diagonal_sums(jnp.concatenate([s_.gb[0, h], s_.gb[1, h]], axis=1)) for h in range(heads)]
    near = jnp.concatenate(near + [jnp.zeros((8 - heads, 2 * QB), F32)], axis=0)
    sums = jnp.zeros((8, 128), F32)
    for _ in range(3):
        term = near.astype(BF16)
        sums = sums + nn(term, s_.pick[...])
        near = near - term.astype(F32)
    lane = lax.broadcasted_iota(jnp.int32, (1, 128), 1)
    place = lax.broadcasted_iota(jnp.int32, (16, 128), 0)
    rows = jnp.zeros((16, 128), F32)
    for h in range(heads):
        far = jnp.sum(jnp.sum(s_.gb[2, h], axis=0, keepdims=True), axis=1, keepdims=True)
        line = sums[h : h + 1, :] + jnp.where(lane == NB - 1, far, 0.0)
        rows = jnp.where(place == n * heads + h, jnp.broadcast_to(line, (16, 128)), rows)
    return rows


def weight_grad(dest, column, left, right, first, width):
    def one(m, carry):
        part = pl.ds(pl.multiple_of(m * 256, 256), 256)
        dest[part, column : column + width] = tn(left[:, part], right[:, first : first + width]).astype(BF16)
        return carry

    lax.fori_loop(0, left.shape[1] // 256, one, 0)


class Layer:
    def __init__(self, zy, sizes, ins, outs, slots):
        self.zy, self.sizes = zy, sizes
        rows, model, cols, hid, wrows, length = sizes
        heads = cols // DH
        self.heads = heads
        s_ = self.shared = SimpleNamespace()
        self.one = Attention(slots, s_, length, cols, True)
        self.two = Attention(slots, s_, length, cols, False)
        wide_rows, acc = VM((heads * QB, cols), BF16), VM((length, cols), F32)
        marked, marked_acc = VM((heads * QB, cols + DH), BF16), VM((length, cols + DH), F32)
        line, tiles = VM((heads, 1, QB), F32), VM((3, heads, QB, QB), F32)
        slots.add(
            s_, bias=tiles, gb=tiles, qm=marked, dm=wide_rows, delta=line,
            oacc=VM((cols, QB), F32), dva=acc, dka=marked_acc, pick=VM((2 * QB, 128), BF16),
        )
        full, own = VM((length, model), BF16), VM((rows, model), F32)
        slots.add(
            self, full_self=full, full_mem=full, full_cross=full, full_ff=full, dy3=full, dy2=full, dy1=full,
            pa=full, pb=full, x_two=own, x_three=own, g=own, dkvq=VM((length, 3 * cols), BF16),
            hidden=VM((length, hid), BF16), cat=VM((length, heads * QB), BF16), dgu=VM((length, 2 * hid), BF16), small=VM((16, model), F32),
        )
        self.gathers = [RowGather(slots, rows) for _ in range(7)]
        self.g_self, self.g_mem, self.g_cross, self.g_ff, self.g_dy3, self.g_dy2, self.g_dy1 = self.gathers
        self.reduces = [RowReduce(slots, rows, model) for _ in range(7)]
        self.r_out1, self.r_out2, self.r_out3, self.r_dn3, self.r_dn2, self.r_mem, self.r_dn1 = self.reduces
        kinds = (
            (4 * cols, (2 * cols, 256, 4 * cols - 2 * cols - 256), 128),
            (4 * cols, (2 * cols, 2 * cols), 384),
            (3 * hid, (768, 3 * hid - 768), 384),
        )
        self.groups = [SimpleNamespace(width=w, parts=p, step=s) for w, p, s in kinds]
        self.ws, self.wc, self.wf = self.groups
        for group in self.groups:
            if zy:
                both = VM((model, group.width), BF16)
                slots.add(group, w=both, gp=both)
                group.gather = WideGather(slots, wrows, group.parts)
                group.reduce = WideReduce(slots, wrows, group.width, group.step)
            else:
                outs.add(group, gp=((model, group.width), BF16))
                group.gather = group.reduce = Idle()
        if zy:
            self.ss = SmallSum(slots, 16, model)

    def blk(self, b):
        return aligned(b * QB, QB)

    def chunk(self, k, block=0):
        size = self.sizes[0] // ROW_CHUNKS
        return aligned(block * self.sizes[0] + k * size, size)

    def far_first(self, i):
        s = self.spot
        far = jnp.where(i < 2, 1 - s.x, s.x)
        return far * 2 + jnp.where(i % 2 == 0, 1 - s.c, s.c)

    def near_tile(self, i):
        s = self.spot
        near = jnp.where(i == 0, s.n, s.sib)
        first = jnp.where(i < 2, 2 * near, 2 * s.xsib + i - 2)
        second = jnp.where(i < 2, 2 * near + 1, 2 * s.xp + i - 2)
        return Tile(i, first, second)

    def near_block(self, i):
        s = self.spot
        far = jnp.where(i < 2, s.x, 1 - s.x)
        return far * 2 + jnp.where(i % 2 == 0, s.c, 1 - s.c)

    def block_tile(self, b):
        return Tile(b, 2 * b, 2 * b + 1)

    def near_waits(self, i, gather):
        @pl.when(i == 1)
        def _():
            gather.have_sib()
            gather.forward(0, 1)

        @pl.when(i == 2)
        def _():
            gather.forward(1, 2)
            gather.have_xsib(0, 2)

        @pl.when(i == 3)
        def _():
            gather.forward(2, 4)
            gather.have_xsib(2, 4)

    def near_sends(self, i, reduce):
        @pl.when(i == 1)
        def _():
            reduce.send_own()

        @pl.when(i == 2)
        def _():
            reduce.send_far(0, 2)
            reduce.cross(0, 2)

        @pl.when(i == 3)
        def _():
            reduce.send_far(2, 4)
            reduce.cross(2, 4)

    def at(self, i, *actions):
        for j, action in enumerate(actions):
            if action is not None:
                pl.when(i == j)(action)

    def pack(self, group, *shards):
        rows = self.sizes[4]
        parts = [ref[...].astype(F32) for ref in shards]
        parts = [p if p.shape[0] == rows else p.T for p in parts]
        group.w[aligned(self.spot.w * rows, rows), :] = jnp.concatenate(parts, axis=1).astype(BF16)

    def ff_tile(self, t):
        f = self.sizes[3]
        step = f // 2
        w = self.wf.w
        x, dy = t.load(self.full_ff), t.load(self.dy3)
        for j in range(0, f, step):
            gate = nn(x, w[:, j : j + step])
            up = nn(x, w[:, f + j : f + j + step])
            dh = nn(dy, w[:, 2 * f + j : 2 * f + j + step])
            value, slope = gelu_parts(gate)
            t.store(self.hidden, (value * up).astype(BF16), j)
            t.store(self.dgu, (dh * up * slope).astype(BF16), j)
            t.store(self.dgu, (dh * value).astype(BF16), f + j)
        t.store(self.pa, nt(t.load(self.dgu), w[:, : 2 * f]).astype(BF16))

    def grads_kv(self):
        c = self.sizes[2]
        self.dkvq[:, : 2 * c] = jnp.concatenate(
            [self.shared.dka[:, :c], self.shared.dva[...]], axis=1
        ).astype(BF16)

    def norm_backward(self, values, gain, reduce, base, done):
        gain_sum = jnp.zeros((1, self.sizes[1]), F32)
        for k in range(ROW_CHUNKS):
            rows = self.chunk(k)
            add, part = norm_back(values[rows, :].astype(F32), gain, reduce.total(k))
            gain_sum = gain_sum + part
            done(k, rows, base[rows, :].astype(F32) + add)
        return gain_sum

    def run(self):
        rows, model, cols, hid, wrows, length = self.sizes
        zy, heads, s_ = self.zy, self.heads, self.shared
        spot = self.spot = Spot(zy)
        one, two = self.one, self.two
        ws, wc, wf = self.groups
        greet(spot, zy)
        for gather, full in zip(
            self.gathers, (self.full_self, self.full_mem, self.full_cross, self.full_ff, self.dy3, self.dy2, self.dy1)
        ):
            gather.bind(spot, full)
        for reduce, part in zip(
            self.reduces, (self.pa, self.pb, self.pb, self.pa, self.pa, self.dgu, self.pa)
        ):
            reduce.bind(spot, part)
        column = 0
        for group in self.groups:
            group.gather.bind(spot, group.w)
            group.reduce.bind(spot, group.gp, self.red if zy else None, column)
            column += group.width
        width = heads * QB
        one.bind(ws.w, self.full_mem, self.cat)
        two.bind(wc.w, self.dgu.at[:, :width], self.cat)
        gain_s, gain_c, gain_f = (ref[...].reshape(1, model) for ref in (self.gain_s, self.gain_c, self.gain_f))

        if zy:
            self.ss.bind(spot)
            self.pack(ws, self.sk, self.sv, self.sq, self.so)
        ws.gather.open_z()
        ws.gather.open_y()
        for k in range(ROW_CHUNKS):
            x = self.x[self.chunk(k), :].astype(F32)
            self.full_self[self.chunk(k, spot.n), :] = norm_rows(x, gain_s).astype(BF16)
            self.g_self.send(k)
        self.full_mem[self.blk(spot.n), :] = self.m[...]
        self.g_mem.send_all()
        self.dy3[self.blk(spot.n), :] = self.cot[...]
        if zy:
            self.pack(wc, self.ck, self.cv, self.cq, self.co)
            self.pack(wf, self.fg, self.fu, self.fd)
        ranges = bucket_ranges(2 * QB)
        document_columns((one.q, two.q), one.k, self.sid, cols)
        make_bias(s_, self.table, heads, ranges)
        ws.gather.forward(1, 0)
        ws.gather.forward(2, 0)
        self.g_self.forward(0, 2)
        ws.gather.forward(3, 0)
        ws.gather.forward(1, 1)
        self.g_self.forward(2, 4)
        ws.gather.forward(2, 1)
        ws.gather.forward(3, 1)
        wc.gather.open_z()
        self.g_self.have_sib()
        self.g_self.have_xsib(0, 4)
        ws.gather.have(0)

        one.project_kv(self.full_self)
        for distance in (1, 2, 3):
            ws.gather.forward(distance, 2)
        wc.gather.open_y()
        ws.gather.have(1, 2)

        def self_block(i, carry):
            b = self.far_first(i)
            t = self.block_tile(b)
            one.project_q(self.full_self, t)
            one.forward(t)
            one.out_part(self.pa, t)

            def after_first():
                self.r_out1.send_far()
                wc.gather.forward(1)
                wf.gather.open_z()
                wc.gather.forward(2, 0)

            def after_second():
                self.r_out1.cross()
                self.g_mem.forward(0, 4)
                wc.gather.forward(3, 0)
                wc.gather.forward(2, 1)

            def after_third():
                self.r_out1.send_own()
                wc.gather.forward(3, 1)
                wf.gather.open_y()

            self.at(i, after_first, after_second, after_third)
            return carry

        lax.fori_loop(0, 4, self_block, 0)
        document_columns(None, two.k, self.mid, cols)
        self.g_mem.have_sib()
        self.g_mem.have_xsib(0, 4)
        wc.gather.have()
        two.project_kv(self.full_mem)
        for k in range(ROW_CHUNKS):
            value = self.x[self.chunk(k), :].astype(F32) + self.r_out1.total(k)
            self.x_two[self.chunk(k), :] = value
            self.full_cross[self.chunk(k, spot.n), :] = norm_rows(value, gain_c).astype(BF16)
            self.g_cross.send(k)
        self.g_dy3.send_all(0, 4)
        wf.gather.forward(1, 0)

        def cross_block(i, carry):
            t = self.near_tile(i)
            self.near_waits(i, self.g_cross)
            two.project_q(self.full_cross, t)
            two.forward(t)
            two.out_part(self.pb, t)
            self.near_sends(i, self.r_out2)
            self.at(i, lambda: [wf.gather.forward(2, 0)] and None, lambda: [wf.gather.forward(3, 0), wf.gather.forward(1, 1)] and None, lambda: [wf.gather.forward(2, 1), wf.gather.forward(3, 1)] and None)
            return carry

        lax.fori_loop(0, 4, cross_block, 0)
        self.g_dy3.forward(0, 4)
        for k in range(ROW_CHUNKS):
            value = self.x_two[self.chunk(k), :] + self.r_out2.total(k)
            self.x_three[self.chunk(k), :] = value
            self.full_ff[self.chunk(k, spot.n), :] = norm_rows(value, gain_f).astype(BF16)
            self.g_ff.send(k)
        self.r_out1.finish()
        self.r_out2.finish()
        self.g_dy3.have_sib()
        self.g_dy3.have_xsib(0, 4)
        wf.gather.have()

        def ff_step(i, carry):
            self.near_waits(i, self.g_ff)
            self.ff_tile(self.near_tile(i))
            self.near_sends(i, self.r_dn3)
            return carry

        lax.fori_loop(0, 4, ff_step, 0)
        weight_grad(wf.gp, 0, self.full_ff, self.dgu, 0, 2 * hid)
        split = wf.reduce.chunks * 2 // 3
        for c in range(split):
            wf.reduce.open(c)

        def ff_out(b, carry):
            self.pb[self.blk(b), :] = nt(self.hidden[self.blk(b), :], wf.w[:, 2 * hid :]).astype(BF16)
            return carry

        lax.fori_loop(0, 4, ff_out, 0)
        self.r_out3.send_far()
        self.r_out3.send_own()
        weight_grad(wf.gp, 2 * hid, self.dy3, self.hidden, 0, hid)
        for c in range(split, wf.reduce.chunks):
            wf.reduce.open(c)

        def back_three(k, at, value):
            self.g[at, :] = value
            self.dy2[self.chunk(k, spot.n), :] = value.astype(BF16)
            self.g_dy2.send(k)

        gain_ff = self.norm_backward(self.x_three, gain_f, self.r_dn3, self.cot, back_three)
        self.small[14:15, :] = gain_ff
        self.r_out3.cross(0, 2)

        self.r_dn3.finish()
        s_.dka[...] = jnp.zeros_like(s_.dka)
        s_.dva[...] = jnp.zeros_like(s_.dva)

        def cross_back(i, carry):
            t = self.near_tile(i)
            self.near_waits(i, self.g_dy2)
            dctx = nn(t.load(self.dy2), two.wcols(3, 1)).astype(BF16)
            dq = two.backward(t, dctx)
            t.store(self.dkvq, dq, 2 * cols)
            t.store(self.pa, nt(dq, two.wcols(2, 1)).astype(BF16))
            self.near_sends(i, self.r_dn2)
            if zy:
                self.at(i, lambda: wf.reduce.first(0), lambda: wf.reduce.first(1), None, lambda: wf.reduce.first(2))
            return carry

        lax.fori_loop(0, 4, cross_back, 0)
        self.grads_kv()

        def memory_part(b, carry):
            blk = self.blk(b)
            self.dgu[blk, 0:model] = nt(self.dkvq[blk, : 2 * cols], two.wcols(0, 2)).astype(BF16)
            return carry

        lax.fori_loop(0, 4, memory_part, 0)
        self.r_mem.send_far()
        self.r_mem.send_own()
        if zy:
            wf.reduce.first(3)

        def back_two(k, at, value):
            self.g[at, :] = value
            self.dy1[self.chunk(k, spot.n), :] = value.astype(BF16)
            self.g_dy1.send(k)

        gain_cross = self.norm_backward(self.x_two, gain_c, self.r_dn2, self.g, back_two)
        self.small[13:14, :] = gain_cross
        self.r_out3.cross(2, 4)
        self.r_mem.cross()
        weight_grad(wc.gp, 0, self.full_mem, self.dkvq, 0, 2 * cols)
        wc.reduce.open(0)
        weight_grad(wc.gp, 2 * cols, self.full_cross, self.dkvq, 2 * cols, cols)
        weight_grad(wc.gp, 3 * cols, self.dy2, two.ctx, 0, cols)
        wc.reduce.open(1)

        self.g_mem.finish()
        s_.dka[...] = jnp.zeros_like(s_.dka)
        s_.dva[...] = jnp.zeros_like(s_.dva)

        def self_waits(i):
            @pl.when(i == 1)
            def _():
                self.g_dy1.have_sib()
                self.g_dy1.forward(0, 1)

            @pl.when(i == 2)
            def _():
                self.g_dy1.forward(1, 4)

            @pl.when(i == 3)
            def _():
                self.g_dy1.have_xsib(0, 4)

        def self_back(i, carry):
            b = self.near_block(i)
            t = self.block_tile(b)
            self_waits(i)
            dctx = nn(t.load(self.dy1), one.wcols(3, 1)).astype(BF16)
            t.store(self.dkvq, one.backward(t, dctx), 2 * cols)

            def ff_totals():
                for c in range(wf.reduce.chunks):
                    wf.reduce.total(c)

            self.at(i, None, lambda: wc.reduce.first(0), ff_totals, lambda: wc.reduce.first(1))
            return carry

        lax.fori_loop(0, 4, self_back, 0)
        self.grads_kv()
        self.r_dn2.finish()

        def last_part(i, carry):
            blk = self.blk(self.far_first(i))
            self.pa[blk, :] = nt(self.dkvq[blk, :], one.wcols(0, 3)).astype(BF16)
            return carry

        lax.fori_loop(0, 2, last_part, 0)
        self.r_dn1.send_far()
        weight_grad(ws.gp, 0, self.full_self, self.dkvq, 0, 3 * cols)
        weight_grad(ws.gp, 3 * cols, self.dy1, one.ctx, 0, cols)
        for c in range(ws.reduce.chunks):
            ws.reduce.open(c)
        self.r_dn1.cross()
        lax.fori_loop(2, 4, last_part, 0)
        self.r_dn1.send_own()

        def gain_part(b, total):
            blk = self.blk(b)
            both = self.full_self[blk, :].astype(F32) * self.pa[blk, :].astype(F32)
            return total + jnp.sum(both, axis=0, keepdims=True)

        gain_self = lax.fori_loop(0, 4, gain_part, jnp.zeros((1, model), F32)) / gain_s
        keep = self.small[13:15, :]
        self.small[...] = jnp.zeros_like(self.small)
        self.small[:, 0:128] = table_rows(s_, heads, spot.n)
        self.small[12:13, :] = gain_self
        self.small[13:15, :] = keep
        if zy:
            self.ss.begin(self.small[...])
        else:
            self.tot[...] = self.small[...]
        for k in range(ROW_CHUNKS):
            value = self.x_three[self.chunk(k), :] + self.r_out3.total(k)
            self.result[self.chunk(k), :] = value.astype(BF16)
        if zy:
            self.ss.to_z()
            ws.reduce.first(0)
            ws.reduce.first(1)
            self.ss.to_x()
        for k in range(ROW_CHUNKS):
            self.gm[self.chunk(k), :] = self.r_mem.total(k).astype(BF16)
        for c in range(wc.reduce.chunks):
            wc.reduce.total(c)
        if zy:
            ws.reduce.first(2)

        def back_one(k, at, value):
            self.gx[at, :] = value.astype(BF16)
            if zy and k == 1:
                ws.reduce.first(3)

        self.norm_backward(self.x, gain_s, self.r_dn1, self.g, back_one)
        if zy:
            self.ss.to_y()
            ws.reduce.first(4)
            ws.reduce.first(5)
            for c in range(ws.reduce.chunks):
                ws.reduce.total(c)
            self.ss.end(self.tot)

        for gather in self.gathers:
            if gather is not self.g_mem:
                gather.finish()
        for reduce in (self.r_out3, self.r_mem, self.r_dn1):
            reduce.finish()
        for group in self.groups:
            group.gather.finish()
            group.reduce.finish()


def deliver(red, tot, passed, sizes, heads):
    rows, model, cols, hid, wrows, length = sizes
    ins, outs = Slots(), Slots()
    packed, small = SimpleNamespace(), SimpleNamespace()
    ins.add(packed, ref=(red, VM))
    ins.add(small, ref=(tot, VM))
    sources, dests = [SimpleNamespace() for _ in passed], [SimpleNamespace() for _ in passed]
    for value, source, dest in zip(passed, sources, dests):
        ins.add(source, ref=(value, VM))
        outs.add(dest, ref=(value.shape, value.dtype))
    places = [(i * cols, cols, i % 4 == 3) for i in (2, 0, 1, 3, 6, 4, 5, 7)]
    places += [(8 * cols + i * hid, hid, False) for i in range(3)]
    cuts = []
    for at, width, turn in places:
        cut = SimpleNamespace(at=at, width=width, turn=turn)
        outs.add(cut, ref=((width, wrows) if turn else (wrows, width), F32))
        cuts.append(cut)
    gains, table = [SimpleNamespace() for _ in range(3)], SimpleNamespace()
    for gain in gains:
        outs.add(gain, ref=((model,), F32))
    outs.add(table, ref=((4 * heads, NB), F32))

    def body():
        for source, dest in zip(sources, dests):
            dest.ref[...] = source.ref[...]
        for cut in cuts:
            part = packed.ref[:, cut.at : cut.at + cut.width]
            cut.ref[...] = part.T if cut.turn else part
        for i, gain in enumerate(gains):
            gain.ref[...] = small.ref[12 + i : 13 + i, :].reshape(model)
        table.ref[...] = small.ref[0 : 4 * heads, 0:NB]

    got = run_kernel(body, ins, outs, Slots(), None, "deliver")
    return got[:3], got[3:14], got[14:17], got[17]


def shards(
    zy, inputs, memory, segment_ids, memory_ids, self_gain, self_query, self_key, self_value, self_out, bias_table,
    cross_gain, cross_query, cross_key, cross_value, cross_out, ff_gain, ff_gate, ff_up, ff_down, cotangent,
):
    rows, model = inputs.shape
    length = segment_ids.shape[1]
    wrows, cols = self_query.shape
    hid = ff_gate.shape[1]
    heads = cols // DH
    assert segment_ids.shape[0] == 1 and rows == QB and length == 4 * QB == memory_ids.shape[1]
    sizes = (rows, model, cols, hid, wrows, length)
    ins, outs, slots = Slots(), Slots(), Slots()
    layer = Layer.__new__(Layer)
    outs.add(
        layer, result=((rows, model), BF16), gx=((rows, model), BF16), gm=((rows, model), BF16), tot=((16, model), F32)
    )
    if zy:
        outs.add(layer, red=((wrows, 8 * cols + 3 * hid), F32))
    layer.__init__(zy, sizes, ins, outs, slots)
    ins.add(
        layer, x=(inputs, VM), m=(memory, VM), cot=(cotangent, VM), sid=(segment_ids, VM), mid=(memory_ids, VM),
        gain_s=(self_gain, VM), gain_c=(cross_gain, VM), gain_f=(ff_gain, VM), table=(bias_table.T, pltpu.SMEM),
    )
    if zy:
        ins.add(
            layer, sq=(self_query, VM), sk=(self_key, VM), sv=(self_value, VM), so=(self_out, VM),
            cq=(cross_query, VM), ck=(cross_key, VM), cv=(cross_value, VM), co=(cross_out, VM),
            fg=(ff_gate, VM), fu=(ff_up, VM), fd=(ff_down.T, VM),
        )
    else:

        def whole(*parts):
            return lax.all_gather(jnp.concatenate(parts, axis=1), WIDE, axis=0, tiled=True)

        ins.add(layer.ws, w=(whole(self_key, self_value, self_query, self_out.T), VM))
        ins.add(layer.wc, w=(whole(cross_key, cross_value, cross_query, cross_out.T), VM))
        ins.add(layer.wf, w=(whole(ff_gate, ff_up, ff_down.T), VM))
    got = run_kernel(layer.run, ins, outs, slots, 0, "layer")
    if zy:
        total, red = got[3], got[4]
    else:
        packed = jnp.concatenate(got[4:7], axis=1)
        red = lax.psum_scatter(packed, WIDE, scatter_dimension=0, tiled=True).astype(F32)
        total = lax.psum(got[3], (WIDE, NARROW))
    row_outs, grads, gains, table = deliver(red, total, got[:3], sizes, heads)
    return (
        *row_outs,
        gains[0],
        *grads[0:4],
        table.T,
        gains[1],
        *grads[4:8],
        gains[2],
        grads[8],
        grads[9],
        grads[10].T,
    )


def solution(mesh):
    zy = mesh.shape[WIDE] == 8
    rows = P((WIDE, NARROW), None)
    w_in, w_out = P(WIDE, NARROW), P(NARROW, WIDE)
    placed = (
        rows, rows, P(WIDE, None), P(WIDE, None), P(),
        w_in, w_in, w_in, w_out, P(None, NARROW), P(),
        w_in, w_in, w_in, w_out, P(), w_in, w_in, w_out, rows,
    )
    outs = (
        rows, rows, rows, P(), w_in, w_in, w_in, w_out, P(), P(),
        w_in, w_in, w_in, w_out, P(), w_in, w_in, w_out,
    )

    def program(*args):
        return shards(zy, *args)

    return jax.shard_map(program, mesh=mesh, in_specs=placed, out_specs=outs, check_vma=False)
```
